32 devices in a mesh: dp: 4 (over y, core), fsdp: 8 (over z, x).
Axes of the slice: x: 2, y: 2, z: 4, core: 2. Of those that a mesh axis runs over, the one named last changes fastest.
Arguments:
- tokens: bfloat16 [32768, 576], P(('dp', 'fsdp')), may hold values from -6 to 6
- segments: int32 [32, 1024], P(('dp', 'fsdp')), may hold values from 0 to 2, as said below
- positions: int32 [32, 1024], P(('dp', 'fsdp')), may hold values from 0 to 2302, as said below
- attn_gain: bfloat16 [576], P('fsdp'), may hold values from 0.25 to 1.75
- mlp_gain: bfloat16 [576], P('fsdp'), may hold values from 0.25 to 1.75
- w_query: bfloat16 [576, 576], P('fsdp', 'dp'), may hold values from -0.375 to 0.375
- w_key: bfloat16 [576, 192], P('fsdp', 'dp'), may hold values from -0.375 to 0.375
- w_value: bfloat16 [576, 192], P('fsdp', 'dp'), may hold values from -0.25 to 0.25
- w_output: bfloat16 [576, 576], P('dp', 'fsdp'), may hold values from -1 to 1
- w_gate: bfloat16 [576, 1536], P('fsdp', 'dp'), may hold values from -0.25 to 0.25
- w_up: bfloat16 [576, 1536], P('fsdp', 'dp'), may hold values from -0.25 to 0.25
- w_down: bfloat16 [1536, 576], P('dp', 'fsdp'), may hold values from -0.21875 to 0.21875
- cotangent: bfloat16 [32768, 576], P(('dp', 'fsdp')), may hold values from -6 to 6
Outputs:
- output: bfloat16 [32768, 576], P(('dp', 'fsdp'))
- grad_tokens: float32 [32768, 576], P(('dp', 'fsdp'))
- grad_attn_gain: float32 [576], P('fsdp')
- grad_mlp_gain: float32 [576], P('fsdp')
- grad_query: float32 [576, 576], P('fsdp', 'dp')
- grad_key: float32 [576, 192], P('fsdp', 'dp')
- grad_value: float32 [576, 192], P('fsdp', 'dp')
- grad_output: float32 [576, 576], P('dp', 'fsdp')
- grad_gate: float32 [576, 1536], P('fsdp', 'dp')
- grad_up: float32 [576, 1536], P('fsdp', 'dp')
- grad_down: float32 [1536, 576], P('dp', 'fsdp')
The draws below stay inside these ranges and needn't reach their ends.
Inputs may be any that keep to these rules, and one draw needn't show every extreme that they name: `segments`: in each sequence the document numbers are 0, then 1, then 2, each a run of 128 tokens or more. `positions`: counts up by one along a document; documents 1 and 2 of a sequence begin at 0, document 0 continues a document begun at most 2047 tokens before the sequence and ends within its first 256 tokens.
All inputs are finite; a program needn't handle non-finite values.
Results may differ from the reference program's by a relative error of at most 0.015.
The reference program's roundings to bfloat16 on the way count: a program that leaves them out, or rounds other values in their place, can miss the bound.
Values may be sent and summed in bfloat16 or wider, within the bound.
A program may use at most 192 MiB of HBM per device.

```python
import jax
import jax.numpy as jnp
from jax import lax

D = 576
Q_HEADS = 9
KV_HEADS = 3
HEAD_DIM = 64
FF = 1536
LEN = 1024
QBLOCK = 512
QW = 576
KVW = 192
SEQS = 32
TOKENS = 32768


def packing(key):
    base = jax.random.fold_in(key, 7)
    first_key, second_key, offset_key = jax.random.split(base, 3)
    first = jax.random.randint(first_key, (SEQS, 1), LEN // 8, LEN // 4 + 1)
    first = first.at[0, 0].set(LEN // 4)
    second = first + jax.random.randint(second_key, (SEQS, 1), LEN // 5, LEN // 2 + 1)
    offset = jax.random.randint(offset_key, (SEQS, 1), 0, 2 * LEN)
    offset = offset.at[0, 0].set(2 * LEN - 1)
    index = jnp.arange(LEN, dtype=jnp.int32)[None, :]
    segment = (index >= first).astype(jnp.int32) + (index >= second).astype(jnp.int32)
    begin = jnp.where(index >= second, second, jnp.where(index >= first, first, -offset))
    return (segment, (index - begin).astype(jnp.int32))


def draw_segments(key, part):
    return packing(key)[0]


def draw_positions(key, part):
    return packing(key)[1]


def block_scale(stream_key, shape, pieces, least, largest):
    factor_of, own = 1.0, jax.random.fold_in(stream_key, 6)
    for axis_at, parts in pieces:
        draws = jnp.exp(jax.random.uniform(jax.random.fold_in(own, axis_at), (parts,), jnp.float32, least / len(pieces), largest / len(pieces)))
        factor_of = factor_of * jnp.repeat(draws, shape[axis_at] // parts).reshape([-1 if axis == axis_at else 1 for axis in range(len(shape))])
    return factor_of


def normal_values(stream_key, extent, scale, limit, cuts=(), kind=jnp.bfloat16):
    drawn = scale * jax.random.normal(stream_key, extent, jnp.float32)
    if cuts:
        drawn = drawn * block_scale(stream_key, extent, cuts, -0.22, 0.18)
    return jnp.clip(drawn, -limit, limit).astype(kind)


def setup_inputs(seed: int = 0) -> dict:
    key_list = jax.random.split(jax.random.key(seed), 14)
    tokens = normal_values(key_list[0], (TOKENS, D), 1.0, 6.0, ((0, 32),))
    segments = draw_segments(jax.random.fold_in(key_list[13], 71), 0)
    positions = draw_positions(jax.random.fold_in(key_list[13], 71), 0)
    attn_gain = jnp.clip(1.0 + 0.15 * jax.random.normal(key_list[3], (D,), jnp.float32), 0.25, 1.75).astype(jnp.bfloat16)
    mlp_gain = jnp.clip(1.0 + 0.15 * jax.random.normal(key_list[4], (D,), jnp.float32), 0.25, 1.75).astype(jnp.bfloat16)
    w_query = normal_values(key_list[5], (D, QW), (D // 2) ** -0.5, 0.375, ((0, 8), (1, 4)))
    w_key = normal_values(key_list[6], (D, KVW), (D // 2) ** -0.5, 0.375, ((0, 8), (1, 4)))
    w_value = normal_values(key_list[7], (D, KVW), D ** -0.5, 0.25, ((0, 8), (1, 4)))
    w_output = normal_values(key_list[8], (QW, D), (max(QW // 16, 1)) ** -0.5, 1.0, ((0, 4), (1, 8)))
    w_gate = normal_values(key_list[9], (D, FF), D ** -0.5, 0.25, ((0, 8), (1, 4)))
    w_up = normal_values(key_list[10], (D, FF), D ** -0.5, 0.25, ((0, 8), (1, 4)))
    w_down = normal_values(key_list[11], (FF, D), (FF // 2) ** -0.5, 0.21875, ((0, 4), (1, 8)))
    cotangent = normal_values(key_list[12], (TOKENS, D), 1.0, 6.0, ((0, 32),))
    return {"tokens": tokens, "segments": segments, "positions": positions, "attn_gain": attn_gain, "mlp_gain": mlp_gain, "w_query": w_query, "w_key": w_key, "w_value": w_value, "w_output": w_output, "w_gate": w_gate, "w_up": w_up, "w_down": w_down, "cotangent": cotangent}


EPS = 1e-05
ROPE_BASE = 100000.0
MASKED = -1e+30
HIGH = lax.Precision.HIGHEST

@jax.custom_vjp
def low(v):
    return lax.optimization_barrier(v.astype(jnp.bfloat16)).astype(jnp.float32)

@jax.custom_vjp
def low_back(v):
    return v

def low_keep(v):
    return (low(v), None)

def low_pass(kept, grad):
    return (grad,)

def back_keep(v):
    return (v, None)

def back_low(kept, grad):
    return (low(grad),)
low.defvjp(low_keep, low_pass)
low_back.defvjp(back_keep, back_low)

def matmul(left, right):
    return jnp.dot(left, right, preferred_element_type=jnp.float32, precision=HIGH)

def tables(position):
    half_dim = HEAD_DIM // 2
    frequency = ROPE_BASE ** (-(2.0 * jnp.arange(half_dim, dtype=jnp.float32)) / HEAD_DIM)
    angles = position.astype(jnp.float32)[:, None] * frequency[None, :]
    angles = jnp.concatenate([angles, angles], axis=1)
    return (jnp.cos(angles), jnp.sin(angles))

def rotate(values, cosine, sine_table):
    half_dim = HEAD_DIM // 2
    turned = jnp.concatenate([-values[..., half_dim:], values[..., :half_dim]], axis=-1)
    return values * cosine[:, None, :] + turned * sine_table[:, None, :]

def norm_rows(values, gain):
    inverse = lax.rsqrt(lax.optimization_barrier(jnp.mean(values * values, axis=-1, keepdims=True)) + EPS)
    return values * inverse * gain

def attend(queries, keys, values, segment):
    group_size = Q_HEADS // KV_HEADS
    blocks = LEN // QBLOCK
    grouped = queries.reshape(blocks, QBLOCK, KV_HEADS, group_size, HEAD_DIM)
    block_segments = segment.reshape(blocks, QBLOCK)
    starts = jnp.arange(blocks, dtype=jnp.int32) * QBLOCK
    scale = HEAD_DIM ** (-0.5)
    col_index = jnp.arange(LEN, dtype=jnp.int32)

    def one_block(block_data):
        query_block, seg_block, block_start = block_data
        row_index = block_start + jnp.arange(QBLOCK, dtype=jnp.int32)
        allowed = (col_index[None, :] <= row_index[:, None]) & (segment[None, :] == seg_block[:, None])
        scores = low_back(jnp.einsum('qkgd,tkd->kgqt', query_block, keys, precision=HIGH) * scale)
        scores = jnp.where(allowed[None, None], scores, MASKED)
        top_value = lax.optimization_barrier(jnp.max(scores, axis=-1, keepdims=True))
        expo = jnp.exp(scores - top_value)
        probability = low(expo / lax.optimization_barrier(jnp.sum(expo, axis=-1, keepdims=True)))
        return jnp.einsum('kgqt,tkd->qkgd', probability, values, precision=HIGH)
    attended = lax.map(jax.checkpoint(one_block), (grouped, block_segments, starts))
    return attended.reshape(LEN, QW)

def layer(rows, segment, position, params):
    gain_attn, gain_mlp, w_query, w_key, w_value, w_output, w_gate, w_up, w_down = params
    cosine, sine_table = tables(position)
    normed_attn = low(norm_rows(rows, gain_attn))
    query_raw = low_back(matmul(normed_attn, w_query))
    key_raw = low_back(matmul(normed_attn, w_key))
    value_raw = low_back(matmul(normed_attn, w_value))
    queries = low(rotate(query_raw.reshape(LEN, Q_HEADS, HEAD_DIM), cosine, sine_table))
    keys = low(rotate(key_raw.reshape(LEN, KV_HEADS, HEAD_DIM), cosine, sine_table))
    values = low(value_raw).reshape(LEN, KV_HEADS, HEAD_DIM)
    mixture = low(low_back(attend(queries, keys, values, segment)))
    resid = rows + low_back(matmul(mixture, w_output))
    normed_mlp = low(norm_rows(resid, gain_mlp))
    gate_pre = low_back(matmul(normed_mlp, w_gate))
    up_pre = low_back(matmul(normed_mlp, w_up))
    hidden = low(jax.nn.silu(gate_pre) * up_pre)
    return resid + matmul(hidden, w_down)

def reference(tokens, segments, positions, attn_gain, mlp_gain, w_query, w_key, w_value, w_output, w_gate, w_up, w_down, cotangent):
    primals = tuple((array_in.astype(jnp.float32) for array_in in (tokens, attn_gain, mlp_gain, w_query, w_key, w_value, w_output, w_gate, w_up, w_down)))

    def forward(inputs, gain_attn, gain_mlp, *matrices):

        def seq_step(params, sequence):
            rows, segment, position = sequence
            return (params, layer(rows, segment, position, params))
        final, outputs = lax.scan(jax.checkpoint(seq_step), (gain_attn, gain_mlp) + tuple(matrices), (inputs.reshape(SEQS, LEN, D), segments, positions))
        return outputs.reshape(SEQS * LEN, D)
    result, pullback = jax.vjp(forward, *primals)
    grads = pullback(cotangent.astype(jnp.float32))
    return (result.astype(jnp.bfloat16), grads[0], grads[1], grads[2], grads[3], grads[4], grads[5], grads[6], grads[7], grads[8], grads[9])
```

```python
import functools

import jax
import jax.numpy as jnp
from jax import lax
from jax.experimental import pallas as pl
from jax.experimental.pallas import tpu as pltpu
from jax.sharding import PartitionSpec as P


Q_HEADS = 9
KV_HEADS = 3
HEAD_DIM = 64
LEN = 1024
QBLOCK = 512
QW = 576
KVW = 192


EPS = 1e-05
ROPE_BASE = 100000.0
MASKED = -1e30


def tables(position):
    half_dim = HEAD_DIM // 2
    frequency = ROPE_BASE ** (-(2.0 * jnp.arange(half_dim, dtype=jnp.float32)) / HEAD_DIM)
    angles = position.astype(jnp.float32)[:, None] * frequency[None, :]
    angles = jnp.concatenate([angles, angles], axis=1)
    return (jnp.cos(angles), jnp.sin(angles))


def rotate(values, cosine, sine_table):
    half_dim = HEAD_DIM // 2
    turned = jnp.concatenate([-values[..., half_dim:], values[..., :half_dim]], axis=-1)
    return values * cosine[:, None, :] + turned * sine_table[:, None, :]


def rotate_back(grads, cosine, sine_table):
    half_dim = HEAD_DIM // 2
    scaled = grads * sine_table[:, None, :]
    return grads * cosine[:, None, :] + jnp.concatenate(
        [scaled[..., half_dim:], -scaled[..., :half_dim]], axis=-1
    )


def norm_rows(values):
    inverse = lax.rsqrt(jnp.mean(values * values, axis=-1, keepdims=True) + EPS)
    return (values * inverse, inverse)


def norm_back(grad_scaled, scaled, inverse):
    return inverse * (grad_scaled - scaled * jnp.mean(grad_scaled * scaled, axis=-1, keepdims=True))


def block_scores(queries, keys, segment, block_index, kv_head):
    group_size = Q_HEADS // KV_HEADS
    first_row = block_index * QBLOCK
    row_index = first_row + jnp.arange(QBLOCK, dtype=jnp.int32)
    last_col = first_row + QBLOCK
    col_index = jnp.arange(last_col, dtype=jnp.int32)
    seg_block = segment[first_row : first_row + QBLOCK]
    allowed = (col_index[None, :] <= row_index[:, None]) & (segment[None, :last_col] == seg_block[:, None])
    width = group_size * HEAD_DIM
    query_block = queries[
        first_row : first_row + QBLOCK, kv_head * width : (kv_head + 1) * width
    ].reshape(QBLOCK, group_size, HEAD_DIM)
    key_head = keys[:last_col, kv_head * HEAD_DIM : (kv_head + 1) * HEAD_DIM]
    scores = jnp.einsum(
        "qgd,td->gqt", query_block, key_head, preferred_element_type=jnp.float32
    ) * HEAD_DIM ** (-0.5)
    return (query_block, key_head, jnp.where(allowed[None], scores, MASKED))


def attend_forward(sequence):
    queries, keys, values, segment = sequence
    group_size = Q_HEADS // KV_HEADS
    block_rows, top_list, total_list = ([], [], [])
    for block_index in range(LEN // QBLOCK):
        head_rows, head_tops, head_totals = ([], [], [])
        for kv_head in range(KV_HEADS):
            query_block, key_head, scores = block_scores(
                queries, keys, segment, block_index, kv_head
            )
            top_value = jnp.max(scores, axis=-1, keepdims=True)
            expo = jnp.exp(scores - top_value)
            total = jnp.sum(expo, axis=-1, keepdims=True)
            probability = (expo / total).astype(jnp.bfloat16)
            value_head = values[: (block_index + 1) * QBLOCK, kv_head * HEAD_DIM : (kv_head + 1) * HEAD_DIM]
            attended = jnp.einsum(
                "gqt,td->qgd", probability, value_head, preferred_element_type=jnp.float32
            )
            head_rows.append(attended.reshape(QBLOCK, group_size * HEAD_DIM))
            head_tops.append(top_value)
            head_totals.append(total)
        block_rows.append(jnp.concatenate(head_rows, axis=1))
        top_list.append(jnp.stack(head_tops))
        total_list.append(jnp.stack(head_totals))
    mixture = jnp.concatenate(block_rows, axis=0).astype(jnp.bfloat16)
    return (mixture, jnp.stack(top_list), jnp.stack(total_list))


def attend_backward(sequence):
    queries, keys, values, segment, tops, totals, grad_mixture = sequence
    group_size = Q_HEADS // KV_HEADS
    scale = HEAD_DIM ** (-0.5)
    width = group_size * HEAD_DIM
    grad_key_heads = [None] * KV_HEADS
    grad_value_heads = [None] * KV_HEADS
    block_rows = []
    for block_index in range(LEN // QBLOCK):
        first_row = block_index * QBLOCK
        head_rows = []
        for kv_head in range(KV_HEADS):
            query_block, key_head, scores = block_scores(
                queries, keys, segment, block_index, kv_head
            )
            expo = jnp.exp(scores - tops[block_index, kv_head])
            prob_full = expo / totals[block_index, kv_head]
            probability = prob_full.astype(jnp.bfloat16)
            value_head = values[: (block_index + 1) * QBLOCK, kv_head * HEAD_DIM : (kv_head + 1) * HEAD_DIM]
            grad_block = grad_mixture[
                first_row : first_row + QBLOCK, kv_head * width : (kv_head + 1) * width
            ].reshape(QBLOCK, group_size, HEAD_DIM)
            grad_probs = jnp.einsum(
                "qgd,td->gqt", grad_block, value_head, preferred_element_type=jnp.float32
            )
            grad_value_heads[kv_head] = add_rows(
                grad_value_heads[kv_head],
                jnp.einsum(
                    "gqt,qgd->td", probability, grad_block, preferred_element_type=jnp.float32
                ),
            )
            delta = jnp.sum(prob_full * grad_probs, axis=-1, keepdims=True)
            grad_scores = (prob_full * (grad_probs - delta)).astype(jnp.bfloat16)
            grad_query_block = (
                jnp.einsum("gqt,td->qgd", grad_scores, key_head, preferred_element_type=jnp.float32)
                * scale
            )
            grad_key_heads[kv_head] = add_rows(
                grad_key_heads[kv_head],
                jnp.einsum(
                    "gqt,qgd->td", grad_scores, query_block, preferred_element_type=jnp.float32
                )
                * scale,
            )
            head_rows.append(grad_query_block.reshape(QBLOCK, width))
        block_rows.append(jnp.concatenate(head_rows, axis=1))
    grad_queries = jnp.concatenate(block_rows, axis=0)
    return (
        grad_queries,
        jnp.concatenate(grad_key_heads, axis=1),
        jnp.concatenate(grad_value_heads, axis=1),
    )


def add_rows(longest, shorter):
    if longest is None:
        return shorter
    rows = longest.shape[0]
    return jnp.concatenate([shorter[:rows] + longest, shorter[rows:]], axis=0)


BF16 = jnp.bfloat16
F32 = jnp.float32
MESH = pl.DeviceIdType.MESH
ANY = pl.BlockSpec(memory_space=pl.ANY)
VMEM = pl.BlockSpec(memory_space=pltpu.VMEM)


def up(value, step):
    return -(-value // step) * step


class Layout:
    def __init__(self, pieces, shards):
        self.pieces, self.shards = pieces, shards
        self.C = 2 if pieces % 2 == 0 else 1
        self.Y = pieces // self.C
        self.X = 2 if shards <= 8 else 4
        self.Z = shards // self.X
        self.H = self.Z // 2
        self.slots = (self.C, self.Y, self.X, self.Z)
        n = (self.X - 1) + (self.Y - 1)
        self.gather_sems = 1 + (self.Z - 1) + 2 * n + 1 + 2 * n
        self.reduce_sems = 2 + 2 * n + (self.Z - 1)
        self.peers = (self.X - 1) + (self.Y - 1) + (self.Z - 1) + (self.C - 1)

    def here(self):
        dp, fs = lax.axis_index("dp"), lax.axis_index("fsdp")
        return lax.rem(dp, self.C), dp // self.C, lax.rem(fs, self.X), fs // self.X

    def device(self, c, y, x, z):
        return (y * self.C + c, z * self.X + x)

    def others(self, me, axis):
        size = self.slots[axis]
        for k in range(1, size):
            place = list(me)
            place[axis] = lax.rem(me[axis] + k, size)
            yield k, place

    def barrier(self, me):
        sem = pltpu.get_barrier_semaphore()
        for axis in range(4):
            for _, place in self.others(me, axis):
                pl.semaphore_signal(sem, inc=1, device_id=self.device(*place), device_id_type=MESH)
        pl.semaphore_wait(sem, self.peers)


class Sender:
    def __init__(self, layout, me, send, recv):
        self.lay, self.me, self.send, self.recv, self.used = layout, me, send, recv, 0

    def to(self, place, src, dst):
        k = self.used
        self.used += 1
        return pltpu.make_async_remote_copy(
            src_ref=src, dst_ref=dst, send_sem=self.send.at[k], recv_sem=self.recv.at[k],
            device_id=self.lay.device(*place), device_id_type=MESH)


def start(copies):
    for copy in copies:
        copy.start()


def wait(copies):
    for copy in copies:
        copy.wait()


class Gather:
    def __init__(self, lay, me, src, slots, send, recv):
        c, y, x, z = me
        s = Sender(lay, me, send, recv)
        X, Y, H, R = lay.X, lay.Y, lay.H, lay.Z - lay.H
        lo, hi = pl.ds(0, H), pl.ds(H, R)
        ax, ay = pl.ds(0, X), pl.ds(0, Y)
        sib = (1 - c, y, x, z)
        self.own = pltpu.make_async_copy(src, slots.at[c, y, x, z], recv.at[s.used])
        s.used += 1
        self.z = [s.to(p, src, slots.at[c, y, x, z]) for _, p in lay.others(me, 3)]
        part = slots.at[c, y, x, lo]
        self.xy1 = [s.to(p, part, part) for _, p in lay.others(me, 2)]
        part2 = slots.at[c, y, x, hi]
        self.xy1 += [s.to(p, part2, part2) for _, p in lay.others(me, 1)]
        part3 = slots.at[c, y, ax, lo]
        self.xy2 = [s.to(p, part3, part3) for _, p in lay.others(me, 1)]
        part4 = slots.at[c, ay, x, hi]
        self.xy2 += [s.to(p, part4, part4) for _, p in lay.others(me, 2)]
        self.core = [[], [], []]
        if lay.C > 1:
            whole = slots.at[c, y, x]
            self.core[0] = [s.to(sib, whole, whole)]
            for _, p in lay.others(me, 2):
                piece = slots.at[c, y, p[2], lo]
                self.core[1].append(s.to(sib, piece, piece))
            for _, p in lay.others(me, 1):
                piece = slots.at[c, p[1], x, hi]
                self.core[1].append(s.to(sib, piece, piece))
            for _, p in lay.others(me, 1):
                piece = slots.at[c, p[1], ax, lo]
                self.core[2].append(s.to(sib, piece, piece))
            for _, p in lay.others(me, 2):
                piece = slots.at[c, ay, p[2], hi]
                self.core[2].append(s.to(sib, piece, piece))

    def step(self, n):
        if n == 0:
            self.own.start()
            start(self.z)
        elif n == 1:
            self.own.wait()
            wait(self.z)
            start(self.xy1)
            start(self.core[0])
        elif n == 2:
            wait(self.xy1)
            start(self.xy2)
            start(self.core[1])
        elif n == 3:
            wait(self.xy2)
            start(self.core[2])
        else:
            for copies in self.core:
                wait(copies)


class Reduce:
    def __init__(self, lay, me, parts, bufs, send, recv):
        c, y, x, z = me
        self.lay, self.me = lay, me
        self.near, self.far, self.total, self.out, self.r2a, self.r2b, self.r3a, self.r3b, self.r4 = bufs
        s = Sender(lay, me, send, recv)
        X, Y, H, R = lay.X, lay.Y, lay.H, lay.Z - lay.H
        lo, hi = pl.ds(0, H), pl.ds(H, R)
        ax, ay = pl.ds(0, X), pl.ds(0, Y)
        out = self.out
        self.own = pltpu.make_async_copy(parts.at[c], self.near, recv.at[s.used])
        s.used += 1
        self.core = [s.to((1 - c, y, x, z), parts.at[1 - c], self.far)] if lay.C > 1 else []
        self.xy1 = [s.to(p, out.at[p[1], ax, lo], self.r2a.at[k - 1]) for k, p in lay.others(me, 1)]
        self.xy1 += [s.to(p, out.at[ay, p[2], hi], self.r2b.at[k - 1]) for k, p in lay.others(me, 2)]
        self.xy2 = [s.to(p, out.at[y, p[2], lo], self.r3a.at[k - 1]) for k, p in lay.others(me, 2)]
        self.xy2 += [s.to(p, out.at[p[1], x, hi], self.r3b.at[k - 1]) for k, p in lay.others(me, 1)]
        self.zs = [s.to(p, out.at[y, x, p[3]], self.r4.at[k - 1]) for k, p in lay.others(me, 3)]

    @staticmethod
    def scratch(lay, rows, width):
        X, Y, Z, H = lay.X, lay.Y, lay.Z, lay.H
        R = Z - H
        tail = (rows, width)
        return [
            pltpu.VMEM((Y, X, Z) + tail, BF16), pltpu.VMEM((Y, X, Z) + tail, BF16),
            pltpu.VMEM((Y, X, Z) + tail, F32), pltpu.VMEM((Y, X, Z) + tail, BF16),
            pltpu.VMEM((Y - 1, X, H) + tail, BF16), pltpu.VMEM((X - 1, Y, R) + tail, BF16),
            pltpu.VMEM((X - 1, H) + tail, BF16), pltpu.VMEM((Y - 1, R) + tail, BF16),
            pltpu.VMEM((Z - 1,) + tail, BF16),
        ]

    def step(self, n, result=None):
        lay, (c, y, x, z) = self.lay, self.me
        X, Y, Z, H = lay.X, lay.Y, lay.Z, lay.H
        total, out = self.total, self.out
        if n == 0:
            self.own.start()
            start(self.core)
        elif n == 1:
            self.own.wait()
            wait(self.core)

            @pl.loop(0, Y * X * Z)
            def _(i):
                yy, xx, zz = i // (X * Z), lax.rem(i // Z, X), lax.rem(i, Z)
                v = self.near[yy, xx, zz].astype(F32)
                if lay.C > 1:
                    v = v + self.far[yy, xx, zz].astype(F32)
                total[yy, xx, zz] = v
                out[yy, xx, zz] = v.astype(BF16)

            start(self.xy1)
        elif n == 2:
            wait(self.xy1)

            @pl.loop(0, X * H)
            def _(i):
                xx, zz = i // H, lax.rem(i, H)
                v = total[y, xx, zz]
                for k in range(Y - 1):
                    v = v + self.r2a[k, xx, zz].astype(F32)
                total[y, xx, zz] = v
                out[y, xx, zz] = v.astype(BF16)

            @pl.loop(0, Y * (Z - H))
            def _(i):
                yy, zz = i // (Z - H), lax.rem(i, Z - H)
                v = total[yy, x, H + zz]
                for k in range(X - 1):
                    v = v + self.r2b[k, yy, zz].astype(F32)
                total[yy, x, H + zz] = v
                out[yy, x, H + zz] = v.astype(BF16)

            start(self.xy2)
        elif n == 3:
            wait(self.xy2)

            @pl.loop(0, H)
            def _(i):
                v = total[y, x, i]
                for k in range(X - 1):
                    v = v + self.r3a[k, i].astype(F32)
                total[y, x, i] = v
                out[y, x, i] = v.astype(BF16)

            @pl.loop(0, Z - H)
            def _(i):
                v = total[y, x, H + i]
                for k in range(Y - 1):
                    v = v + self.r3b[k, i].astype(F32)
                total[y, x, H + i] = v
                out[y, x, H + i] = v.astype(BF16)

            start(self.zs)
        else:
            wait(self.zs)
            v = total[y, x, z]
            for k in range(Z - 1):
                v = v + self.r4[k].astype(F32)
            result[...] = v


def gather_all(lay, attn_pack, mlp_pack):
    def kernel(a_ref, m_ref, ga_ref, gm_ref, sa, ra, sm, rm):
        me = lay.here()
        lay.barrier(me)
        ga = Gather(lay, me, a_ref, ga_ref, sa, ra)
        gm = Gather(lay, me, m_ref, gm_ref, sm, rm)
        for n in range(5):
            ga.step(n)
        for n in range(5):
            gm.step(n)

    n = lay.gather_sems
    return pl.pallas_call(
        kernel,
        out_shape=[jax.ShapeDtypeStruct(lay.slots + attn_pack.shape, BF16), jax.ShapeDtypeStruct(lay.slots + mlp_pack.shape, BF16)],
        in_specs=[VMEM, VMEM], out_specs=[ANY, ANY],
        scratch_shapes=[pltpu.SemaphoreType.DMA((n,))] * 4,
        compiler_params=pltpu.CompilerParams(collective_id=0, has_side_effects=True, vmem_limit_bytes=50 * 2**20),
        name="gather_weights",
    )(attn_pack, mlp_pack)


def reduce_all(lay, parts, which):
    rows, width = parts.shape[-2:]

    def kernel(p_ref, o_ref, *rest):
        bufs, (send, recv) = rest[:-2], rest[-2:]
        me = lay.here()
        lay.barrier(me)
        red = Reduce(lay, me, p_ref, bufs, send, recv)
        for n in range(5):
            red.step(n, o_ref)

    n = lay.reduce_sems
    return pl.pallas_call(
        kernel,
        out_shape=jax.ShapeDtypeStruct((rows, width), F32),
        in_specs=[ANY], out_specs=VMEM,
        scratch_shapes=Reduce.scratch(lay, rows, width) + [pltpu.SemaphoreType.DMA((n,))] * 2,
        compiler_params=pltpu.CompilerParams(collective_id=which, has_side_effects=True, vmem_limit_bytes=50 * 2**20),
        name="reduce_grads",
    )(parts)


def pack(parts, gains, rows_p):
    packed = jnp.concatenate(parts, axis=1)
    width = up(packed.shape[1], 128)
    packed = jnp.pad(packed, ((0, 0), (0, width - packed.shape[1])))
    if gains:
        rows = jnp.stack([jnp.pad(g, (0, width - g.shape[0])) for g in gains])
        packed = jnp.concatenate([packed, rows], axis=0)
    return jnp.pad(packed, ((0, rows_p - packed.shape[0]), (0, 0)))


def on_device(
    tokens,
    segments,
    positions,
    attn_gain,
    mlp_gain,
    w_query,
    w_key,
    w_value,
    w_output,
    w_gate,
    w_up,
    w_down,
    cotangent,
):
    model_part = attn_gain.shape[0]
    lay = Layout(lax.axis_size("dp"), lax.axis_size("fsdp"))
    rows_p = up(model_part + 2, 16)
    attn_widths = (w_query.shape[1], w_output.shape[0], w_key.shape[1], w_value.shape[1])
    mlp_widths = (w_gate.shape[1], w_up.shape[1], w_down.shape[0])
    attn_pack = pack((w_query, w_output.T, w_key, w_value), (attn_gain, mlp_gain), rows_p)
    mlp_pack = pack((w_gate, w_up, w_down.T), (), rows_p)
    attn_all, mlp_all = gather_all(lay, attn_pack, mlp_pack)

    def unpack(slots, widths):
        order = slots.transpose(1, 0, 3, 2, 4, 5).reshape((lay.pieces, lay.shards) + slots.shape[4:])
        body = order[:, :, :model_part]
        parts, at = [], 0
        for width in widths:
            piece = body[..., at : at + width]
            parts.append(piece.transpose(1, 2, 0, 3).reshape(lay.shards * model_part, lay.pieces * width))
            at += width
        gains = order[0, :, model_part : model_part + 2, :model_part]
        return parts, gains

    (full_query, full_output, full_key, full_value), gains = unpack(attn_all, attn_widths)
    (full_gate, full_up, full_down), _ = unpack(mlp_all, mlp_widths)
    weights = (gains[:, 0].reshape(-1), gains[:, 1].reshape(-1), full_query, full_key, full_value, full_output, full_gate, full_up, full_down)
    row_count = tokens.shape[0]
    seq_count = segments.shape[0]
    gain_attn = weights[0].astype(jnp.float32)
    gain_mlp = weights[1].astype(jnp.float32)
    inputs = tokens.astype(jnp.float32)
    cosine, sine_table = tables(positions.reshape(row_count))
    scaled_attn, inverse_attn = norm_rows(inputs)
    normed_attn = (scaled_attn * gain_attn).astype(jnp.bfloat16)
    query_raw = jnp.dot(normed_attn, weights[2], preferred_element_type=jnp.float32)
    key_raw = jnp.dot(normed_attn, weights[3], preferred_element_type=jnp.float32)
    value_raw = jnp.dot(normed_attn, weights[4], preferred_element_type=jnp.float32)
    queries = (
        rotate(query_raw.reshape(row_count, Q_HEADS, HEAD_DIM), cosine, sine_table)
        .reshape(row_count, QW)
        .astype(jnp.bfloat16)
    )
    keys = (
        rotate(key_raw.reshape(row_count, KV_HEADS, HEAD_DIM), cosine, sine_table)
        .reshape(row_count, KVW)
        .astype(jnp.bfloat16)
    )
    values = value_raw.astype(jnp.bfloat16)
    seq_queries = queries.reshape(seq_count, LEN, QW)
    seq_keys = keys.reshape(seq_count, LEN, KVW)
    seq_values = values.reshape(seq_count, LEN, KVW)
    mixture, tops, totals = lax.map(attend_forward, (seq_queries, seq_keys, seq_values, segments))
    mixture = mixture.reshape(row_count, QW)
    resid = inputs + jnp.einsum("rq,dq->rd", mixture, weights[5], preferred_element_type=jnp.float32)
    scaled_mlp, inverse_mlp = norm_rows(resid)
    normed_mlp = (scaled_mlp * gain_mlp).astype(jnp.bfloat16)
    gate_pre = jnp.dot(normed_mlp, weights[6], preferred_element_type=jnp.float32)
    up_pre = jnp.dot(normed_mlp, weights[7], preferred_element_type=jnp.float32)
    hidden = (jax.nn.silu(gate_pre) * up_pre).astype(jnp.bfloat16)
    output = (resid + jnp.einsum("rf,df->rd", hidden, weights[8], preferred_element_type=jnp.float32)).astype(
        jnp.bfloat16
    )
    back_weights = weights
    grad_down = jnp.einsum("rd,rf->df", cotangent, hidden, preferred_element_type=jnp.float32)
    grad_hidden = jnp.einsum(
        "rd,df->rf", cotangent, back_weights[8], preferred_element_type=jnp.float32
    )
    sigmoid = jax.nn.sigmoid(gate_pre)
    grad_gate_pre = (grad_hidden * up_pre * sigmoid * (1.0 + gate_pre * (1.0 - sigmoid))).astype(
        jnp.bfloat16
    )
    grad_up_pre = (grad_hidden * (gate_pre * sigmoid)).astype(jnp.bfloat16)
    grad_gate = jnp.einsum(
        "rd,rf->df", normed_mlp, grad_gate_pre, preferred_element_type=jnp.float32
    )
    grad_up = jnp.einsum("rd,rf->df", normed_mlp, grad_up_pre, preferred_element_type=jnp.float32)
    grad_normed_mlp = jnp.einsum(
        "rf,df->rd", grad_gate_pre, back_weights[6], preferred_element_type=jnp.float32
    )
    grad_normed_mlp = grad_normed_mlp + jnp.einsum(
        "rf,df->rd", grad_up_pre, back_weights[7], preferred_element_type=jnp.float32
    )
    grad_mlp_gain = jnp.sum(grad_normed_mlp * scaled_mlp, axis=0)
    grad_resid = cotangent.astype(jnp.float32) + norm_back(
        grad_normed_mlp * back_weights[1].astype(jnp.float32), scaled_mlp, inverse_mlp
    )
    grad_branch = grad_resid.astype(jnp.bfloat16)
    grad_output = jnp.einsum("rd,rq->dq", grad_branch, mixture, preferred_element_type=jnp.float32)
    grad_mixture = jnp.einsum(
        "rd,dq->rq", grad_branch, back_weights[5], preferred_element_type=jnp.float32
    ).astype(jnp.bfloat16)
    grad_queries, grad_keys, grad_values = lax.map(
        attend_backward,
        (
            seq_queries,
            seq_keys,
            seq_values,
            segments,
            tops,
            totals,
            grad_mixture.reshape(seq_count, LEN, QW),
        ),
    )
    grad_query_raw = (
        rotate_back(grad_queries.reshape(row_count, Q_HEADS, HEAD_DIM), cosine, sine_table)
        .reshape(row_count, QW)
        .astype(jnp.bfloat16)
    )
    grad_key_raw = (
        rotate_back(grad_keys.reshape(row_count, KV_HEADS, HEAD_DIM), cosine, sine_table)
        .reshape(row_count, KVW)
        .astype(jnp.bfloat16)
    )
    grad_value_raw = grad_values.reshape(row_count, KVW).astype(jnp.bfloat16)
    grad_query = jnp.einsum(
        "rd,rq->dq", normed_attn, grad_query_raw, preferred_element_type=jnp.float32
    )
    grad_key = jnp.einsum(
        "rd,rq->dq", normed_attn, grad_key_raw, preferred_element_type=jnp.float32
    )
    grad_value = jnp.einsum(
        "rd,rq->dq", normed_attn, grad_value_raw, preferred_element_type=jnp.float32
    )
    grad_normed_attn = jnp.einsum(
        "rq,dq->rd", grad_query_raw, back_weights[2], preferred_element_type=jnp.float32
    )
    grad_normed_attn = grad_normed_attn + jnp.einsum(
        "rq,dq->rd", grad_key_raw, back_weights[3], preferred_element_type=jnp.float32
    )
    grad_normed_attn = grad_normed_attn + jnp.einsum(
        "rq,dq->rd", grad_value_raw, back_weights[4], preferred_element_type=jnp.float32
    )
    grad_attn_gain = jnp.sum(grad_normed_attn * scaled_attn, axis=0)
    grad_tokens = grad_resid + norm_back(
        grad_normed_attn * back_weights[0].astype(jnp.float32), scaled_attn, inverse_attn
    )

    def repack(grads, gain_grads):
        pieces = []
        for grad in grads:
            width = grad.shape[1] // lay.pieces
            pieces.append(grad.reshape(lay.shards, model_part, lay.pieces, width).transpose(2, 0, 1, 3))
        packed = jnp.concatenate(pieces, axis=-1)
        width = up(packed.shape[-1], 128)
        packed = jnp.pad(packed, ((0, 0), (0, 0), (0, 0), (0, width - packed.shape[-1])))
        if gain_grads:
            rows = jnp.stack([g.reshape(lay.shards, model_part) for g in gain_grads], axis=1)
            rows = jnp.pad(rows, ((0, 0), (0, 0), (0, width - model_part)))
            rows = jnp.broadcast_to(rows[None], (lay.pieces,) + rows.shape)
            packed = jnp.concatenate([packed, rows], axis=2)
        packed = jnp.pad(packed, ((0, 0), (0, 0), (0, rows_p - packed.shape[2]), (0, 0)))
        packed = packed.astype(BF16).reshape(lay.Y, lay.C, lay.Z, lay.X, rows_p, width)
        return packed.transpose(1, 0, 3, 2, 4, 5)

    mlp_sum = reduce_all(lay, repack((grad_gate, grad_up, grad_down), ()), 1)
    attn_sum = reduce_all(lay, repack((grad_query, grad_output, grad_key, grad_value), (grad_attn_gain, grad_mlp_gain)), 2)

    def own(packed, widths):
        parts, at = [], 0
        for width in widths:
            parts.append(packed[:model_part, at : at + width])
            at += width
        return parts

    own_gate, own_up, own_down = own(mlp_sum, mlp_widths)
    own_query, own_output, own_key, own_value = own(attn_sum, attn_widths)
    own_attn_gain = attn_sum[model_part, :model_part]
    own_mlp_gain = attn_sum[model_part + 1, :model_part]
    return (
        output,
        grad_tokens,
        own_attn_gain,
        own_mlp_gain,
        own_query,
        own_key,
        own_value,
        own_output.T,
        own_gate,
        own_up,
        own_down.T,
    )


def solution(mesh):
    in_specs = (
        P(("dp", "fsdp"), None),
        P(("dp", "fsdp"), None),
        P(("dp", "fsdp"), None),
        P("fsdp"),
        P("fsdp"),
        P("fsdp", "dp"),
        P("fsdp", "dp"),
        P("fsdp", "dp"),
        P("dp", "fsdp"),
        P("fsdp", "dp"),
        P("fsdp", "dp"),
        P("dp", "fsdp"),
        P(("dp", "fsdp"), None),
    )
    out_specs = (
        P(("dp", "fsdp"), None),
        P(("dp", "fsdp"), None),
        P("fsdp"),
        P("fsdp"),
        P("fsdp", "dp"),
        P("fsdp", "dp"),
        P("fsdp", "dp"),
        P("dp", "fsdp"),
        P("fsdp", "dp"),
        P("fsdp", "dp"),
        P("dp", "fsdp"),
    )
    return jax.shard_map(
        on_device, mesh=mesh, in_specs=in_specs, out_specs=out_specs, check_vma=False
    )
```

```python
import jax
import jax.numpy as jnp
from jax import lax
from jax.experimental import pallas as pl
from jax.experimental.pallas import tpu as pltpu
from jax.sharding import PartitionSpec as P


Q_HEADS = 9
KV_HEADS = 3
HEAD_DIM = 64
QW = 576
KVW = 192
EPS = 1e-05
ROPE_BASE = 100000.0
MASKED = -1e30
BF16 = jnp.bfloat16
F32 = jnp.float32
MESH = pl.DeviceIdType.MESH
ANY = pl.BlockSpec(memory_space=pl.ANY)
VMEM = pl.BlockSpec(memory_space=pltpu.VMEM)


def up(value, step):
    return -(-value // step) * step


class Layout:
    def __init__(self, pieces, shards):
        self.pieces, self.shards = pieces, shards
        self.C = 2 if pieces % 2 == 0 else 1
        self.Y = pieces // self.C
        self.X = 2 if shards <= 8 else 4
        self.Z = shards // self.X
        self.H = self.Z // 2
        self.slots = (self.C, self.Y, self.X, self.Z)
        n = (self.X - 1) + (self.Y - 1)
        self.gather_sems = 1 + (self.Z - 1) + 2 * n + 1 + 2 * n
        self.reduce_sems = 2 + 2 * n + (self.Z - 1)
        self.peers = (self.X - 1) + (self.Y - 1) + (self.Z - 1) + (self.C - 1)

    def here(self):
        dp, fs = lax.axis_index("dp"), lax.axis_index("fsdp")
        return lax.rem(dp, self.C), dp // self.C, lax.rem(fs, self.X), fs // self.X

    def device(self, c, y, x, z):
        return (y * self.C + c, z * self.X + x)

    def others(self, me, axis):
        size = self.slots[axis]
        for k in range(1, size):
            place = list(me)
            place[axis] = lax.rem(me[axis] + k, size)
            yield k, place

    def barrier(self, me):
        sem = pltpu.get_barrier_semaphore()
        for axis in range(4):
            for _, place in self.others(me, axis):
                pl.semaphore_signal(sem, inc=1, device_id=self.device(*place), device_id_type=MESH)
        pl.semaphore_wait(sem, self.peers)


class Sender:
    def __init__(self, layout, me, send, recv):
        self.lay, self.me, self.send, self.recv, self.used = layout, me, send, recv, 0

    def to(self, place, src, dst):
        k = self.used
        self.used += 1
        return pltpu.make_async_remote_copy(
            src_ref=src, dst_ref=dst, send_sem=self.send.at[k], recv_sem=self.recv.at[k],
            device_id=self.lay.device(*place), device_id_type=MESH)


def start(copies):
    for copy in copies:
        copy.start()


def wait(copies):
    for copy in copies:
        copy.wait()


class Gather:
    def __init__(self, lay, me, src, slots, send, recv):
        c, y, x, z = me
        s = Sender(lay, me, send, recv)
        X, Y, H, R = lay.X, lay.Y, lay.H, lay.Z - lay.H
        lo, hi = pl.ds(0, H), pl.ds(H, R)
        ax, ay = pl.ds(0, X), pl.ds(0, Y)
        sib = (1 - c, y, x, z)
        self.own = pltpu.make_async_copy(src, slots.at[c, y, x, z], recv.at[s.used])
        s.used += 1
        self.z = [s.to(p, src, slots.at[c, y, x, z]) for _, p in lay.others(me, 3)]
        part = slots.at[c, y, x, lo]
        self.xy1 = [s.to(p, part, part) for _, p in lay.others(me, 2)]
        part2 = slots.at[c, y, x, hi]
        self.xy1 += [s.to(p, part2, part2) for _, p in lay.others(me, 1)]
        part3 = slots.at[c, y, ax, lo]
        self.xy2 = [s.to(p, part3, part3) for _, p in lay.others(me, 1)]
        part4 = slots.at[c, ay, x, hi]
        self.xy2 += [s.to(p, part4, part4) for _, p in lay.others(me, 2)]
        self.core = [[], [], []]
        if lay.C > 1:
            whole = slots.at[c, y, x]
            self.core[0] = [s.to(sib, whole, whole)]
            for _, p in lay.others(me, 2):
                piece = slots.at[c, y, p[2], lo]
                self.core[1].append(s.to(sib, piece, piece))
            for _, p in lay.others(me, 1):
                piece = slots.at[c, p[1], x, hi]
                self.core[1].append(s.to(sib, piece, piece))
            for _, p in lay.others(me, 1):
                piece = slots.at[c, p[1], ax, lo]
                self.core[2].append(s.to(sib, piece, piece))
            for _, p in lay.others(me, 2):
                piece = slots.at[c, ay, p[2], hi]
                self.core[2].append(s.to(sib, piece, piece))

    def step(self, n):
        if n == 0:
            self.own.start()
            start(self.z)
        elif n == 1:
            self.own.wait()
            wait(self.z)
            start(self.xy1)
            start(self.core[0])
        elif n == 2:
            wait(self.xy1)
            start(self.xy2)
            start(self.core[1])
        elif n == 3:
            wait(self.xy2)
            start(self.core[2])
        else:
            for copies in self.core:
                wait(copies)


class Reduce:
    def __init__(self, lay, me, parts, bufs, send, recv, inplace):
        c, y, x, z = me
        self.lay, self.me = lay, me
        self.far, self.r2a, self.r2b, self.r3a, self.r3b, self.r4 = bufs[:6]
        self.out = parts.at[c] if inplace else bufs[6]
        s = Sender(lay, me, send, recv)
        X, Y, H, R = lay.X, lay.Y, lay.H, lay.Z - lay.H
        lo, hi = pl.ds(0, H), pl.ds(H, R)
        ax, ay = pl.ds(0, X), pl.ds(0, Y)
        out = self.out
        self.own = None if inplace else pltpu.make_async_copy(parts.at[c], self.out, recv.at[s.used])
        s.used += 1
        self.core = [s.to((1 - c, y, x, z), parts.at[1 - c], self.far)] if lay.C > 1 else []
        self.xy1 = [s.to(p, out.at[p[1], ax, lo], self.r2a.at[k - 1]) for k, p in lay.others(me, 1)]
        self.xy1 += [s.to(p, out.at[ay, p[2], hi], self.r2b.at[k - 1]) for k, p in lay.others(me, 2)]
        self.xy2 = [s.to(p, out.at[y, p[2], lo], self.r3a.at[k - 1]) for k, p in lay.others(me, 2)]
        self.xy2 += [s.to(p, out.at[p[1], x, hi], self.r3b.at[k - 1]) for k, p in lay.others(me, 1)]
        self.zs = [s.to(p, out.at[y, x, p[3]], self.r4.at[k - 1]) for k, p in lay.others(me, 3)]

    @staticmethod
    def scratch(lay, rows, width, inplace):
        X, Y, Z, H = lay.X, lay.Y, lay.Z, lay.H
        R = Z - H
        tail = (rows, width)
        return [
            pltpu.VMEM((Y, X, Z) + tail, BF16),
            pltpu.VMEM((Y - 1, X, H) + tail, BF16), pltpu.VMEM((X - 1, Y, R) + tail, BF16),
            pltpu.VMEM((X - 1, H) + tail, BF16), pltpu.VMEM((Y - 1, R) + tail, BF16),
            pltpu.VMEM((Z - 1,) + tail, BF16),
        ] + ([] if inplace else [pltpu.VMEM((Y, X, Z) + tail, BF16)])

    def step(self, n, result=None):
        lay, (c, y, x, z) = self.lay, self.me
        X, Y, Z, H = lay.X, lay.Y, lay.Z, lay.H
        out = self.out
        if n == 0:
            if self.own is not None:
                self.own.start()
            start(self.core)
        elif n == 1:
            if self.own is not None:
                self.own.wait()
            wait(self.core)

            @pl.loop(0, Y * X * Z)
            def _(i):
                yy, xx, zz = i // (X * Z), lax.rem(i // Z, X), lax.rem(i, Z)
                v = out[yy, xx, zz].astype(F32)
                if lay.C > 1:
                    v = v + self.far[yy, xx, zz].astype(F32)
                out[yy, xx, zz] = v.astype(BF16)

            start(self.xy1)
        elif n == 2:
            wait(self.xy1)

            @pl.loop(0, X * H)
            def _(i):
                xx, zz = i // H, lax.rem(i, H)
                v = out[y, xx, zz].astype(F32)
                for k in range(Y - 1):
                    v = v + self.r2a[k, xx, zz].astype(F32)
                out[y, xx, zz] = v.astype(BF16)

            @pl.loop(0, Y * (Z - H))
            def _(i):
                yy, zz = i // (Z - H), lax.rem(i, Z - H)
                v = out[yy, x, H + zz].astype(F32)
                for k in range(X - 1):
                    v = v + self.r2b[k, yy, zz].astype(F32)
                out[yy, x, H + zz] = v.astype(BF16)

            start(self.xy2)
        elif n == 3:
            wait(self.xy2)

            @pl.loop(0, H)
            def _(i):
                v = out[y, x, i].astype(F32)
                for k in range(X - 1):
                    v = v + self.r3a[k, i].astype(F32)
                out[y, x, i] = v.astype(BF16)

            @pl.loop(0, Z - H)
            def _(i):
                v = out[y, x, H + i].astype(F32)
                for k in range(Y - 1):
                    v = v + self.r3b[k, i].astype(F32)
                out[y, x, H + i] = v.astype(BF16)

            start(self.zs)
        else:
            wait(self.zs)
            v = out[y, x, z].astype(F32)
            for k in range(Z - 1):
                v = v + self.r4[k].astype(F32)
            result[...] = v


QB = 256


def dot(a, b, ca=1, cb=0):
    return lax.dot_general(a, b, (((ca,), (cb,)), ((), ())), preferred_element_type=F32)


def slot_of(lay, d, f):
    return (d % lay.C, d // lay.C, f % lay.X, f // lay.X)


def assemble(lay, slots, tmp, part, d, store):
    for f in range(lay.shards):
        tmp[f * part : (f + 1) * part, :] = slots[slot_of(lay, d, f)].astype(F32)[:part]
    store(d)


def params(which=None):
    extra = {} if which is None else dict(collective_id=which, has_side_effects=True)
    return pltpu.CompilerParams(vmem_limit_bytes=62 * 2**20, **extra)


def front(lay, part, attn_pack, mlp_pack, tokens, cosine, sine, kcols, qrows):
    T, D = tokens.shape
    E = QW + 2 * KVW
    nq, nk = QW // lay.pieces, KVW // lay.pieces
    width = attn_pack.shape[1]

    def kernel(a_ref, m_ref, x_ref, cos_ref, sin_ref, kc_ref, qr_ref,
               gm_ref, wqkv_ref, wo_ref, gain_ref, qa_ref, ka_ref, kv_ref, mix_ref, lse_ref,
               ga_ref, tmp, scaled, normed, wt, sa, ra, sm, rm):
        me = lay.here()
        lay.barrier(me)
        ga = Gather(lay, me, a_ref, ga_ref, sa, ra)
        gm = Gather(lay, me, m_ref, gm_ref, sm, rm)
        ga.step(0)
        for i in range(T // QB):
            rows = slice(i * QB, (i + 1) * QB)
            v = x_ref[rows, :].astype(F32)
            scaled[rows, :] = v * lax.rsqrt(jnp.mean(v * v, axis=1, keepdims=True) + EPS)
        ga.step(1)
        ga.step(2)
        ga.step(3)
        gm.step(0)
        ga.step(4)

        def store(d):
            wqkv_ref[:, d * nq : (d + 1) * nq] = tmp[:, 0:nq].astype(BF16)
            wo_ref[:, d * nq : (d + 1) * nq] = tmp[:, nq : 2 * nq].astype(BF16)
            wqkv_ref[:, QW + d * nk : QW + (d + 1) * nk] = tmp[:, 2 * nq : 2 * nq + nk].astype(BF16)
            at = QW + KVW
            wqkv_ref[:, at + d * nk : at + (d + 1) * nk] = tmp[:, 2 * nq + nk : 2 * nq + 2 * nk].astype(BF16)

        for d in range(lay.pieces):
            assemble(lay, ga_ref, tmp, part, d, store)
        for f in range(lay.shards):
            rows = ga_ref[slot_of(lay, 0, f)].astype(F32)
            gain_ref[0:2, f * part : (f + 1) * part] = rows[part : part + 2, 0:part]
        wt[...] = jnp.transpose(wqkv_ref[...])
        gain = gain_ref[0:1, :]
        for i in range(T // QB):
            rows = slice(i * QB, (i + 1) * QB)
            normed[rows, :] = (scaled[rows, :] * gain).astype(BF16)
        half = HEAD_DIM // 2

        @pl.loop(0, T // QB)
        def _(i):
            at = pl.multiple_of(i * QB, QB)
            cols = pl.ds(at, QB)
            raw = dot(wt[...], normed[cols, :], 1, 1)
            cs, sn = cos_ref[:, cols], sin_ref[:, cols]
            for h in range(Q_HEADS + KV_HEADS):
                u1, u2 = raw[h * HEAD_DIM : h * HEAD_DIM + half], raw[h * HEAD_DIM + half : (h + 1) * HEAD_DIM]
                o1 = (u1 * cs - u2 * sn).astype(BF16)
                o2 = (u2 * cs + u1 * sn).astype(BF16)
                if h < Q_HEADS:
                    scale = HEAD_DIM ** (-0.5)
                    qa_ref[h, 0:half, cols] = o1 * scale
                    qa_ref[h, half:HEAD_DIM, cols] = o2 * scale
                else:
                    g = (h - Q_HEADS) * HEAD_DIM
                    kv_ref[g : g + half, cols] = o1
                    kv_ref[g + half : g + HEAD_DIM, cols] = o2
            kv_ref[KVW:, cols] = raw[QW + KVW :].astype(BF16)

        gm.step(1)
        for h in range(Q_HEADS):
            qa_ref[h, HEAD_DIM:, :] = qr_ref[...]
        for g in range(KV_HEADS):
            ka_ref[g, :, 0:HEAD_DIM] = jnp.transpose(kv_ref[g * HEAD_DIM : (g + 1) * HEAD_DIM, :])
            ka_ref[g, :, HEAD_DIM:] = kc_ref[...]
        causal = lax.broadcasted_iota(jnp.int32, (QB, QB), 0) <= lax.broadcasted_iota(jnp.int32, (QB, QB), 1)
        for i in range(T // QB):
            q0, k0 = i * QB, 0 if i == 0 else 128

            @pl.loop(0, Q_HEADS)
            def _(h):
                g = h // (Q_HEADS // KV_HEADS)
                vrow = pl.ds(pl.multiple_of(KVW + g * HEAD_DIM, HEAD_DIM), HEAD_DIM)
                qcol = qa_ref[h, :, q0 : q0 + QB]
                s = jnp.where(causal, dot(ka_ref[g, q0 : q0 + QB, :], qcol), MASKED)
                top = jnp.max(s, axis=0, keepdims=True)
                if i:
                    s2 = dot(ka_ref[g, k0:q0, :], qcol)
                    top = jnp.maximum(top, jnp.max(s2, axis=0, keepdims=True))
                e = jnp.exp(s - top)
                total = jnp.sum(e, axis=0, keepdims=True)
                if i:
                    e2 = jnp.exp(s2 - top)
                    total = total + jnp.sum(e2, axis=0, keepdims=True)
                inv = 1.0 / total
                out = dot(kv_ref[vrow, q0 : q0 + QB], (e * inv).astype(BF16))
                if i:
                    out = out + dot(kv_ref[vrow, k0:q0], (e2 * inv).astype(BF16))
                mix_ref[pl.ds(pl.multiple_of(h * HEAD_DIM, HEAD_DIM), HEAD_DIM), q0 : q0 + QB] = out.astype(BF16)
                lse_ref[h, :, q0 : q0 + QB] = top + jnp.log(total)

            if i == 1:
                gm.step(2)
            if i == 2:
                gm.step(3)
        gm.step(4)

    n = lay.gather_sems
    sd = jax.ShapeDtypeStruct
    aug = HEAD_DIM + 16
    return pl.pallas_call(
        kernel,
        out_shape=[sd(lay.slots + mlp_pack.shape, BF16), sd((D, E), BF16), sd((D, QW), BF16), sd((8, D), F32),
                   sd((Q_HEADS, aug, T), BF16), sd((KV_HEADS, T, aug), BF16), sd((2 * KVW, T), BF16), sd((QW, T), BF16),
                   sd((Q_HEADS, 1, T), F32)],
        in_specs=[VMEM] * 7, out_specs=[ANY] + [VMEM] * 8,
        scratch_shapes=[pltpu.VMEM(lay.slots + attn_pack.shape, BF16), pltpu.VMEM((D, width), F32), pltpu.VMEM((T, D), F32),
                        pltpu.VMEM((T, D), BF16), pltpu.VMEM((E, D), BF16)] + [pltpu.SemaphoreType.DMA((n,))] * 4,
        compiler_params=params(0), name="gather_attend",
    )(attn_pack, mlp_pack, tokens, cosine, sine, kcols, qrows)


def middle(lay, part, gm, mix, wo, gain, tokens, cotangent):
    T, D = tokens.shape
    FF = 1536
    nf = FF // lay.pieces
    rows_p, width = gm.shape[-2:]

    def kernel(gm_ref, mix_ref, wo_ref, gain_ref, x_ref, c_ref, out_ref, gr_ref, parts_ref, gg_ref,
               tmp, wg, wu, wd, mixn, normed, hidden, dgate, dup, nt, ct):
        def store(d):
            wg[:, d * nf : (d + 1) * nf] = tmp[:, 0:nf].astype(BF16)
            wu[:, d * nf : (d + 1) * nf] = tmp[:, nf : 2 * nf].astype(BF16)
            wd[:, d * nf : (d + 1) * nf] = tmp[:, 2 * nf : 3 * nf].astype(BF16)

        for d in range(lay.pieces):
            assemble(lay, gm_ref, tmp, part, d, store)
        mixn[...] = jnp.transpose(mix_ref[...])
        ct[...] = jnp.transpose(c_ref[...])
        gain = gain_ref[1:2, :]
        gg_ref[...] = jnp.zeros_like(gg_ref)

        @pl.loop(0, T // QB)
        def _(i):
            rows = pl.ds(pl.multiple_of(i * QB, QB), QB)
            cot = c_ref[rows, :]
            resid = x_ref[rows, :].astype(F32) + dot(mixn[rows, :], wo_ref[...], 1, 1)
            inverse = lax.rsqrt(jnp.mean(resid * resid, axis=1, keepdims=True) + EPS)
            scaled = resid * inverse
            nb = (scaled * gain).astype(BF16)
            normed[rows, :] = nb
            out = resid
            gnm = jnp.zeros_like(resid)
            for j in range(FF // 512):
                cols = slice(j * 512, (j + 1) * 512)
                gate = dot(nb, wg[:, cols])
                upp = dot(nb, wu[:, cols])
                gh = dot(cot, wd[:, cols])
                s = jax.nn.sigmoid(gate)
                act = gate * s
                hb = (act * upp).astype(BF16)
                hidden[rows, cols] = hb
                dg = (gh * upp * (s * (1.0 + gate * (1.0 - s)))).astype(BF16)
                du = (gh * act).astype(BF16)
                dgate[rows, cols] = dg
                dup[rows, cols] = du
                out = out + dot(hb, wd[:, cols], 1, 1)
                gnm = gnm + dot(dg, wg[:, cols], 1, 1) + dot(du, wu[:, cols], 1, 1)
            out_ref[rows, :] = out.astype(BF16)
            gg_ref[0:1, :] += jnp.sum(gnm * scaled, axis=0, keepdims=True)
            m = gnm * gain
            back = inverse * (m - scaled * jnp.mean(m * scaled, axis=1, keepdims=True))
            gr_ref[rows, :] = cot.astype(F32) + back

        nt[...] = jnp.transpose(normed[...])
        for d in range(lay.pieces):
            cols = slice(d * nf, (d + 1) * nf)
            for k, (left, right) in enumerate(((nt, dgate), (nt, dup), (ct, hidden))):
                tmp[:, k * nf : (k + 1) * nf] = dot(left[...], right[:, cols])
            for f in range(lay.shards):
                parts_ref[slot_of(lay, d, f) + (slice(0, part),)] = tmp[f * part : (f + 1) * part, :].astype(BF16)

    sd = jax.ShapeDtypeStruct
    return pl.pallas_call(
        kernel,
        out_shape=[sd((T, D), BF16), sd((T, D), F32), sd(gm.shape, BF16), sd((8, D), F32)],
        in_specs=[VMEM] * 6, out_specs=[VMEM] * 4,
        scratch_shapes=[pltpu.VMEM((D, width), F32)] + [pltpu.VMEM((D, FF), BF16)] * 3
        + [pltpu.VMEM((T, D), BF16)] * 2 + [pltpu.VMEM((T, FF), BF16)] * 3 + [pltpu.VMEM((D, T), BF16)] * 2,
        compiler_params=params(), name="mlp",
    )(gm, mix, wo, gain, tokens, cotangent)


def split_rows(value, first, base):
    hi = value.astype(BF16).astype(F32)
    mid = (value - hi).astype(BF16).astype(F32)
    low = value - hi - mid
    row = lax.broadcasted_iota(jnp.int32, base.shape, 0)
    return jnp.where(row == first, hi, jnp.where(row == first + 1, mid, jnp.where(row == first + 2, low, base)))


def back(lay, part, mlp_parts, gr, tokens, mix, qa, ka, kv, lse, wqkv, wo, gain, ggain, cosine, sine, qrows, attn_shape):
    T, D = tokens.shape
    E = QW + 2 * KVW
    nq, nk = QW // lay.pieces, KVW // lay.pieces
    aug = HEAD_DIM + 16
    half = HEAD_DIM // 2

    def kernel(p_ref, gr_ref, x_ref, mix_ref, qa_ref, ka_ref, kv_ref, lse_ref, wqkv_ref, wo_ref, gain_ref, gg_ref,
               cos_ref, sin_ref, qr_ref, gt_ref, om_ref, oa_ref, *rest):
        mbufs, abufs, rest = rest[:7], rest[7:13], rest[13:]
        (gb, don, doa, qn, qb, va, dk, dv, dq, draw, tmp_n, dw, tmp, gsl, pa, sm, rm, sa, ra) = rest
        me = lay.here()
        lay.barrier(me)
        red = Reduce(lay, me, p_ref, mbufs, sm, rm, False)
        red.step(0)
        gb[...] = gr_ref[...].astype(BF16)
        for i in range(T // QB):
            rows = slice(i * QB, (i + 1) * QB)
            full = dot(gb[rows, :], wo_ref[...]).astype(BF16)
            for h in range(Q_HEADS):
                don[h, rows, :] = full[:, h * HEAD_DIM : (h + 1) * HEAD_DIM]
        zero = jnp.zeros((16, T), F32)
        base = qr_ref[...].astype(F32)

        @pl.loop(0, Q_HEADS)
        def _(h):
            t = jnp.transpose(don[h])
            doa[h, 0:HEAD_DIM, :] = t
            m = mix_ref[pl.ds(pl.multiple_of(h * HEAD_DIM, HEAD_DIM), HEAD_DIM), :]
            delta = jnp.sum(t.astype(F32) * m.astype(F32), axis=0, keepdims=True)
            doa[h, HEAD_DIM:, :] = split_rows(-delta, 0, zero).astype(BF16)
            q = qa_ref[h, 0:HEAD_DIM, :]
            qn[h] = jnp.transpose(q)
            qb[h, 0:HEAD_DIM, :] = q
            qb[h, HEAD_DIM:, :] = split_rows(-lse_ref[h], 3, base).astype(BF16)

        ones = jnp.where(lax.broadcasted_iota(jnp.int32, (T, 16), 1) < 3, 1.0, 0.0).astype(BF16)
        for g in range(KV_HEADS):
            va[g, :, 0:HEAD_DIM] = jnp.transpose(kv_ref[KVW + g * HEAD_DIM : KVW + (g + 1) * HEAD_DIM, :])
            va[g, :, HEAD_DIM:] = ones
        dk[...] = jnp.zeros_like(dk)
        dv[...] = jnp.zeros_like(dv)
        causal = lax.broadcasted_iota(jnp.int32, (QB, QB), 0) <= lax.broadcasted_iota(jnp.int32, (QB, QB), 1)

        @pl.loop(0, Q_HEADS)
        def _(h):
            g = h // (Q_HEADS // KV_HEADS)
            krow = pl.ds(pl.multiple_of(g * HEAD_DIM, HEAD_DIM), HEAD_DIM)
            for j in range(T // QB):
                k0, k1 = j * QB, (j + 1) * QB
                blocks = [(k0, k1, k0, k1, True)]
                if k1 < T:
                    blocks.append((k0 if j else 128, k1, k1, T, False))
                for a, b, c, d, diagonal in blocks:
                    st = dot(ka_ref[g, a:b, :], qb[h, :, c:d])
                    p = jnp.exp(st)
                    if diagonal:
                        p = jnp.where(causal, p, 0.0)
                    dp = dot(va[g, a:b, :], doa[h, :, c:d])
                    ds = (p * dp).astype(BF16)
                    dv[g, a:b, :] += dot(p.astype(BF16), don[h, c:d, :])
                    dk[g, a:b, :] += dot(ds, qn[h, c:d, :])
                    part_q = dot(kv_ref[krow, a:b], ds)
                    if j == 0:
                        dq[:, c:d] = part_q
                    else:
                        dq[:, c:d] += part_q
            scale = HEAD_DIM ** (-0.5)
            d1, d2 = dq[0:half, :] * scale, dq[half:, :] * scale
            cs, sn = cos_ref[...], sin_ref[...]
            at = pl.multiple_of(h * HEAD_DIM, HEAD_DIM)
            draw[pl.ds(at, half), :] = (d1 * cs + d2 * sn).astype(BF16)
            draw[pl.ds(at + half, half), :] = (d2 * cs - d1 * sn).astype(BF16)
            for n, when in ((1, 1), (2, 4), (3, 6)):

                @pl.when(h == when)
                def _():
                    red.step(n)

        cs, sn = cos_ref[...], sin_ref[...]
        for g in range(KV_HEADS):
            t = jnp.transpose(dk[g])
            d1, d2 = t[0:half], t[half:]
            at = QW + g * HEAD_DIM
            draw[at : at + half, :] = (d1 * cs + d2 * sn).astype(BF16)
            draw[at + half : at + HEAD_DIM, :] = (d2 * cs - d1 * sn).astype(BF16)
            at = QW + KVW + g * HEAD_DIM
            draw[at : at + HEAD_DIM, :] = jnp.transpose(dv[g]).astype(BF16)
        red.step(4, om_ref)
        again = gain_ref[0:1, :]
        gattn = jnp.zeros((1, D), F32)
        for i in range(T // QB):
            rows = slice(i * QB, (i + 1) * QB)
            v = x_ref[rows, :].astype(F32)
            inverse = lax.rsqrt(jnp.mean(v * v, axis=1, keepdims=True) + EPS)
            scaled = v * inverse
            gna = dot(jnp.transpose(draw[:, rows]), wqkv_ref[...], 1, 1)
            gattn = gattn + jnp.sum(gna * scaled, axis=0, keepdims=True)
            m = gna * again
            gt_ref[rows, :] = gr_ref[rows, :] + inverse * (m - scaled * jnp.mean(m * scaled, axis=1, keepdims=True))
            tmp_n[rows, :] = (scaled * again).astype(BF16)
        gsl[...] = jnp.zeros_like(gsl)
        gmlp = gg_ref[0:1, :]
        for f in range(lay.shards):
            gsl[f, 0:1, 0:part] = gattn[:, f * part : (f + 1) * part]
            gsl[f, 1:2, 0:part] = gmlp[:, f * part : (f + 1) * part]
        dw[:, 0:E] = dot(jnp.transpose(tmp_n[...]), draw[...], 1, 1)
        dw[:, 1024 : 1024 + QW] = dot(jnp.transpose(gb[...]), mix_ref[...], 1, 1)
        for d in range(lay.pieces):
            tmp[:, 0:nq] = dw[:, d * nq : (d + 1) * nq]
            tmp[:, nq : 2 * nq] = dw[:, 1024 + d * nq : 1024 + (d + 1) * nq]
            tmp[:, 2 * nq : 2 * nq + nk] = dw[:, QW + d * nk : QW + (d + 1) * nk]
            tmp[:, 2 * nq + nk : 2 * nq + 2 * nk] = dw[:, QW + KVW + d * nk : QW + KVW + (d + 1) * nk]
            for f in range(lay.shards):
                slot = slot_of(lay, d, f)
                pa[slot + (slice(0, part),)] = tmp[f * part : (f + 1) * part, :].astype(BF16)
                pa[slot + (slice(part, part + 2),)] = gsl[f, 0:2, :].astype(BF16)
        ared = Reduce(lay, me, pa, abufs, sa, ra, True)
        for n in range(5):
            ared.step(n, oa_ref)

    n = lay.reduce_sems
    sd = jax.ShapeDtypeStruct
    rows_p, width = attn_shape
    mshape = mlp_parts.shape[-2:]
    V = pltpu.VMEM
    return pl.pallas_call(
        kernel,
        out_shape=[sd((T, D), F32), sd(mshape, F32), sd((rows_p, width), F32)],
        in_specs=[ANY] + [VMEM] * 14, out_specs=[VMEM] * 3,
        scratch_shapes=Reduce.scratch(lay, *mshape, False) + Reduce.scratch(lay, rows_p, width, True)
        + [V((T, D), BF16), V((Q_HEADS, T, HEAD_DIM), BF16), V((Q_HEADS, aug, T), BF16), V((Q_HEADS, T, HEAD_DIM), BF16),
           V((Q_HEADS, aug, T), BF16), V((KV_HEADS, T, aug), BF16), V((KV_HEADS, T, HEAD_DIM), F32),
           V((KV_HEADS, T, HEAD_DIM), F32), V((HEAD_DIM, T), F32), V((E, T), BF16), V((T, D), BF16), V((D, 1024 + QW), F32), V((D, width), F32),
           V((lay.shards, 8, width), F32), V(lay.slots + (rows_p, width), BF16)]
        + [pltpu.SemaphoreType.DMA((n,))] * 4,
        compiler_params=params(1), name="attend_back",
    )(mlp_parts, gr, tokens, mix, qa, ka, kv, lse, wqkv, wo, gain, ggain, cosine, sine, qrows)


def pack(parts, gains, rows_p):
    packed = jnp.concatenate(parts, axis=1)
    width = up(packed.shape[1], 128)
    packed = jnp.pad(packed, ((0, 0), (0, width - packed.shape[1])))
    if gains:
        rows = jnp.stack([jnp.pad(g, (0, width - g.shape[0])) for g in gains])
        packed = jnp.concatenate([packed, rows], axis=0)
    return jnp.pad(packed, ((0, rows_p - packed.shape[0]), (0, 0)))


def on_device(tokens, segments, positions, attn_gain, mlp_gain, w_query, w_key, w_value, w_output, w_gate, w_up, w_down, cotangent):
    lay = Layout(lax.axis_size("dp"), lax.axis_size("fsdp"))
    part = attn_gain.shape[0]
    rows_p = up(part + 2, 16)
    nq, nk, nf = w_query.shape[1], w_key.shape[1], w_gate.shape[1]
    attn_pack = pack((w_query, w_output.T, w_key, w_value), (attn_gain, mlp_gain), rows_p)
    mlp_pack = pack((w_gate, w_up, w_down.T), (), rows_p)
    half = HEAD_DIM // 2
    frequency = ROPE_BASE ** (-(2.0 * jnp.arange(half, dtype=jnp.float32)) / HEAD_DIM)
    angles = frequency[:, None] * positions.astype(jnp.float32)
    cosine, sine = jnp.cos(angles), jnp.sin(angles)
    row = jnp.arange(16, dtype=jnp.int32)[:, None]
    qrows = jnp.where((row < 3) & (row != segments), MASKED, 0.0).astype(BF16)
    kcols = (((row < 3) & (row == segments)) | ((row >= 3) & (row < 6))).astype(BF16).T
    gm, wqkv, wo, gain, qa, ka, kv, mix, lse = front(lay, part, attn_pack, mlp_pack, tokens, cosine, sine, kcols, qrows)
    output, gr, parts, ggain = middle(lay, part, gm, mix, wo, gain, tokens, cotangent)
    grad_tokens, mlp_sum, attn_sum = back(
        lay, part, parts, gr, tokens, mix, qa, ka, kv, lse, wqkv, wo, gain, ggain, cosine, sine, qrows, attn_pack.shape)
    m, a = mlp_sum[:part], attn_sum[:part]
    return (
        output, grad_tokens, attn_sum[part, :part], attn_sum[part + 1, :part],
        a[:, :nq], a[:, 2 * nq : 2 * nq + nk], a[:, 2 * nq + nk : 2 * nq + 2 * nk], a[:, nq : 2 * nq].T,
        m[:, :nf], m[:, nf : 2 * nf], m[:, 2 * nf : 3 * nf].T,
    )


def solution(mesh):
    in_specs = (
        P(("dp", "fsdp"), None),
        P(("dp", "fsdp"), None),
        P(("dp", "fsdp"), None),
        P("fsdp"),
        P("fsdp"),
        P("fsdp", "dp"),
        P("fsdp", "dp"),
        P("fsdp", "dp"),
        P("dp", "fsdp"),
        P("fsdp", "dp"),
        P("fsdp", "dp"),
        P("dp", "fsdp"),
        P(("dp", "fsdp"), None),
    )
    out_specs = (
        P(("dp", "fsdp"), None),
        P(("dp", "fsdp"), None),
        P("fsdp"),
        P("fsdp"),
        P("fsdp", "dp"),
        P("fsdp", "dp"),
        P("fsdp", "dp"),
        P("dp", "fsdp"),
        P("fsdp", "dp"),
        P("fsdp", "dp"),
        P("dp", "fsdp"),
    )
    return jax.shard_map(
        on_device, mesh=mesh, in_specs=in_specs, out_specs=out_specs, check_vma=False
    )
```

```python
import numpy as np

import jax
import jax.numpy as jnp
from jax import lax
from jax.experimental import pallas as pl
from jax.experimental.pallas import tpu as pltpu
from jax.sharding import PartitionSpec as P


Q_HEADS = 9
KV_HEADS = 3
HEAD_DIM = 64
QW = 576
KVW = 192
EPS = 1e-05
ROPE_BASE = 100000.0
MASKED = -1e30
BF16 = jnp.bfloat16
F32 = jnp.float32
MESH = pl.DeviceIdType.MESH
ANY = pl.BlockSpec(memory_space=pl.ANY)
VMEM = pl.BlockSpec(memory_space=pltpu.VMEM)


def up(value, step):
    return -(-value // step) * step


class Layout:
    def __init__(self, pieces, shards):
        self.pieces, self.shards = pieces, shards
        self.C = 2 if pieces % 2 == 0 else 1
        self.Y = pieces // self.C
        self.X = 2 if shards <= 8 else 4
        self.Z = shards // self.X
        self.H = self.Z // 2
        self.slots = (self.C, self.Y, self.X, self.Z)
        n = (self.X - 1) + (self.Y - 1)
        self.gather_sems = 1 + (self.Z - 1) + 2 * n + 1 + 2 * n
        self.reduce_sems = 2 + 2 * n + (self.Z - 1)
        self.peers = (self.X - 1) + (self.Y - 1) + (self.Z - 1) + (self.C - 1)

    def here(self):
        dp, fs = lax.axis_index("dp"), lax.axis_index("fsdp")
        return lax.rem(dp, self.C), dp // self.C, lax.rem(fs, self.X), fs // self.X

    def device(self, c, y, x, z):
        return (y * self.C + c, z * self.X + x)

    def others(self, me, axis):
        size = self.slots[axis]
        for k in range(1, size):
            place = list(me)
            place[axis] = lax.rem(me[axis] + k, size)
            yield k, place

    def barrier(self, me):
        sem = pltpu.get_barrier_semaphore()
        for axis in range(4):
            for _, place in self.others(me, axis):
                pl.semaphore_signal(sem, inc=1, device_id=self.device(*place), device_id_type=MESH)
        pl.semaphore_wait(sem, self.peers)


class Sender:
    def __init__(self, layout, me, send, recv):
        self.lay, self.me, self.send, self.recv, self.used = layout, me, send, recv, 0

    def to(self, place, src, dst):
        k = self.used
        self.used += 1
        return pltpu.make_async_remote_copy(
            src_ref=src, dst_ref=dst, send_sem=self.send.at[k], recv_sem=self.recv.at[k],
            device_id=self.lay.device(*place), device_id_type=MESH)


def start(copies):
    for copy in copies:
        copy.start()


def wait(copies):
    for copy in copies:
        copy.wait()


class Gather:
    def __init__(self, lay, me, src, slots, send, recv):
        c, y, x, z = me
        s = Sender(lay, me, send, recv)
        X, Y, H, R = lay.X, lay.Y, lay.H, lay.Z - lay.H
        lo, hi = pl.ds(0, H), pl.ds(H, R)
        ax, ay = pl.ds(0, X), pl.ds(0, Y)
        sib = (1 - c, y, x, z)
        self.own = pltpu.make_async_copy(src, slots.at[c, y, x, z], recv.at[s.used])
        s.used += 1
        self.z = [s.to(p, src, slots.at[c, y, x, z]) for _, p in lay.others(me, 3)]
        part = slots.at[c, y, x, lo]
        self.xy1 = [s.to(p, part, part) for _, p in lay.others(me, 2)]
        part2 = slots.at[c, y, x, hi]
        self.xy1 += [s.to(p, part2, part2) for _, p in lay.others(me, 1)]
        part3 = slots.at[c, y, ax, lo]
        self.xy2 = [s.to(p, part3, part3) for _, p in lay.others(me, 1)]
        part4 = slots.at[c, ay, x, hi]
        self.xy2 += [s.to(p, part4, part4) for _, p in lay.others(me, 2)]
        self.core = [[], [], []]
        if lay.C > 1:
            whole = slots.at[c, y, x]
            self.core[0] = [s.to(sib, whole, whole)]
            for _, p in lay.others(me, 2):
                piece = slots.at[c, y, p[2], lo]
                self.core[1].append(s.to(sib, piece, piece))
            for _, p in lay.others(me, 1):
                piece = slots.at[c, p[1], x, hi]
                self.core[1].append(s.to(sib, piece, piece))
            for _, p in lay.others(me, 1):
                piece = slots.at[c, p[1], ax, lo]
                self.core[2].append(s.to(sib, piece, piece))
            for _, p in lay.others(me, 2):
                piece = slots.at[c, ay, p[2], hi]
                self.core[2].append(s.to(sib, piece, piece))

    def step(self, n):
        if n == 0:
            self.own.start()
            start(self.z)
        elif n == 1:
            self.own.wait()
            wait(self.z)
            start(self.xy1)
            start(self.core[0])
        elif n == 2:
            wait(self.xy1)
            start(self.xy2)
            start(self.core[1])
        elif n == 3:
            wait(self.xy2)
            start(self.core[2])
        else:
            for copies in self.core:
                wait(copies)


class Reduce:
    def __init__(self, lay, me, parts, bufs, send, recv, inplace):
        c, y, x, z = me
        self.lay, self.me = lay, me
        self.far, self.r2a, self.r2b, self.r3a, self.r3b, self.r4 = bufs[:6]
        self.out = parts.at[c] if inplace else bufs[6]
        s = Sender(lay, me, send, recv)
        X, Y, H, R = lay.X, lay.Y, lay.H, lay.Z - lay.H
        lo, hi = pl.ds(0, H), pl.ds(H, R)
        ax, ay = pl.ds(0, X), pl.ds(0, Y)
        out = self.out
        self.own = None if inplace else pltpu.make_async_copy(parts.at[c], self.out, recv.at[s.used])
        s.used += 1
        self.core = [s.to((1 - c, y, x, z), parts.at[1 - c], self.far)] if lay.C > 1 else []
        self.xy1 = [s.to(p, out.at[p[1], ax, lo], self.r2a.at[k - 1]) for k, p in lay.others(me, 1)]
        self.xy1 += [s.to(p, out.at[ay, p[2], hi], self.r2b.at[k - 1]) for k, p in lay.others(me, 2)]
        self.xy2 = [s.to(p, out.at[y, p[2], lo], self.r3a.at[k - 1]) for k, p in lay.others(me, 2)]
        self.xy2 += [s.to(p, out.at[p[1], x, hi], self.r3b.at[k - 1]) for k, p in lay.others(me, 1)]
        self.zs = [s.to(p, out.at[y, x, p[3]], self.r4.at[k - 1]) for k, p in lay.others(me, 3)]

    @staticmethod
    def scratch(lay, rows, width, inplace):
        X, Y, Z, H = lay.X, lay.Y, lay.Z, lay.H
        R = Z - H
        tail = (rows, width)
        return [
            pltpu.VMEM((Y, X, Z) + tail, BF16),
            pltpu.VMEM((Y - 1, X, H) + tail, BF16), pltpu.VMEM((X - 1, Y, R) + tail, BF16),
            pltpu.VMEM((X - 1, H) + tail, BF16), pltpu.VMEM((Y - 1, R) + tail, BF16),
            pltpu.VMEM((Z - 1,) + tail, BF16),
        ] + ([] if inplace else [pltpu.VMEM((Y, X, Z) + tail, BF16)])

    def step(self, n, result=None):
        lay, (c, y, x, z) = self.lay, self.me
        X, Y, Z, H = lay.X, lay.Y, lay.Z, lay.H
        out = self.out
        if n == 0:
            if self.own is not None:
                self.own.start()
            start(self.core)
        elif n == 1:
            if self.own is not None:
                self.own.wait()
            wait(self.core)

            @pl.loop(0, Y * X * Z)
            def _(i):
                yy, xx, zz = i // (X * Z), lax.rem(i // Z, X), lax.rem(i, Z)
                v = out[yy, xx, zz].astype(F32)
                if lay.C > 1:
                    v = v + self.far[yy, xx, zz].astype(F32)
                out[yy, xx, zz] = v.astype(BF16)

            start(self.xy1)
        elif n == 2:
            wait(self.xy1)

            @pl.loop(0, X * H)
            def _(i):
                xx, zz = i // H, lax.rem(i, H)
                v = out[y, xx, zz].astype(F32)
                for k in range(Y - 1):
                    v = v + self.r2a[k, xx, zz].astype(F32)
                out[y, xx, zz] = v.astype(BF16)

            @pl.loop(0, Y * (Z - H))
            def _(i):
                yy, zz = i // (Z - H), lax.rem(i, Z - H)
                v = out[yy, x, H + zz].astype(F32)
                for k in range(X - 1):
                    v = v + self.r2b[k, yy, zz].astype(F32)
                out[yy, x, H + zz] = v.astype(BF16)

            start(self.xy2)
        elif n == 3:
            wait(self.xy2)

            @pl.loop(0, H)
            def _(i):
                v = out[y, x, i].astype(F32)
                for k in range(X - 1):
                    v = v + self.r3a[k, i].astype(F32)
                out[y, x, i] = v.astype(BF16)

            @pl.loop(0, Z - H)
            def _(i):
                v = out[y, x, H + i].astype(F32)
                for k in range(Y - 1):
                    v = v + self.r3b[k, i].astype(F32)
                out[y, x, H + i] = v.astype(BF16)

            start(self.zs)
        else:
            wait(self.zs)
            v = out[y, x, z].astype(F32)
            for k in range(Z - 1):
                v = v + self.r4[k].astype(F32)
            result[...] = v


QB = 256


def dot(a, b, ca=1, cb=0):
    return lax.dot_general(a, b, (((ca,), (cb,)), ((), ())), preferred_element_type=F32)


def slot_of(lay, d, f):
    return (d % lay.C, d // lay.C, f % lay.X, f // lay.X)


def groups_of(nf, nq):
    if nf % 128 == 0:
        return (((0, 0, nf),), ((1, 0, nf),), ((2, 0, nf), (3, nf, nq)))
    return (((0, 0, nf), (1, nf, nf)), ((2, 0, nf), (3, nf, nq)))


def width_of(group):
    return up(group[-1][1] + group[-1][2], 128)


def params(which=None):
    extra = {} if which is None else dict(collective_id=which, has_side_effects=True)
    return pltpu.CompilerParams(vmem_limit_bytes=62 * 2**20, **extra)


def eye(n):
    return (lax.broadcasted_iota(jnp.int32, (n, n), 0) == lax.broadcasted_iota(jnp.int32, (n, n), 1)).astype(F32).astype(BF16)


def column(one, ref):
    wide = jnp.broadcast_to(ref[...].astype(F32), (16, ref.shape[1])).astype(BF16)
    return dot(one, wide, 1, 1)[:, 0:1].astype(BF16)


def front(lay, weights, gains, xt, segments, positions, frequency):
    wq, wkt, wvt, wo, wg, wu, wdt = weights
    part, nq = wq.shape
    nk, nf = wkt.shape[0], wg.shape[1]
    rows_p = up(part, 16)
    wa = up(nq + 2 * nk + 2, 128)
    D, T = xt.shape
    E = QW + 2 * KVW
    half = HEAD_DIM // 2
    groups = groups_of(nf, nq)
    G = len(groups)
    aug = HEAD_DIM + 16

    def kernel(wq_ref, wkt_ref, wvt_ref, wo_in, wg_ref, wu_ref, wdt_ref, ag_ref, mg_ref, x_ref, seg_ref, pos_ref, fr_ref, *rest):
        gms, rest = rest[:G], rest[G:]
        (wqkv_ref, gain_ref, nt_ref, qa_ref, ka_ref, kv_ref, mix_ref, lse_ref, cos_ref, sin_ref), rest = rest[:10], rest[10:]
        pms, rest = rest[:G], rest[G:]
        (pa, ga_ref, tmp, scaled, wt, kt), sems = rest[:6], rest[6:]
        one = eye(part)
        pa[0:part, 0:nq] = wq_ref[...]
        pa[0:part, nq : nq + nk] = dot(one, wkt_ref[...], 1, 1).astype(BF16)
        pa[0:part, nq + nk : nq + 2 * nk] = dot(one, wvt_ref[...], 1, 1).astype(BF16)
        pa[0:part, nq + 2 * nk : nq + 2 * nk + 1] = column(one, ag_ref)
        pa[0:part, nq + 2 * nk + 1 : nq + 2 * nk + 2] = column(one, mg_ref)
        me = lay.here()
        lay.barrier(me)
        ga = Gather(lay, me, pa, ga_ref, sems[0], sems[1])
        gm = [Gather(lay, me, pms[k], gms[k], sems[2 + 2 * k], sems[3 + 2 * k]) for k in range(G)]
        ga.step(0)
        for k, group in enumerate(groups):
            for which, at, size in group:
                if which == 3:
                    pms[k][0:part, at : at + size] = dot(one, wo_in[...], 1, 1).astype(BF16)
                else:
                    pms[k][0:part, at : at + size] = (wg_ref, wu_ref, wdt_ref)[which][...]
        v = x_ref[...].astype(F32)
        scaled[...] = v * lax.rsqrt(jnp.mean(v * v, axis=0, keepdims=True) + EPS)
        angles = fr_ref[...] * pos_ref[...].astype(F32)
        cos_ref[...] = jnp.cos(angles)
        sin_ref[...] = jnp.sin(angles)
        ga.step(1)
        gm[0].step(0)
        ga.step(2)
        ga.step(3)
        gm[0].step(1)
        gm[1].step(0)
        ga.step(4)
        for d in range(lay.pieces):
            for f in range(lay.shards):
                tmp[f * part : (f + 1) * part, :] = ga_ref[slot_of(lay, d, f)].astype(F32)[:part]
            wqkv_ref[:, d * nq : (d + 1) * nq] = tmp[:, 0:nq].astype(BF16)
            wqkv_ref[:, QW + d * nk : QW + (d + 1) * nk] = tmp[:, nq : nq + nk].astype(BF16)
            wqkv_ref[:, QW + KVW + d * nk : QW + KVW + (d + 1) * nk] = tmp[:, nq + nk : nq + 2 * nk].astype(BF16)
        gain_ref[:, 0:2] = tmp[:, nq + 2 * nk : nq + 2 * nk + 2]
        gm[0].step(2)
        gm[1].step(1)
        if G > 2:
            gm[2].step(0)
        wt[...] = jnp.transpose(wqkv_ref[...])
        nt_ref[...] = (scaled[...] * gain_ref[:, 0:1]).astype(BF16)

        @pl.loop(0, T // QB)
        def _(i):
            cols = pl.ds(pl.multiple_of(i * QB, QB), QB)
            raw = dot(wt[...], nt_ref[:, cols])
            cs, sn = cos_ref[:, cols], sin_ref[:, cols]
            for h in range(Q_HEADS + KV_HEADS):
                u1, u2 = raw[h * HEAD_DIM : h * HEAD_DIM + half], raw[h * HEAD_DIM + half : (h + 1) * HEAD_DIM]
                o1 = (u1 * cs - u2 * sn).astype(BF16)
                o2 = (u2 * cs + u1 * sn).astype(BF16)
                if h < Q_HEADS:
                    scale = HEAD_DIM ** (-0.5)
                    qa_ref[h, 0:half, cols] = o1 * scale
                    qa_ref[h, half:HEAD_DIM, cols] = o2 * scale
                else:
                    g = (h - Q_HEADS) * HEAD_DIM
                    kv_ref[g : g + half, cols] = o1
                    kv_ref[g + half : g + HEAD_DIM, cols] = o2
            kv_ref[KVW:, cols] = raw[QW + KVW :].astype(BF16)

        gm[0].step(3)
        gm[1].step(2)
        if G > 2:
            gm[2].step(1)
        row = lax.broadcasted_iota(jnp.int32, (16, T), 0)
        same = row == seg_ref[...]
        qrows = jnp.where(row < 3, jnp.where(same, 0.0, MASKED), 0.0).astype(BF16)
        kt[HEAD_DIM:, :] = jnp.where(row < 3, jnp.where(same, 1.0, 0.0), jnp.where(row < 6, 1.0, 0.0)).astype(BF16)
        for h in range(Q_HEADS):
            qa_ref[h, HEAD_DIM:, :] = qrows
        for g in range(KV_HEADS):
            kt[0:HEAD_DIM, :] = kv_ref[g * HEAD_DIM : (g + 1) * HEAD_DIM, :]
            ka_ref[g] = jnp.transpose(kt[...])
        causal = lax.broadcasted_iota(jnp.int32, (QB, QB), 0) <= lax.broadcasted_iota(jnp.int32, (QB, QB), 1)
        for i in range(T // QB):
            q0, k0 = i * QB, 0 if i == 0 else 128

            @pl.loop(0, Q_HEADS)
            def _(h):
                g = h // (Q_HEADS // KV_HEADS)
                vrow = pl.ds(pl.multiple_of(KVW + g * HEAD_DIM, HEAD_DIM), HEAD_DIM)
                qcol = qa_ref[h, :, q0 : q0 + QB]
                s = jnp.where(causal, dot(ka_ref[g, q0 : q0 + QB, :], qcol), MASKED)
                top = jnp.max(s, axis=0, keepdims=True)
                if i:
                    s2 = dot(ka_ref[g, k0:q0, :], qcol)
                    top = jnp.maximum(top, jnp.max(s2, axis=0, keepdims=True))
                e = jnp.exp(s - top)
                total = jnp.sum(e, axis=0, keepdims=True)
                if i:
                    e2 = jnp.exp(s2 - top)
                    total = total + jnp.sum(e2, axis=0, keepdims=True)
                inv = 1.0 / total
                out = dot(kv_ref[vrow, q0 : q0 + QB], (e * inv).astype(BF16))
                if i:
                    out = out + dot(kv_ref[vrow, k0:q0], (e2 * inv).astype(BF16))
                mix_ref[pl.ds(pl.multiple_of(h * HEAD_DIM, HEAD_DIM), HEAD_DIM), q0 : q0 + QB] = out.astype(BF16)
                lse_ref[h, :, q0 : q0 + QB] = top + jnp.log(total)

            if i == 1:
                gm[1].step(3)
                if G > 2:
                    gm[2].step(2)
            if i == 2 and G > 2:
                gm[2].step(3)
        for gather in gm:
            gather.step(4)

    n = lay.gather_sems
    sd = jax.ShapeDtypeStruct
    V = pltpu.VMEM
    return pl.pallas_call(
        kernel,
        out_shape=[sd(lay.slots + (rows_p, width_of(g)), BF16) for g in groups]
        + [sd((D, E), BF16), sd((D, 8), F32), sd((D, T), BF16),
           sd((Q_HEADS, aug, T), BF16), sd((KV_HEADS, T, aug), BF16), sd((2 * KVW, T), BF16), sd((QW, T), BF16),
           sd((Q_HEADS, 1, T), F32), sd((half, T), F32), sd((half, T), F32)],
        in_specs=[VMEM] * 13, out_specs=[ANY] * G + [VMEM] * 10,
        scratch_shapes=[V((rows_p, width_of(g)), BF16) for g in groups]
        + [V((rows_p, wa), BF16), V(lay.slots + (rows_p, wa), BF16), V((D, wa), F32), V((D, T), F32), V((E, D), BF16), V((aug, T), BF16)]
        + [pltpu.SemaphoreType.DMA((n,))] * (2 + 2 * G),
        compiler_params=params(0), name="gather_attend",
    )(*weights, *gains, xt, segments, positions, frequency)


def middle(lay, part, nf, nq, gms, mix, gain, xt, ct):
    D, T = xt.shape
    FF = nf * lay.pieces
    groups = groups_of(nf, nq)
    G = len(groups)
    wmax = max(width_of(g) for g in groups)
    rows_p = gms[0].shape[-2]
    items = [(k, d) for k in range(G) for d in range(lay.pieces)]

    def kernel(*rest):
        gm_refs, rest = rest[:G], rest[G:]
        (mix_ref, gain_ref, x_ref, c_ref, out_ref, gr_ref, gg_ref, wo_ref), rest = rest[:8], rest[8:]
        parts, rest = rest[:G], rest[G:]
        stages, rest = rest[:G], rest[G:]
        tmp, wg, wu, wd, wgt, wut, wdt, normed, hidden, dgate, dup, sem = rest

        def fetch(n):
            k, d = items[n]
            c, y = d % lay.C, d // lay.C
            return pltpu.make_async_copy(gm_refs[k].at[c, y], stages[k].at[d % 2], sem.at[n])

        fetch(0).start()
        fetch(1).start()
        for n, (k, d) in enumerate(items):
            fetch(n).wait()
            size = width_of(groups[k])
            for f in range(lay.shards):
                tmp[f * part : (f + 1) * part, 0:size] = stages[k][d % 2, f % lay.X, f // lay.X].astype(F32)[:part]
            if n + 2 < len(items):
                fetch(n + 2).start()
            for which, at, w in groups[k]:
                (wg, wu, wd, wo_ref)[which][:, d * w : (d + 1) * w] = tmp[:, at : at + w].astype(BF16)
        wgt[...] = jnp.transpose(wg[...])
        wut[...] = jnp.transpose(wu[...])
        wdt[...] = jnp.transpose(wd[...])
        gain = gain_ref[:, 1:2]
        gg_ref[...] = jnp.zeros_like(gg_ref)

        @pl.loop(0, T // QB)
        def _(i):
            cols = pl.ds(pl.multiple_of(i * QB, QB), QB)
            cot = c_ref[:, cols]
            resid = x_ref[:, cols].astype(F32) + dot(wo_ref[...], mix_ref[:, cols])
            inverse = lax.rsqrt(jnp.mean(resid * resid, axis=0, keepdims=True) + EPS)
            scaled = resid * inverse
            nb = (scaled * gain).astype(BF16)
            normed[:, cols] = nb
            out = resid
            gnm = jnp.zeros_like(resid)
            for j in range(FF // 512):
                rows = slice(j * 512, (j + 1) * 512)
                gate = dot(wgt[rows, :], nb)
                upp = dot(wut[rows, :], nb)
                gh = dot(wdt[rows, :], cot)
                s = jax.nn.sigmoid(gate)
                act = gate * s
                hb = (act * upp).astype(BF16)
                hidden[rows, cols] = hb
                dg = (gh * upp * (s * (1.0 + gate * (1.0 - s)))).astype(BF16)
                du = (gh * act).astype(BF16)
                dgate[rows, cols] = dg
                dup[rows, cols] = du
                out = out + dot(wd[:, rows], hb)
                gnm = gnm + dot(wg[:, rows], dg) + dot(wu[:, rows], du)
            out_ref[:, cols] = out.astype(BF16)
            gg_ref[:, 0:1] += jnp.sum(gnm * scaled, axis=1, keepdims=True)
            m = gnm * gain
            back = inverse * (m - scaled * jnp.mean(m * scaled, axis=0, keepdims=True))
            gr_ref[:, cols] = cot.astype(F32) + back

        for d in range(lay.pieces):
            for k, group in enumerate(groups):
                for which, at, w in group:
                    rows = slice(d * w, (d + 1) * w)
                    if which == 3:
                        value = dot(gr_ref[...].astype(BF16), mix_ref[rows, :], 1, 1)
                    else:
                        value = dot(c_ref[...] if which == 2 else normed[...], (dgate, dup, hidden)[which][rows, :], 1, 1)
                    tmp[:, at : at + w] = value
                size = width_of(group)
                for f in range(lay.shards):
                    parts[k][slot_of(lay, d, f) + (slice(0, part),)] = tmp[f * part : (f + 1) * part, 0:size].astype(BF16)

    sd = jax.ShapeDtypeStruct
    V = pltpu.VMEM
    res = pl.pallas_call(
        kernel,
        out_shape=[sd((D, T), BF16), sd((D, T), F32), sd((D, 8), F32), sd((D, QW), BF16)] + [sd(g.shape, BF16) for g in gms],
        in_specs=[ANY] * G + [VMEM] * 4, out_specs=[VMEM] * (4 + G),
        scratch_shapes=[V((2, lay.X, lay.Z) + g.shape[-2:], BF16) for g in gms]
        + [V((D, wmax), F32)] + [V((D, FF), BF16)] * 3 + [V((FF, D), BF16)] * 3
        + [V((D, T), BF16)] + [V((FF, T), BF16)] * 3 + [pltpu.SemaphoreType.DMA((len(items),))],
        compiler_params=params(), name="mlp",
    )(*gms, mix, gain, xt, ct)
    return res[:4], res[4:]


def split_rows(value, first, base):
    hi = value.astype(BF16).astype(F32)
    mid = (value - hi).astype(BF16).astype(F32)
    low = value - hi - mid
    row = lax.broadcasted_iota(jnp.int32, base.shape, 0)
    return jnp.where(row == first, hi, jnp.where(row == first + 1, mid, jnp.where(row == first + 2, low, base)))


def back(lay, part, nf, nq, nk, pieces, gr, xt, nt, mix, qa, ka, kv, lse, wqkv, wo, gain, ggain, cosine, sine):
    D, T = xt.shape
    E = QW + 2 * KVW
    aug = HEAD_DIM + 16
    half = HEAD_DIM // 2
    groups = groups_of(nf, nq)
    G = len(groups)
    rows_p = pieces[0].shape[-2]
    wa = up(nq + 2 * nk + 2, 128)
    if G > 2:
        plan = ((1, 0, 1), (2, 1, 1), (3, 0, 2), (4, 2, 1), (5, 1, 2), (5, 0, 3), (7, 2, 2), (7, 1, 3), (8, 0, 4))
        tail = ((2, 3), (1, 4))
    else:
        plan = ((1, 0, 1), (2, 1, 1), (4, 0, 2), (5, 1, 2), (6, 0, 3), (8, 0, 4))
        tail = ((1, 3),)

    def kernel(*rest):
        p_refs, rest = rest[:G], rest[G:]
        (gr_ref, x_ref, nt_ref, mix_ref, qa_ref, ka_ref, kv_ref, lse_ref, wqkv_ref, wo_ref, gain_ref, gg_ref, cos_ref, sin_ref), rest = rest[:14], rest[14:]
        (gt_ref, gq_ref, gk_ref, gv_ref, go_ref, gg_out, gu_out, gd_out, gain_out), rest = rest[:9], rest[9:]
        mbufs, rest = [rest[7 * k : 7 * k + 7] for k in range(G)], rest[7 * G :]
        abufs, rest = rest[:6], rest[6:]
        oms, rest = rest[:G], rest[G:]
        (oa, gb, don, doa, qn, qb, va, dk, dv, dq, draw, tmp, dw, pa), sems = rest[:14], rest[14:]
        me = lay.here()
        lay.barrier(me)
        reds = [Reduce(lay, me, p_refs[k], mbufs[k], sems[2 * k], sems[2 * k + 1], False) for k in range(G)]
        for red in reds:
            red.step(0)
        gb[...] = gr_ref[...].astype(BF16)
        wot = jnp.transpose(wo_ref[...])
        tmp[...] = wot
        zero = jnp.zeros((16, T), F32)
        base = qa_ref[0, HEAD_DIM:, :].astype(F32)

        @pl.loop(0, Q_HEADS)
        def _(h):
            rows = pl.ds(pl.multiple_of(h * HEAD_DIM, HEAD_DIM), HEAD_DIM)
            t = dot(tmp[rows, :], gb[...]).astype(BF16)
            doa[h, 0:HEAD_DIM, :] = t
            don[h] = jnp.transpose(t)
            delta = jnp.sum(t.astype(F32) * mix_ref[rows, :].astype(F32), axis=0, keepdims=True)
            doa[h, HEAD_DIM:, :] = split_rows(-delta, 0, zero).astype(BF16)
            q = qa_ref[h, 0:HEAD_DIM, :]
            qn[h] = jnp.transpose(q)
            qb[h, 0:HEAD_DIM, :] = q
            qb[h, HEAD_DIM:, :] = split_rows(-lse_ref[h], 3, base).astype(BF16)

        ones = jnp.where(lax.broadcasted_iota(jnp.int32, (T, 16), 1) < 3, 1.0, 0.0).astype(BF16)
        for g in range(KV_HEADS):
            va[g, :, 0:HEAD_DIM] = jnp.transpose(kv_ref[KVW + g * HEAD_DIM : KVW + (g + 1) * HEAD_DIM, :])
            va[g, :, HEAD_DIM:] = ones
        dk[...] = jnp.zeros_like(dk)
        dv[...] = jnp.zeros_like(dv)
        causal = lax.broadcasted_iota(jnp.int32, (QB, QB), 0) <= lax.broadcasted_iota(jnp.int32, (QB, QB), 1)

        @pl.loop(0, Q_HEADS)
        def _(h):
            g = h // (Q_HEADS // KV_HEADS)
            krow = pl.ds(pl.multiple_of(g * HEAD_DIM, HEAD_DIM), HEAD_DIM)
            for j in range(T // QB):
                k0, k1 = j * QB, (j + 1) * QB
                blocks = [(k0, k1, k0, k1, True)]
                if k1 < T:
                    blocks.append((k0 if j else 128, k1, k1, T, False))
                for a, b, c, d, diagonal in blocks:
                    st = dot(ka_ref[g, a:b, :], qb[h, :, c:d])
                    p = jnp.exp(st)
                    if diagonal:
                        p = jnp.where(causal, p, 0.0)
                    dp = dot(va[g, a:b, :], doa[h, :, c:d])
                    ds = (p * dp).astype(BF16)
                    dv[g, a:b, :] += dot(p.astype(BF16), don[h, c:d, :])
                    dk[g, a:b, :] += dot(ds, qn[h, c:d, :])
                    part_q = dot(kv_ref[krow, a:b], ds)
                    if j == 0:
                        dq[:, c:d] = part_q
                    else:
                        dq[:, c:d] += part_q
            scale = HEAD_DIM ** (-0.5)
            d1, d2 = dq[0:half, :] * scale, dq[half:, :] * scale
            cs, sn = cos_ref[...], sin_ref[...]
            at = pl.multiple_of(h * HEAD_DIM, HEAD_DIM)
            draw[pl.ds(at, half), :] = (d1 * cs + d2 * sn).astype(BF16)
            draw[pl.ds(at + half, half), :] = (d2 * cs - d1 * sn).astype(BF16)
            for when, k, n in plan:

                @pl.when(h == when)
                def _():
                    reds[k].step(n, oms[k])

        cs, sn = cos_ref[...], sin_ref[...]
        for g in range(KV_HEADS):
            t = jnp.transpose(dk[g])
            d1, d2 = t[0:half], t[half:]
            at = QW + g * HEAD_DIM
            draw[at : at + half, :] = (d1 * cs + d2 * sn).astype(BF16)
            draw[at + half : at + HEAD_DIM, :] = (d2 * cs - d1 * sn).astype(BF16)
            at = QW + KVW + g * HEAD_DIM
            draw[at : at + HEAD_DIM, :] = jnp.transpose(dv[g]).astype(BF16)
        for k, n in tail:
            reds[k].step(n, oms[k])
        wide = dot(nt_ref[...], draw[...], 1, 1)
        again = gain_ref[:, 0:1]
        gattn = jnp.sum(wide * wqkv_ref[...].astype(F32), axis=1, keepdims=True) / again
        for d in range(lay.pieces):
            dw[:, 0:nq] = wide[:, d * nq : (d + 1) * nq]
            dw[:, nq : nq + nk] = wide[:, QW + d * nk : QW + (d + 1) * nk]
            dw[:, nq + nk : nq + 2 * nk] = wide[:, QW + KVW + d * nk : QW + KVW + (d + 1) * nk]
            dw[:, nq + 2 * nk : nq + 2 * nk + 1] = gattn
            dw[:, nq + 2 * nk + 1 : nq + 2 * nk + 2] = gg_ref[:, 0:1]
            for f in range(lay.shards):
                pa[slot_of(lay, d, f) + (slice(0, part),)] = dw[f * part : (f + 1) * part, :].astype(BF16)
        ared = Reduce(lay, me, pa, abufs, sems[2 * G], sems[2 * G + 1], True)
        ared.step(0)
        for i in range(4):
            cols = slice(i * (T // 4), (i + 1) * (T // 4))
            v = x_ref[:, cols].astype(F32)
            inverse = lax.rsqrt(jnp.mean(v * v, axis=0, keepdims=True) + EPS)
            scaled = v * inverse
            m = dot(wqkv_ref[...], draw[:, cols]) * again
            gt_ref[:, cols] = gr_ref[:, cols] + inverse * (m - scaled * jnp.mean(m * scaled, axis=0, keepdims=True))
            if i == 0:
                ared.step(1)
                reds[G - 1].step(4, oms[G - 1])
            if i == 1:
                ared.step(2)
            if i == 2:
                ared.step(3)
        for k, group in enumerate(groups):
            for which, at, w in group:
                if which < 3:
                    (gg_out, gu_out, gd_out)[which][...] = oms[k][0:part, at : at + w]
                else:
                    go_ref[...] = jnp.transpose(oms[k][...])[at : at + w, 0:part]
        ared.step(4, oa)
        gq_ref[...] = oa[0:part, 0:nq]
        turned = jnp.transpose(oa[...])
        gk_ref[...] = turned[nq : nq + nk, 0:part]
        gv_ref[...] = turned[nq + nk : nq + 2 * nk, 0:part]
        gain_out[...] = turned[nq + 2 * nk : nq + 2 * nk + 2, 0:part]

    n = lay.reduce_sems
    sd = jax.ShapeDtypeStruct
    V = pltpu.VMEM
    scratch = []
    for g in groups:
        scratch += Reduce.scratch(lay, rows_p, width_of(g), False)
    scratch += Reduce.scratch(lay, rows_p, wa, True)
    return pl.pallas_call(
        kernel,
        out_shape=[sd((D, T), F32), sd((part, nq), F32), sd((nk, part), F32), sd((nk, part), F32), sd((nq, part), F32)]
        + [sd((part, nf), F32)] * 3 + [sd((2, part), F32)],
        in_specs=[ANY] * G + [VMEM] * 14, out_specs=[VMEM] * 9,
        scratch_shapes=scratch + [V((rows_p, width_of(g)), F32) for g in groups]
        + [V((rows_p, wa), F32), V((D, T), BF16), V((Q_HEADS, T, HEAD_DIM), BF16), V((Q_HEADS, aug, T), BF16),
           V((Q_HEADS, T, HEAD_DIM), BF16), V((Q_HEADS, aug, T), BF16), V((KV_HEADS, T, aug), BF16),
           V((KV_HEADS, T, HEAD_DIM), F32), V((KV_HEADS, T, HEAD_DIM), F32), V((HEAD_DIM, T), F32), V((E, T), BF16),
           V((QW, D), BF16), V((D, wa), F32), V(lay.slots + (rows_p, wa), BF16)]
        + [pltpu.SemaphoreType.DMA((n,))] * (2 * G + 2),
        compiler_params=params(1), name="attend_back",
    )(*pieces, gr, xt, nt, mix, qa, ka, kv, lse, wqkv, wo, gain, ggain, cosine, sine)


def on_device(tokens, segments, positions, attn_gain, mlp_gain, w_query, w_key, w_value, w_output, w_gate, w_up, w_down, cotangent):
    lay = Layout(lax.axis_size("dp"), lax.axis_size("fsdp"))
    part = attn_gain.shape[0]
    nq, nk, nf = w_query.shape[1], w_key.shape[1], w_gate.shape[1]
    half = HEAD_DIM // 2
    frequency = ROPE_BASE ** (-(2.0 * np.arange(half, dtype=np.float64)) / HEAD_DIM)
    frequency = jnp.asarray(frequency.astype(np.float32)[:, None])
    xt, ct = tokens.T, cotangent.T
    weights = (w_query, w_key.T, w_value.T, w_output, w_gate, w_up, w_down.T)
    gains = (attn_gain[None], mlp_gain[None])
    res = front(lay, weights, gains, xt, segments, positions, frequency)
    gms, (wqkv, gain, nt, qa, ka, kv, mix, lse, cosine, sine) = res[:-10], res[-10:]
    (out, gr, ggain, wo), pieces = middle(lay, part, nf, nq, gms, mix, gain, xt, ct)
    gt, gq, gk, gv, go, gg, gu, gd, gains = back(
        lay, part, nf, nq, nk, pieces, gr, xt, nt, mix, qa, ka, kv, lse, wqkv, wo, gain, ggain, cosine, sine)
    return (out.T, gt.T, gains[0], gains[1], gq, gk.T, gv.T, go, gg, gu, gd.T)


def solution(mesh):
    in_specs = (
        P(("dp", "fsdp"), None),
        P(("dp", "fsdp"), None),
        P(("dp", "fsdp"), None),
        P("fsdp"),
        P("fsdp"),
        P("fsdp", "dp"),
        P("fsdp", "dp"),
        P("fsdp", "dp"),
        P("dp", "fsdp"),
        P("fsdp", "dp"),
        P("fsdp", "dp"),
        P("dp", "fsdp"),
        P(("dp", "fsdp"), None),
    )
    out_specs = (
        P(("dp", "fsdp"), None),
        P(("dp", "fsdp"), None),
        P("fsdp"),
        P("fsdp"),
        P("fsdp", "dp"),
        P("fsdp", "dp"),
        P("fsdp", "dp"),
        P("dp", "fsdp"),
        P("fsdp", "dp"),
        P("fsdp", "dp"),
        P("dp", "fsdp"),
    )
    return jax.shard_map(
        on_device, mesh=mesh, in_specs=in_specs, out_specs=out_specs, check_vma=False
    )
```

```python
import numpy as np

import jax
import jax.numpy as jnp
from jax import lax
from jax.experimental import pallas as pl
from jax.experimental.pallas import tpu as pltpu
from jax.sharding import PartitionSpec as P


Q_HEADS = 9
KV_HEADS = 3
HEAD_DIM = 64
QW = 576
KVW = 192
EPS = 1e-05
ROPE_BASE = 100000.0
MASKED = -1e30
BF16 = jnp.bfloat16
F32 = jnp.float32
MESH = pl.DeviceIdType.MESH
ANY = pl.BlockSpec(memory_space=pl.ANY)
VMEM = pl.BlockSpec(memory_space=pltpu.VMEM)


def up(value, step):
    return -(-value // step) * step


class Layout:
    def __init__(self, pieces, shards):
        self.pieces, self.shards = pieces, shards
        self.C = 2 if pieces % 2 == 0 else 1
        self.Y = pieces // self.C
        self.X = 2 if shards <= 8 else 4
        self.Z = shards // self.X
        self.H = self.Z // 2
        self.slots = (self.C, self.Y, self.X, self.Z)
        n = (self.X - 1) + (self.Y - 1)
        self.gather_sems = 1 + (self.Z - 1) + 2 * n + 1 + 2 * n
        self.reduce_sems = 2 + 2 * n + (self.Z - 1)
        self.peers = (self.X - 1) + (self.Y - 1) + (self.Z - 1) + (self.C - 1)

    def here(self):
        dp, fs = lax.axis_index("dp"), lax.axis_index("fsdp")
        return lax.rem(dp, self.C), dp // self.C, lax.rem(fs, self.X), fs // self.X

    def device(self, c, y, x, z):
        return (y * self.C + c, z * self.X + x)

    def others(self, me, axis):
        size = self.slots[axis]
        for k in range(1, size):
            place = list(me)
            place[axis] = lax.rem(me[axis] + k, size)
            yield k, place

    def barrier(self, me):
        sem = pltpu.get_barrier_semaphore()
        for axis in range(4):
            for _, place in self.others(me, axis):
                pl.semaphore_signal(sem, inc=1, device_id=self.device(*place), device_id_type=MESH)
        pl.semaphore_wait(sem, self.peers)


class Sender:
    def __init__(self, layout, me, send, recv):
        self.lay, self.me, self.send, self.recv, self.used = layout, me, send, recv, 0

    def to(self, place, src, dst):
        k = self.used
        self.used += 1
        return pltpu.make_async_remote_copy(
            src_ref=src, dst_ref=dst, send_sem=self.send.at[k], recv_sem=self.recv.at[k],
            device_id=self.lay.device(*place), device_id_type=MESH)


def start(copies):
    for copy in copies:
        copy.start()


def wait(copies):
    for copy in copies:
        copy.wait()


class Gather:
    def __init__(self, lay, me, src, slots, send, recv):
        c, y, x, z = me
        s = Sender(lay, me, send, recv)
        X, Y, H, R = lay.X, lay.Y, lay.H, lay.Z - lay.H
        lo, hi = pl.ds(0, H), pl.ds(H, R)
        ax, ay = pl.ds(0, X), pl.ds(0, Y)
        sib = (1 - c, y, x, z)
        self.own = pltpu.make_async_copy(src, slots.at[c, y, x, z], recv.at[s.used])
        s.used += 1
        self.z = [s.to(p, src, slots.at[c, y, x, z]) for _, p in lay.others(me, 3)]
        part = slots.at[c, y, x, lo]
        self.xy1 = [s.to(p, part, part) for _, p in lay.others(me, 2)]
        part2 = slots.at[c, y, x, hi]
        self.xy1 += [s.to(p, part2, part2) for _, p in lay.others(me, 1)]
        part3 = slots.at[c, y, ax, lo]
        self.xy2 = [s.to(p, part3, part3) for _, p in lay.others(me, 1)]
        part4 = slots.at[c, ay, x, hi]
        self.xy2 += [s.to(p, part4, part4) for _, p in lay.others(me, 2)]
        self.core = [[], [], []]
        if lay.C > 1:
            whole = slots.at[c, y, x]
            self.core[0] = [s.to(sib, whole, whole)]
            for _, p in lay.others(me, 2):
                piece = slots.at[c, y, p[2], lo]
                self.core[1].append(s.to(sib, piece, piece))
            for _, p in lay.others(me, 1):
                piece = slots.at[c, p[1], x, hi]
                self.core[1].append(s.to(sib, piece, piece))
            for _, p in lay.others(me, 1):
                piece = slots.at[c, p[1], ax, lo]
                self.core[2].append(s.to(sib, piece, piece))
            for _, p in lay.others(me, 2):
                piece = slots.at[c, ay, p[2], hi]
                self.core[2].append(s.to(sib, piece, piece))

    def step(self, n):
        if n == 0:
            self.own.start()
            start(self.z)
        elif n == 1:
            self.own.wait()
            wait(self.z)
            start(self.xy1)
            start(self.core[0])
        elif n == 2:
            wait(self.xy1)
            start(self.xy2)
            start(self.core[1])
        elif n == 3:
            wait(self.xy2)
            start(self.core[2])
        else:
            for copies in self.core:
                wait(copies)


class Reduce:
    def __init__(self, lay, me, parts, bufs, send, recv, inplace):
        c, y, x, z = me
        self.lay, self.me = lay, me
        self.far, self.r2a, self.r2b, self.r3a, self.r3b, self.r4 = bufs[:6]
        self.out = parts.at[c] if inplace else bufs[6]
        s = Sender(lay, me, send, recv)
        X, Y, H, R = lay.X, lay.Y, lay.H, lay.Z - lay.H
        lo, hi = pl.ds(0, H), pl.ds(H, R)
        ax, ay = pl.ds(0, X), pl.ds(0, Y)
        out = self.out
        self.own = None if inplace else pltpu.make_async_copy(parts.at[c], self.out, recv.at[s.used])
        s.used += 1
        self.core = [s.to((1 - c, y, x, z), parts.at[1 - c], self.far)] if lay.C > 1 else []
        self.xy1 = [s.to(p, out.at[p[1], ax, lo], self.r2a.at[k - 1]) for k, p in lay.others(me, 1)]
        self.xy1 += [s.to(p, out.at[ay, p[2], hi], self.r2b.at[k - 1]) for k, p in lay.others(me, 2)]
        self.xy2 = [s.to(p, out.at[y, p[2], lo], self.r3a.at[k - 1]) for k, p in lay.others(me, 2)]
        self.xy2 += [s.to(p, out.at[p[1], x, hi], self.r3b.at[k - 1]) for k, p in lay.others(me, 1)]
        self.zs = [s.to(p, out.at[y, x, p[3]], self.r4.at[k - 1]) for k, p in lay.others(me, 3)]

    @staticmethod
    def scratch(lay, rows, width, inplace):
        X, Y, Z, H = lay.X, lay.Y, lay.Z, lay.H
        R = Z - H
        tail = (rows, width)
        return [
            pltpu.VMEM((Y, X, Z) + tail, BF16),
            pltpu.VMEM((Y - 1, X, H) + tail, BF16), pltpu.VMEM((X - 1, Y, R) + tail, BF16),
            pltpu.VMEM((X - 1, H) + tail, BF16), pltpu.VMEM((Y - 1, R) + tail, BF16),
            pltpu.VMEM((Z - 1,) + tail, BF16),
        ] + ([] if inplace else [pltpu.VMEM((Y, X, Z) + tail, BF16)])

    def step(self, n, result=None):
        lay, (c, y, x, z) = self.lay, self.me
        X, Y, Z, H = lay.X, lay.Y, lay.Z, lay.H
        out = self.out
        if n == 0:
            if self.own is not None:
                self.own.start()
            start(self.core)
        elif n == 1:
            if self.own is not None:
                self.own.wait()
            wait(self.core)

            @pl.loop(0, Y * X * Z)
            def _(i):
                yy, xx, zz = i // (X * Z), lax.rem(i // Z, X), lax.rem(i, Z)
                v = out[yy, xx, zz].astype(F32)
                if lay.C > 1:
                    v = v + self.far[yy, xx, zz].astype(F32)
                out[yy, xx, zz] = v.astype(BF16)

            start(self.xy1)
        elif n == 2:
            wait(self.xy1)

            @pl.loop(0, X * H)
            def _(i):
                xx, zz = i // H, lax.rem(i, H)
                v = out[y, xx, zz].astype(F32)
                for k in range(Y - 1):
                    v = v + self.r2a[k, xx, zz].astype(F32)
                out[y, xx, zz] = v.astype(BF16)

            @pl.loop(0, Y * (Z - H))
            def _(i):
                yy, zz = i // (Z - H), lax.rem(i, Z - H)
                v = out[yy, x, H + zz].astype(F32)
                for k in range(X - 1):
                    v = v + self.r2b[k, yy, zz].astype(F32)
                out[yy, x, H + zz] = v.astype(BF16)

            start(self.xy2)
        elif n == 3:
            wait(self.xy2)

            @pl.loop(0, H)
            def _(i):
                v = out[y, x, i].astype(F32)
                for k in range(X - 1):
                    v = v + self.r3a[k, i].astype(F32)
                out[y, x, i] = v.astype(BF16)

            @pl.loop(0, Z - H)
            def _(i):
                v = out[y, x, H + i].astype(F32)
                for k in range(Y - 1):
                    v = v + self.r3b[k, i].astype(F32)
                out[y, x, H + i] = v.astype(BF16)

            start(self.zs)
        else:
            wait(self.zs)
            v = out[y, x, z].astype(F32)
            for k in range(Z - 1):
                v = v + self.r4[k].astype(F32)
            result[...] = v


QB = 256


def dot(a, b, ca=1, cb=0):
    return lax.dot_general(a, b, (((ca,), (cb,)), ((), ())), preferred_element_type=F32)


def slot_of(lay, d, f):
    return (d % lay.C, d // lay.C, f % lay.X, f // lay.X)


def groups_of(nf):
    if nf % 128 == 0:
        return (((0, 0, nf),), ((1, 0, nf),), ((2, 0, nf),))
    return (((0, 0, nf), (1, nf, nf)), ((2, 0, nf),))


def out_places(part, nq, groups, wa):
    places = []
    for k, width in enumerate([width_of(g) for g in groups] + [wa]):
        places += [(k, j * part) for j in range(width // part)]
    return places[: nq // 8]


def width_of(group):
    return up(group[-1][1] + group[-1][2], 128)


def params(which=None):
    extra = {} if which is None else dict(collective_id=which, has_side_effects=True)
    return pltpu.CompilerParams(vmem_limit_bytes=62 * 2**20, **extra)


def eye(n):
    return (lax.broadcasted_iota(jnp.int32, (n, n), 0) == lax.broadcasted_iota(jnp.int32, (n, n), 1)).astype(F32).astype(BF16)


def split_rows(value, first, base):
    hi = value.astype(BF16).astype(F32)
    mid = (value - hi).astype(BF16).astype(F32)
    low = value - hi - mid
    row = lax.broadcasted_iota(jnp.int32, base.shape, 0)
    return jnp.where(row == first, hi, jnp.where(row == first + 1, mid, jnp.where(row == first + 2, low, base)))


def column(one, ref):
    wide = jnp.broadcast_to(ref[...].astype(F32), (16, ref.shape[1])).astype(BF16)
    return dot(one, wide, 1, 1)[:, 0:1].astype(BF16)


def front(lay, weights, gains, xt, segments, positions, frequency):
    wq, wkt, wvt, wo, wg, wu, wdt = weights
    part, nq = wq.shape
    nk, nf = wkt.shape[0], wg.shape[1]
    rows_p = up(part + 8, 16)
    wa = up(nq + 2 * nk + 2, 128)
    D, T = xt.shape
    E = QW + 2 * KVW
    half = HEAD_DIM // 2
    groups = groups_of(nf)
    G = len(groups)
    places = out_places(part, nq, groups, wa)
    last = slice(rows_p - 8, rows_p)
    aug = HEAD_DIM + 16

    def kernel(wq_ref, wkt_ref, wvt_ref, wo_in, wg_ref, wu_ref, wdt_ref, ag_ref, mg_ref, x_ref, seg_ref, pos_ref, fr_ref, *rest):
        gms, rest = rest[:G], rest[G:]
        (wqkv_ref, gain_ref, nt_ref, qa_ref, ka_ref, kv_ref, mix_ref, cos_ref, sin_ref, oex_ref), rest = rest[:10], rest[10:]
        pms, rest = rest[:G], rest[G:]
        (pa, ga_ref, tmp, scaled, wt, kt, lse_ref), sems = rest[:7], rest[7:]
        one = eye(part)
        pa[0:part, 0:nq] = wq_ref[...]
        pa[0:part, nq : nq + nk] = dot(one, wkt_ref[...], 1, 1).astype(BF16)
        pa[0:part, nq + nk : nq + 2 * nk] = dot(one, wvt_ref[...], 1, 1).astype(BF16)
        pa[0:part, nq + 2 * nk : nq + 2 * nk + 1] = column(one, ag_ref)
        pa[0:part, nq + 2 * nk + 1 : nq + 2 * nk + 2] = column(one, mg_ref)
        for b, (k, lane) in enumerate(places):
            (list(pms) + [pa])[k][last, lane : lane + part] = wo_in[8 * b : 8 * b + 8, :]
        me = lay.here()
        lay.barrier(me)
        ga = Gather(lay, me, pa, ga_ref, sems[0], sems[1])
        gm = [Gather(lay, me, pms[k], gms[k], sems[2 + 2 * k], sems[3 + 2 * k]) for k in range(G)]
        ga.step(0)
        for k, group in enumerate(groups):
            for which, at, size in group:
                pms[k][0:part, at : at + size] = (wg_ref, wu_ref, wdt_ref)[which][...]
        v = x_ref[...].astype(F32)
        scaled[...] = v * lax.rsqrt(jnp.mean(v * v, axis=0, keepdims=True) + EPS)
        angles = fr_ref[...] * pos_ref[...].astype(F32)
        cos_ref[...] = jnp.cos(angles)
        sin_ref[...] = jnp.sin(angles)
        ga.step(1)
        gm[0].step(0)
        ga.step(2)
        ga.step(3)
        gm[0].step(1)
        gm[1].step(0)
        ga.step(4)
        for d in range(lay.pieces):
            for f in range(lay.shards):
                tmp[f * part : (f + 1) * part, :] = ga_ref[slot_of(lay, d, f)].astype(F32)[:part]
                oex_ref[d * lay.shards + f] = ga_ref[slot_of(lay, d, f) + (last,)]
            wqkv_ref[:, d * nq : (d + 1) * nq] = tmp[:, 0:nq].astype(BF16)
            wqkv_ref[:, QW + d * nk : QW + (d + 1) * nk] = tmp[:, nq : nq + nk].astype(BF16)
            wqkv_ref[:, QW + KVW + d * nk : QW + KVW + (d + 1) * nk] = tmp[:, nq + nk : nq + 2 * nk].astype(BF16)
        gain_ref[:, 0:2] = tmp[:, nq + 2 * nk : nq + 2 * nk + 2]
        gm[0].step(2)
        gm[1].step(1)
        if G > 2:
            gm[2].step(0)
        wt[...] = jnp.transpose(wqkv_ref[...])
        nt_ref[...] = (scaled[...] * gain_ref[:, 0:1]).astype(BF16)

        @pl.loop(0, T // QB)
        def _(i):
            cols = pl.ds(pl.multiple_of(i * QB, QB), QB)
            raw = dot(wt[...], nt_ref[:, cols])
            cs, sn = cos_ref[:, cols], sin_ref[:, cols]
            for h in range(Q_HEADS + KV_HEADS):
                u1, u2 = raw[h * HEAD_DIM : h * HEAD_DIM + half], raw[h * HEAD_DIM + half : (h + 1) * HEAD_DIM]
                o1 = (u1 * cs - u2 * sn).astype(BF16)
                o2 = (u2 * cs + u1 * sn).astype(BF16)
                if h < Q_HEADS:
                    scale = HEAD_DIM ** (-0.5)
                    qa_ref[h, 0:half, cols] = o1 * scale
                    qa_ref[h, half:HEAD_DIM, cols] = o2 * scale
                else:
                    g = (h - Q_HEADS) * HEAD_DIM
                    kv_ref[g : g + half, cols] = o1
                    kv_ref[g + half : g + HEAD_DIM, cols] = o2
            kv_ref[KVW:, cols] = raw[QW + KVW :].astype(BF16)

        gm[0].step(3)
        gm[1].step(2)
        if G > 2:
            gm[2].step(1)
        row = lax.broadcasted_iota(jnp.int32, (16, T), 0)
        same = row == seg_ref[...]
        qrows = jnp.where(row < 3, jnp.where(same, 0.0, MASKED), 0.0).astype(BF16)
        kt[HEAD_DIM:, :] = jnp.where(row < 3, jnp.where(same, 1.0, 0.0), jnp.where(row < 6, 1.0, 0.0)).astype(BF16)
        for h in range(Q_HEADS):
            qa_ref[h, HEAD_DIM:, :] = qrows
        for g in range(KV_HEADS):
            kt[0:HEAD_DIM, :] = kv_ref[g * HEAD_DIM : (g + 1) * HEAD_DIM, :]
            ka_ref[g] = jnp.transpose(kt[...])
        causal = lax.broadcasted_iota(jnp.int32, (QB, QB), 0) <= lax.broadcasted_iota(jnp.int32, (QB, QB), 1)
        for i in range(T // QB):
            q0, k0 = i * QB, 0 if i == 0 else 128

            @pl.loop(0, Q_HEADS)
            def _(h):
                g = h // (Q_HEADS // KV_HEADS)
                vrow = pl.ds(pl.multiple_of(KVW + g * HEAD_DIM, HEAD_DIM), HEAD_DIM)
                qcol = qa_ref[h, :, q0 : q0 + QB]
                s = jnp.where(causal, dot(ka_ref[g, q0 : q0 + QB, :], qcol), MASKED)
                top = jnp.max(s, axis=0, keepdims=True)
                if i:
                    s2 = dot(ka_ref[g, k0:q0, :], qcol)
                    top = jnp.maximum(top, jnp.max(s2, axis=0, keepdims=True))
                e = jnp.exp(s - top)
                total = jnp.sum(e, axis=0, keepdims=True)
                if i:
                    e2 = jnp.exp(s2 - top)
                    total = total + jnp.sum(e2, axis=0, keepdims=True)
                inv = 1.0 / total
                out = dot(kv_ref[vrow, q0 : q0 + QB], (e * inv).astype(BF16))
                if i:
                    out = out + dot(kv_ref[vrow, k0:q0], (e2 * inv).astype(BF16))
                mix_ref[pl.ds(pl.multiple_of(h * HEAD_DIM, HEAD_DIM), HEAD_DIM), q0 : q0 + QB] = out.astype(BF16)
                lse_ref[h, :, q0 : q0 + QB] = top + jnp.log(total)

            if i == 1:
                gm[1].step(3)
                if G > 2:
                    gm[2].step(2)
            if i == 2 and G > 2:
                gm[2].step(3)
        base = qrows.astype(F32)
        for h in range(Q_HEADS):
            qa_ref[h, HEAD_DIM:, :] = split_rows(-lse_ref[h], 3, base).astype(BF16)
        for gather in gm:
            gather.step(4)

    n = lay.gather_sems
    sd = jax.ShapeDtypeStruct
    V = pltpu.VMEM
    return pl.pallas_call(
        kernel,
        out_shape=[sd(lay.slots + (rows_p, width_of(g)), BF16) for g in groups]
        + [sd((D, E), BF16), sd((D, 8), F32), sd((D, T), BF16),
           sd((Q_HEADS, aug, T), BF16), sd((KV_HEADS, T, aug), BF16), sd((2 * KVW, T), BF16), sd((QW, T), BF16),
           sd((half, T), F32), sd((half, T), F32), sd((lay.pieces * lay.shards, 8, wa), BF16)],
        in_specs=[VMEM] * 13, out_specs=[ANY] * G + [VMEM] * 10,
        scratch_shapes=[V((rows_p, width_of(g)), BF16) for g in groups]
        + [V((rows_p, wa), BF16), V(lay.slots + (rows_p, wa), BF16), V((D, wa), F32), V((D, T), F32), V((E, D), BF16), V((aug, T), BF16), V((Q_HEADS, 1, T), F32)]
        + [pltpu.SemaphoreType.DMA((n,))] * (2 + 2 * G),
        compiler_params=params(0), name="gather_attend",
    )(*weights, *gains, xt, segments, positions, frequency)


def middle(lay, part, nf, nq, gms, oex, mix, gain, xt, ct):
    D, T = xt.shape
    FF = nf * lay.pieces
    groups = groups_of(nf)
    G = len(groups)
    places = out_places(part, nq, groups, oex.shape[-1])
    wmax = max(width_of(g) for g in groups)
    rows_p = gms[0].shape[-2]
    items = [(k, d) for k in range(G) for d in range(lay.pieces)]

    def kernel(*rest):
        gm_refs, rest = rest[:G], rest[G:]
        oex_ref, rest = rest[0], rest[1:]
        (mix_ref, gain_ref, x_ref, c_ref, out_ref, gr_ref, gg_ref, wo_ref, normed, h_out, g_out, u_out), rest = rest[:12], rest[12:]
        stages, rest = rest[:G], rest[G:]
        tmp, wg, wu, wd, wgt, wut, wdt, wot, hidden, dgate, dup, sem, out_sem = rest

        def fetch(n):
            k, d = items[n]
            c, y = d % lay.C, d // lay.C
            return pltpu.make_async_copy(gm_refs[k].at[c, y], stages[k].at[d % 2], sem.at[n])

        def put(k, d, f, rows):
            for b, (pack, lane) in enumerate(places):
                if pack == k:
                    at = d * nq + 8 * b
                    gr_ref[at : at + 8, f * part : (f + 1) * part] = rows[:, lane : lane + part]

        fetch(0).start()
        fetch(1).start()
        for n, (k, d) in enumerate(items):
            fetch(n).wait()
            size = width_of(groups[k])
            for f in range(lay.shards):
                piece = stages[k][d % 2, f % lay.X, f // lay.X].astype(F32)
                tmp[f * part : (f + 1) * part, 0:size] = piece[:part]
                put(k, d, f, piece[rows_p - 8 :])
            if n + 2 < len(items):
                fetch(n + 2).start()
            for which, at, w in groups[k]:
                (wg, wu, wd)[which][:, d * w : (d + 1) * w] = tmp[:, at : at + w].astype(BF16)
        for d in range(lay.pieces):
            for f in range(lay.shards):
                put(G, d, f, oex_ref[d * lay.shards + f].astype(F32))
        wo_ref[...] = gr_ref[:, 0:D].astype(BF16)
        wot[...] = jnp.transpose(wo_ref[...])
        wgt[...] = jnp.transpose(wg[...])
        wut[...] = jnp.transpose(wu[...])
        wdt[...] = jnp.transpose(wd[...])
        gain = gain_ref[:, 1:2]

        def send(i, cols):
            pairs = ((hidden, h_out), (dgate, g_out), (dup, u_out))
            return [pltpu.make_async_copy(a.at[:, cols], b.at[:, cols], out_sem.at[i, k]) for k, (a, b) in enumerate(pairs)]

        gg_ref[...] = jnp.zeros_like(gg_ref)

        @pl.loop(0, T // QB)
        def _(i):
            cols = pl.ds(pl.multiple_of(i * QB, QB), QB)
            cot = c_ref[:, cols]
            resid = x_ref[:, cols].astype(F32) + dot(wot[...], mix_ref[:, cols])
            inverse = lax.rsqrt(jnp.mean(resid * resid, axis=0, keepdims=True) + EPS)
            scaled = resid * inverse
            nb = (scaled * gain).astype(BF16)
            normed[:, cols] = nb
            out = resid
            gnm = jnp.zeros_like(resid)
            for j in range(2):
                rows = slice(j * (FF // 2), (j + 1) * (FF // 2))
                gate = dot(wgt[rows, :], nb)
                upp = dot(wut[rows, :], nb)
                gh = dot(wdt[rows, :], cot)
                s = jax.nn.sigmoid(gate)
                act = gate * s
                hb = (act * upp).astype(BF16)
                hidden[rows, cols] = hb
                dg = (gh * upp * (s * (1.0 + gate * (1.0 - s)))).astype(BF16)
                du = (gh * act).astype(BF16)
                dgate[rows, cols] = dg
                dup[rows, cols] = du
                out = out + dot(wd[:, rows], hb)
                gnm = gnm + dot(wg[:, rows], dg) + dot(wu[:, rows], du)
            out_ref[:, cols] = out.astype(BF16)
            gg_ref[:, 0:1] += jnp.sum(gnm * scaled, axis=1, keepdims=True)
            m = gnm * gain
            back = inverse * (m - scaled * jnp.mean(m * scaled, axis=0, keepdims=True))
            gr_ref[:, cols] = cot.astype(F32) + back
            for copy in send(i, cols):
                copy.start()

        for i in range(T // QB):
            for copy in send(i, slice(i * QB, (i + 1) * QB)):
                copy.wait()

    sd = jax.ShapeDtypeStruct
    V = pltpu.VMEM
    res = pl.pallas_call(
        kernel,
        out_shape=[sd((D, T), BF16), sd((D, T), F32), sd((D, 8), F32), sd((QW, D), BF16), sd((D, T), BF16)] + [sd((FF, T), BF16)] * 3,
        in_specs=[ANY] * G + [VMEM] * 5, out_specs=[VMEM] * 5 + [ANY] * 3,
        scratch_shapes=[V((2, lay.X, lay.Z) + g.shape[-2:], BF16) for g in gms]
        + [V((D, wmax), F32)] + [V((D, FF), BF16)] * 3 + [V((FF, D), BF16)] * 3 + [V((D, QW), BF16)]
        + [V((FF, T), BF16)] * 3 + [pltpu.SemaphoreType.DMA((len(items),)), pltpu.SemaphoreType.DMA((T // QB, 3))],
        compiler_params=params(), name="mlp",
    )(*gms, oex, mix, gain, xt, ct)
    return res


def back(lay, part, nf, nq, nk, acts, gr, ct, nm, xt, nt, mix, qa, ka, kv, wqkv, wo, gain, ggain, cosine, sine):
    D, T = xt.shape
    E = QW + 2 * KVW
    aug = HEAD_DIM + 16
    half = HEAD_DIM // 2
    groups = groups_of(nf)
    G = len(groups)
    rows_p = up(part + 8, 16)
    wa = up(nq + 2 * nk + 2, 128)
    places = out_places(part, nq, groups, wa)
    last = slice(rows_p - 8, rows_p)
    FF = nf * lay.pieces
    if G > 2:
        early = ((), ((0, 1),), ((1, 1),))
        ready = ((0, 2),)
        plan = ((1, 2, 1), (2, 1, 2), (2, 0, 3), (4, 1, 3), (5, 2, 2), (6, 0, 4), (7, 1, 4), (8, 2, 3))
    else:
        early = ((), ((0, 1),))
        ready = ()
        plan = ((0, 1, 1), (1, 0, 2), (3, 0, 3), (4, 1, 2), (6, 0, 4), (7, 1, 3))
    nbuf = 2 if G > 2 else 1

    def kernel(*rest):
        a_refs, gr_in, rest = rest[:3], rest[3], rest[4:]
        (ct_ref, nm_ref, x_ref, nt_ref, mix_ref, qa_ref, ka_ref, kv_ref, wqkv_ref, wo_ref, gain_ref, gg_ref, cos_ref, sin_ref), rest = rest[:14], rest[14:]
        gt_ref, oa, rest = rest[0], rest[1], rest[2:]
        oms, rest = rest[:G], rest[G:]
        mbufs, rest = [rest[6 * k : 6 * k + 6] for k in range(G)], rest[6 * G :]
        abufs, rest = rest[:6], rest[6:]
        p_refs, rest = rest[:G], rest[G:]
        (big, gb, don, doa, qn, va, dk, dv, dq, draw, dw, wide, line, pa, big_sem), sems = rest[:15], rest[15:]
        me = lay.here()
        lay.barrier(me)
        reds = [Reduce(lay, me, p_refs[k], mbufs[k], sems[2 * k], sems[2 * k + 1], True) for k in range(G)]

        def fetch(which):
            return pltpu.make_async_copy(a_refs[which], big.at[which % nbuf], big_sem.at[which])

        load = pltpu.make_async_copy(gr_in, gt_ref, big_sem.at[3])
        for which in range(nbuf):
            fetch(which).start()
        load.start()
        load.wait()
        gb[...] = gt_ref[...].astype(BF16)
        wide[:, 0:D] = dot(mix_ref[...], gb[...], 1, 1)
        packs = list(p_refs) + [pa]
        for d in range(lay.pieces):
            for f in range(lay.shards):
                for k in sorted({pack for pack, _ in places}):
                    for b, (pack, lane) in enumerate(places):
                        if pack == k:
                            at = d * nq + 8 * b
                            line[k, :, lane : lane + part] = wide[at : at + 8, f * part : (f + 1) * part]
                    width = packs[k].shape[-1]
                    packs[k][slot_of(lay, d, f) + (last,)] = line[k, :, 0:width].astype(BF16)
        for k, group in enumerate(groups):
            for which, at, w in group:
                fetch(which).wait()
                for d in range(lay.pieces):
                    rows = slice(d * w, (d + 1) * w)
                    value = dot(ct_ref[...] if which == 2 else nm_ref[...], big[which % nbuf, rows, :], 1, 1)
                    wide[:, 0:w] = value
                    for f in range(lay.shards):
                        p_refs[k][slot_of(lay, d, f) + (slice(0, part), slice(at, at + w))] = wide[f * part : (f + 1) * part, 0:w].astype(BF16)
                if which + nbuf < 3:
                    fetch(which + nbuf).start()
            reds[k].step(0)
            for kk, n in early[k]:
                reds[kk].step(n)
        zero = jnp.zeros((16, T), F32)

        @pl.loop(0, Q_HEADS)
        def _(h):
            rows = pl.ds(pl.multiple_of(h * HEAD_DIM, HEAD_DIM), HEAD_DIM)
            t = dot(wo_ref[rows, :], gb[...]).astype(BF16)
            doa[h, 0:HEAD_DIM, :] = t
            don[h] = jnp.transpose(t)
            delta = jnp.sum(t.astype(F32) * mix_ref[rows, :].astype(F32), axis=0, keepdims=True)
            doa[h, HEAD_DIM:, :] = split_rows(-delta, 0, zero).astype(BF16)
            qn[h] = jnp.transpose(qa_ref[h, 0:HEAD_DIM, :])

        for k, n in ready:
            reds[k].step(n)
        ones = jnp.where(lax.broadcasted_iota(jnp.int32, (T, 16), 1) < 3, 1.0, 0.0).astype(BF16)
        for g in range(KV_HEADS):
            va[g, :, 0:HEAD_DIM] = jnp.transpose(kv_ref[KVW + g * HEAD_DIM : KVW + (g + 1) * HEAD_DIM, :])
            va[g, :, HEAD_DIM:] = ones
        dk[...] = jnp.zeros_like(dk)
        dv[...] = jnp.zeros_like(dv)
        causal = lax.broadcasted_iota(jnp.int32, (QB, QB), 0) <= lax.broadcasted_iota(jnp.int32, (QB, QB), 1)

        @pl.loop(0, Q_HEADS)
        def _(h):
            g = h // (Q_HEADS // KV_HEADS)
            krow = pl.ds(pl.multiple_of(g * HEAD_DIM, HEAD_DIM), HEAD_DIM)
            for j in range(T // QB):
                k0, k1 = j * QB, (j + 1) * QB
                blocks = [(k0, k1, k0, k1, True)]
                if k1 < T:
                    blocks.append((k0 if j else 128, k1, k1, T, False))
                for a, b, c, d, diagonal in blocks:
                    st = dot(ka_ref[g, a:b, :], qa_ref[h, :, c:d])
                    p = jnp.exp(st)
                    if diagonal:
                        p = jnp.where(causal, p, 0.0)
                    dp = dot(va[g, a:b, :], doa[h, :, c:d])
                    ds = (p * dp).astype(BF16)
                    dv[g, a:b, :] += dot(p.astype(BF16), don[h, c:d, :])
                    dk[g, a:b, :] += dot(ds, qn[h, c:d, :])
                    part_q = dot(kv_ref[krow, a:b], ds)
                    if j == 0:
                        dq[:, c:d] = part_q
                    else:
                        dq[:, c:d] += part_q
            scale = HEAD_DIM ** (-0.5)
            d1, d2 = dq[0:half, :] * scale, dq[half:, :] * scale
            cs, sn = cos_ref[...], sin_ref[...]
            at = pl.multiple_of(h * HEAD_DIM, HEAD_DIM)
            draw[pl.ds(at, half), :] = (d1 * cs + d2 * sn).astype(BF16)
            draw[pl.ds(at + half, half), :] = (d2 * cs - d1 * sn).astype(BF16)
            for when, k, n in plan:

                @pl.when(h == when)
                def _():
                    reds[k].step(n, oms[k])

        cs, sn = cos_ref[...], sin_ref[...]
        for g in range(KV_HEADS):
            t = jnp.transpose(dk[g])
            d1, d2 = t[0:half], t[half:]
            at = QW + g * HEAD_DIM
            draw[at : at + half, :] = (d1 * cs + d2 * sn).astype(BF16)
            draw[at + half : at + HEAD_DIM, :] = (d2 * cs - d1 * sn).astype(BF16)
            at = QW + KVW + g * HEAD_DIM
            draw[at : at + HEAD_DIM, :] = jnp.transpose(dv[g]).astype(BF16)
        wide[:, 0:E] = dot(nt_ref[...], draw[...], 1, 1)
        again = gain_ref[:, 0:1]
        gattn = jnp.sum(wide[:, 0:E] * wqkv_ref[...].astype(F32), axis=1, keepdims=True) / again
        for d in range(lay.pieces):
            dw[:, 0:nq] = wide[:, d * nq : (d + 1) * nq]
            dw[:, nq : nq + nk] = wide[:, QW + d * nk : QW + (d + 1) * nk]
            dw[:, nq + nk : nq + 2 * nk] = wide[:, QW + KVW + d * nk : QW + KVW + (d + 1) * nk]
            dw[:, nq + 2 * nk : nq + 2 * nk + 1] = gattn
            dw[:, nq + 2 * nk + 1 : nq + 2 * nk + 2] = gg_ref[:, 0:1]
            for f in range(lay.shards):
                pa[slot_of(lay, d, f) + (slice(0, part),)] = dw[f * part : (f + 1) * part, :].astype(BF16)
        ared = Reduce(lay, me, pa, abufs, sems[2 * G], sems[2 * G + 1], True)
        ared.step(0)
        for i in range(4):
            cols = slice(i * (T // 4), (i + 1) * (T // 4))
            v = x_ref[:, cols].astype(F32)
            inverse = lax.rsqrt(jnp.mean(v * v, axis=0, keepdims=True) + EPS)
            scaled = v * inverse
            m = dot(wqkv_ref[...], draw[:, cols]) * again
            gt_ref[:, cols] += inverse * (m - scaled * jnp.mean(m * scaled, axis=0, keepdims=True))
            if i == 0:
                ared.step(1)
                reds[G - 1].step(4, oms[G - 1])
            if i == 1:
                ared.step(2)
            if i == 2:
                ared.step(3)
        ared.step(4, oa)

    n = lay.reduce_sems
    sd = jax.ShapeDtypeStruct
    V = pltpu.VMEM
    scratch = []
    for g in groups:
        scratch += Reduce.scratch(lay, rows_p, width_of(g), True)
    scratch += Reduce.scratch(lay, rows_p, wa, True)
    res = pl.pallas_call(
        kernel,
        out_shape=[sd((D, T), F32), sd((rows_p, wa), F32)] + [sd((rows_p, width_of(g)), F32) for g in groups],
        in_specs=[ANY] * 4 + [VMEM] * 14, out_specs=[VMEM] * (2 + G),
        scratch_shapes=scratch + [V(lay.slots + (rows_p, width_of(g)), BF16) for g in groups]
        + [V((nbuf, FF, T), BF16), V((D, T), BF16), V((Q_HEADS, T, HEAD_DIM), BF16), V((Q_HEADS, aug, T), BF16),
           V((Q_HEADS, T, HEAD_DIM), BF16), V((KV_HEADS, T, aug), BF16),
           V((KV_HEADS, T, HEAD_DIM), F32), V((KV_HEADS, T, HEAD_DIM), F32), V((HEAD_DIM, T), F32), V((E, T), BF16),
           V((D, wa), F32), V((D, E), F32), V((G + 1, 8, max([wa] + [width_of(g) for g in groups])), F32), V(lay.slots + (rows_p, wa), BF16), pltpu.SemaphoreType.DMA((4,))]
        + [pltpu.SemaphoreType.DMA((n,))] * (2 * G + 2),
        compiler_params=params(1), name="attend_back",
    )(*acts, gr, ct, nm, xt, nt, mix, qa, ka, kv, wqkv, wo, gain, ggain, cosine, sine)
    return finish(part, nf, nq, nk, groups, places, *res)


def finish(part, nf, nq, nk, groups, places, gt, attn, *mlp):
    G = len(groups)

    def kernel(*rest):
        gt_in, oa, oms, outs = rest[0], rest[1], rest[2 : 2 + G], rest[2 + G :]
        gt_ref, gq_ref, gk_ref, gv_ref, go_ref, gg_out, gu_out, gd_out, ga_out, gm_out = outs
        gt_ref[...] = gt_in[...]
        for k, group in enumerate(groups):
            for which, at, w in group:
                (gg_out, gu_out, gd_out)[which][...] = oms[k][0:part, at : at + w]
        rows_p = oa.shape[0]
        for b, (k, lane) in enumerate(places):
            go_ref[8 * b : 8 * b + 8, :] = (list(oms) + [oa])[k][rows_p - 8 : rows_p, lane : lane + part]
        gq_ref[...] = oa[0:part, 0:nq]
        turned = jnp.transpose(oa[...])
        gk_ref[...] = turned[nq : nq + nk, 0:part]
        gv_ref[...] = turned[nq + nk : nq + 2 * nk, 0:part]
        ga_out[...] = turned[nq + 2 * nk : nq + 2 * nk + 1, 0:part]
        gm_out[...] = turned[nq + 2 * nk + 1 : nq + 2 * nk + 2, 0:part]

    sd = jax.ShapeDtypeStruct
    return pl.pallas_call(
        kernel,
        out_shape=[sd(gt.shape, F32), sd((part, nq), F32), sd((nk, part), F32), sd((nk, part), F32), sd((nq, part), F32)]
        + [sd((part, nf), F32)] * 3 + [sd((1, part), F32)] * 2,
        in_specs=[VMEM] * (2 + G), out_specs=[VMEM] * 10,
        compiler_params=params(), name="cut_out",
    )(gt, attn, *mlp)


def on_device(tokens, segments, positions, attn_gain, mlp_gain, w_query, w_key, w_value, w_output, w_gate, w_up, w_down, cotangent):
    lay = Layout(lax.axis_size("dp"), lax.axis_size("fsdp"))
    part = attn_gain.shape[0]
    nq, nk, nf = w_query.shape[1], w_key.shape[1], w_gate.shape[1]
    half = HEAD_DIM // 2
    frequency = ROPE_BASE ** (-(2.0 * np.arange(half, dtype=np.float64)) / HEAD_DIM)
    frequency = jnp.asarray(frequency.astype(np.float32)[:, None])
    xt, ct = tokens.T, cotangent.T
    weights = (w_query, w_key.T, w_value.T, w_output, w_gate, w_up, w_down.T)
    gains = (attn_gain[None], mlp_gain[None])
    res = front(lay, weights, gains, xt, segments, positions, frequency)
    gms, (wqkv, gain, nt, qa, ka, kv, mix, cosine, sine, oex) = res[:-10], res[-10:]
    out, gr, ggain, wo, nm, hidden, dgate, dup = middle(lay, part, nf, nq, gms, oex, mix, gain, xt, ct)
    gt, gq, gk, gv, go, gg, gu, gd, ga, gm = back(
        lay, part, nf, nq, nk, (dgate, dup, hidden), gr, ct, nm, xt, nt, mix, qa, ka, kv, wqkv, wo, gain, ggain, cosine, sine)
    return (out.T, gt.T, ga[0], gm[0], gq, gk.T, gv.T, go, gg, gu, gd.T)


def solution(mesh):
    in_specs = (
        P(("dp", "fsdp"), None),
        P(("dp", "fsdp"), None),
        P(("dp", "fsdp"), None),
        P("fsdp"),
        P("fsdp"),
        P("fsdp", "dp"),
        P("fsdp", "dp"),
        P("fsdp", "dp"),
        P("dp", "fsdp"),
        P("fsdp", "dp"),
        P("fsdp", "dp"),
        P("dp", "fsdp"),
        P(("dp", "fsdp"), None),
    )
    out_specs = (
        P(("dp", "fsdp"), None),
        P(("dp", "fsdp"), None),
        P("fsdp"),
        P("fsdp"),
        P("fsdp", "dp"),
        P("fsdp", "dp"),
        P("fsdp", "dp"),
        P("dp", "fsdp"),
        P("fsdp", "dp"),
        P("fsdp", "dp"),
        P("dp", "fsdp"),
    )
    return jax.shard_map(
        on_device, mesh=mesh, in_specs=in_specs, out_specs=out_specs, check_vma=False
    )
```

```python
import numpy as np

import jax
import jax.numpy as jnp
from jax import lax
from jax.experimental import pallas as pl
from jax.experimental.pallas import tpu as pltpu
from jax.sharding import PartitionSpec as P


Q_HEADS = 9
KV_HEADS = 3
HEAD_DIM = 64
QW = 576
KVW = 192
EPS = 1e-05
ROPE_BASE = 100000.0
MASKED = -1e30
BF16 = jnp.bfloat16
F32 = jnp.float32
MESH = pl.DeviceIdType.MESH
ANY = pl.BlockSpec(memory_space=pl.ANY)
VMEM = pl.BlockSpec(memory_space=pltpu.VMEM)


def up(value, step):
    return -(-value // step) * step


class Layout:
    def __init__(self, pieces, shards):
        self.pieces, self.shards = pieces, shards
        self.C = 2 if pieces % 2 == 0 else 1
        self.Y = pieces // self.C
        self.X = 2 if shards <= 8 else 4
        self.Z = shards // self.X
        self.H = self.Z // 2
        self.slots = (self.C, self.Y, self.X, self.Z)
        n = (self.X - 1) + (self.Y - 1)
        self.gather_sems = 1 + (self.Z - 1) + 2 * n + 1 + 2 * n
        self.reduce_sems = 2 + 2 * n + (self.Z - 1)
        self.peers = (self.X - 1) + (self.Y - 1) + (self.Z - 1) + (self.C - 1)

    def here(self):
        dp, fs = lax.axis_index("dp"), lax.axis_index("fsdp")
        return lax.rem(dp, self.C), dp // self.C, lax.rem(fs, self.X), fs // self.X

    def device(self, c, y, x, z):
        return (y * self.C + c, z * self.X + x)

    def others(self, me, axis):
        size = self.slots[axis]
        for k in range(1, size):
            place = list(me)
            place[axis] = lax.rem(me[axis] + k, size)
            yield k, place

    def barrier(self, me):
        sem = pltpu.get_barrier_semaphore()
        for axis in range(4):
            for _, place in self.others(me, axis):
                pl.semaphore_signal(sem, inc=1, device_id=self.device(*place), device_id_type=MESH)
        pl.semaphore_wait(sem, self.peers)


class Sender:
    def __init__(self, layout, me, send, recv):
        self.lay, self.me, self.send, self.recv, self.used = layout, me, send, recv, 0

    def to(self, place, src, dst):
        k = self.used
        self.used += 1
        return pltpu.make_async_remote_copy(
            src_ref=src, dst_ref=dst, send_sem=self.send.at[k], recv_sem=self.recv.at[k],
            device_id=self.lay.device(*place), device_id_type=MESH)


def start(copies):
    for copy in copies:
        copy.start()


def wait(copies):
    for copy in copies:
        copy.wait()


class Gather:
    def __init__(self, lay, me, src, slots, send, recv):
        c, y, x, z = me
        s = Sender(lay, me, send, recv)
        X, Y, H, R = lay.X, lay.Y, lay.H, lay.Z - lay.H
        lo, hi = pl.ds(0, H), pl.ds(H, R)
        ax, ay = pl.ds(0, X), pl.ds(0, Y)
        sib = (1 - c, y, x, z)
        self.own = pltpu.make_async_copy(src, slots.at[c, y, x, z], recv.at[s.used])
        s.used += 1
        self.z = [s.to(p, src, slots.at[c, y, x, z]) for _, p in lay.others(me, 3)]
        part = slots.at[c, y, x, lo]
        self.xy1 = [s.to(p, part, part) for _, p in lay.others(me, 2)]
        part2 = slots.at[c, y, x, hi]
        self.xy1 += [s.to(p, part2, part2) for _, p in lay.others(me, 1)]
        part3 = slots.at[c, y, ax, lo]
        self.xy2 = [s.to(p, part3, part3) for _, p in lay.others(me, 1)]
        part4 = slots.at[c, ay, x, hi]
        self.xy2 += [s.to(p, part4, part4) for _, p in lay.others(me, 2)]
        self.core = [[], [], []]
        if lay.C > 1:
            whole = slots.at[c, y, x]
            self.core[0] = [s.to(sib, whole, whole)]
            for _, p in lay.others(me, 2):
                piece = slots.at[c, y, p[2], lo]
                self.core[1].append(s.to(sib, piece, piece))
            for _, p in lay.others(me, 1):
                piece = slots.at[c, p[1], x, hi]
                self.core[1].append(s.to(sib, piece, piece))
            for _, p in lay.others(me, 1):
                piece = slots.at[c, p[1], ax, lo]
                self.core[2].append(s.to(sib, piece, piece))
            for _, p in lay.others(me, 2):
                piece = slots.at[c, ay, p[2], hi]
                self.core[2].append(s.to(sib, piece, piece))

    def step(self, n):
        if n == 0:
            self.own.start()
            start(self.z)
        elif n == 1:
            self.own.wait()
            wait(self.z)
            start(self.xy1)
            start(self.core[0])
        elif n == 2:
            wait(self.xy1)
            start(self.xy2)
            start(self.core[1])
        elif n == 3:
            wait(self.xy2)
            start(self.core[2])
        else:
            for copies in self.core:
                wait(copies)


class Reduce:
    def __init__(self, lay, me, parts, bufs, send, recv, inplace):
        c, y, x, z = me
        self.lay, self.me = lay, me
        self.far, self.r2a, self.r2b, self.r3a, self.r3b, self.r4 = bufs[:6]
        self.out = parts.at[c] if inplace else bufs[6]
        s = Sender(lay, me, send, recv)
        X, Y, H, R = lay.X, lay.Y, lay.H, lay.Z - lay.H
        lo, hi = pl.ds(0, H), pl.ds(H, R)
        ax, ay = pl.ds(0, X), pl.ds(0, Y)
        out = self.out
        self.own = None if inplace else pltpu.make_async_copy(parts.at[c], self.out, recv.at[s.used])
        s.used += 1
        self.core = [s.to((1 - c, y, x, z), parts.at[1 - c], self.far)] if lay.C > 1 else []
        self.xy1 = [s.to(p, out.at[p[1], ax, lo], self.r2a.at[k - 1]) for k, p in lay.others(me, 1)]
        self.xy1 += [s.to(p, out.at[ay, p[2], hi], self.r2b.at[k - 1]) for k, p in lay.others(me, 2)]
        self.xy2 = [s.to(p, out.at[y, p[2], lo], self.r3a.at[k - 1]) for k, p in lay.others(me, 2)]
        self.xy2 += [s.to(p, out.at[p[1], x, hi], self.r3b.at[k - 1]) for k, p in lay.others(me, 1)]
        self.zs = [s.to(p, out.at[y, x, p[3]], self.r4.at[k - 1]) for k, p in lay.others(me, 3)]

    @staticmethod
    def scratch(lay, rows, width, inplace):
        X, Y, Z, H = lay.X, lay.Y, lay.Z, lay.H
        R = Z - H
        tail = (rows, width)
        return [
            pltpu.VMEM((Y, X, Z) + tail, BF16),
            pltpu.VMEM((Y - 1, X, H) + tail, BF16), pltpu.VMEM((X - 1, Y, R) + tail, BF16),
            pltpu.VMEM((X - 1, H) + tail, BF16), pltpu.VMEM((Y - 1, R) + tail, BF16),
            pltpu.VMEM((Z - 1,) + tail, BF16),
        ] + ([] if inplace else [pltpu.VMEM((Y, X, Z) + tail, BF16)])

    def step(self, n, result=None):
        lay, (c, y, x, z) = self.lay, self.me
        X, Y, Z, H = lay.X, lay.Y, lay.Z, lay.H
        out = self.out
        if n == 0:
            if self.own is not None:
                self.own.start()
            start(self.core)
        elif n == 1:
            if self.own is not None:
                self.own.wait()
            wait(self.core)

            @pl.loop(0, Y * X * Z)
            def _(i):
                yy, xx, zz = i // (X * Z), lax.rem(i // Z, X), lax.rem(i, Z)
                v = out[yy, xx, zz].astype(F32)
                if lay.C > 1:
                    v = v + self.far[yy, xx, zz].astype(F32)
                out[yy, xx, zz] = v.astype(BF16)

            start(self.xy1)
        elif n == 2:
            wait(self.xy1)

            @pl.loop(0, X * H)
            def _(i):
                xx, zz = i // H, lax.rem(i, H)
                v = out[y, xx, zz].astype(F32)
                for k in range(Y - 1):
                    v = v + self.r2a[k, xx, zz].astype(F32)
                out[y, xx, zz] = v.astype(BF16)

            @pl.loop(0, Y * (Z - H))
            def _(i):
                yy, zz = i // (Z - H), lax.rem(i, Z - H)
                v = out[yy, x, H + zz].astype(F32)
                for k in range(X - 1):
                    v = v + self.r2b[k, yy, zz].astype(F32)
                out[yy, x, H + zz] = v.astype(BF16)

            start(self.xy2)
        elif n == 3:
            wait(self.xy2)

            @pl.loop(0, H)
            def _(i):
                v = out[y, x, i].astype(F32)
                for k in range(X - 1):
                    v = v + self.r3a[k, i].astype(F32)
                out[y, x, i] = v.astype(BF16)

            @pl.loop(0, Z - H)
            def _(i):
                v = out[y, x, H + i].astype(F32)
                for k in range(Y - 1):
                    v = v + self.r3b[k, i].astype(F32)
                out[y, x, H + i] = v.astype(BF16)

            start(self.zs)
        else:
            wait(self.zs)
            v = out[y, x, z].astype(F32)
            for k in range(Z - 1):
                v = v + self.r4[k].astype(F32)
            result[...] = v


QB = 256


def dot(a, b, ca=1, cb=0):
    return lax.dot_general(a, b, (((ca,), (cb,)), ((), ())), preferred_element_type=F32)


def slot_of(lay, d, f):
    return (d % lay.C, d // lay.C, f % lay.X, f // lay.X)


def groups_of(nf):
    if nf % 128 == 0:
        return (((0, 0, nf),), ((1, 0, nf),), ((2, 0, nf),))
    return (((0, 0, nf), (1, nf, nf)), ((2, 0, nf),))


def out_places(part, nq, groups, wa):
    places = []
    for k, width in enumerate([width_of(g) for g in groups] + [wa]):
        places += [(k, j * part) for j in range(width // part)]
    return places[: nq // 8]


def width_of(group):
    return up(group[-1][1] + group[-1][2], 128)


def params(which=None):
    extra = {} if which is None else dict(collective_id=which, has_side_effects=True)
    return pltpu.CompilerParams(vmem_limit_bytes=62 * 2**20, **extra)


def eye(n):
    return (lax.broadcasted_iota(jnp.int32, (n, n), 0) == lax.broadcasted_iota(jnp.int32, (n, n), 1)).astype(F32).astype(BF16)


def split_rows(value, first, base):
    hi = value.astype(BF16).astype(F32)
    mid = (value - hi).astype(BF16).astype(F32)
    low = value - hi - mid
    row = lax.broadcasted_iota(jnp.int32, base.shape, 0)
    return jnp.where(row == first, hi, jnp.where(row == first + 1, mid, jnp.where(row == first + 2, low, base)))


def column(one, ref):
    wide = jnp.broadcast_to(ref[...].astype(F32), (16, ref.shape[1])).astype(BF16)
    return dot(one, wide, 1, 1)[:, 0:1].astype(BF16)


def front(lay, weights, gains, xt, segments, positions, frequency):
    wq, wkt, wvt, wo, wg, wu, wdt = weights
    part, nq = wq.shape
    nk, nf = wkt.shape[0], wg.shape[1]
    rows_p = up(part + 8, 16)
    wa = up(nq + 2 * nk + 2, 128)
    D, T = xt.shape
    E = QW + 2 * KVW
    half = HEAD_DIM // 2
    groups = groups_of(nf)
    G = len(groups)
    places = out_places(part, nq, groups, wa)
    last = slice(rows_p - 8, rows_p)
    aug = HEAD_DIM + 16

    def kernel(wq_ref, wkt_ref, wvt_ref, wo_in, wg_ref, wu_ref, wdt_ref, ag_ref, mg_ref, x_ref, seg_ref, pos_ref, fr_ref, *rest):
        gms, rest = rest[:G], rest[G:]
        (wqkv_ref, gain_ref, nt_ref, qa_ref, ka_ref, kv_ref, mix_ref, cos_ref, sin_ref, oex_ref), rest = rest[:10], rest[10:]
        pms, rest = rest[:G], rest[G:]
        (pa, ga_ref, tmp, scaled, wt, kt, lse_ref), sems = rest[:7], rest[7:]
        one = eye(part)
        pa[0:part, 0:nq] = wq_ref[...]
        pa[0:part, nq : nq + nk] = dot(one, wkt_ref[...], 1, 1).astype(BF16)
        pa[0:part, nq + nk : nq + 2 * nk] = dot(one, wvt_ref[...], 1, 1).astype(BF16)
        pa[0:part, nq + 2 * nk : nq + 2 * nk + 1] = column(one, ag_ref)
        pa[0:part, nq + 2 * nk + 1 : nq + 2 * nk + 2] = column(one, mg_ref)
        for b, (k, lane) in enumerate(places):
            (list(pms) + [pa])[k][last, lane : lane + part] = wo_in[8 * b : 8 * b + 8, :]
        me = lay.here()
        lay.barrier(me)
        ga = Gather(lay, me, pa, ga_ref, sems[0], sems[1])
        gm = [Gather(lay, me, pms[k], gms[k], sems[2 + 2 * k], sems[3 + 2 * k]) for k in range(G)]
        ga.step(0)
        for k, group in enumerate(groups):
            for which, at, size in group:
                pms[k][0:part, at : at + size] = (wg_ref, wu_ref, wdt_ref)[which][...]
        v = x_ref[...].astype(F32)
        scaled[...] = v * lax.rsqrt(jnp.mean(v * v, axis=0, keepdims=True) + EPS)
        angles = fr_ref[...] * pos_ref[...].astype(F32)
        cos_ref[...] = jnp.cos(angles)
        sin_ref[...] = jnp.sin(angles)
        ga.step(1)
        for gather in gm:
            gather.step(0)
        ga.step(2)
        ga.step(3)
        gm[0].step(1)
        ga.step(4)
        for d in range(lay.pieces):
            for f in range(lay.shards):
                tmp[f * part : (f + 1) * part, :] = ga_ref[slot_of(lay, d, f)].astype(F32)[:part]
                oex_ref[d * lay.shards + f] = ga_ref[slot_of(lay, d, f) + (last,)]
            wqkv_ref[:, d * nq : (d + 1) * nq] = tmp[:, 0:nq].astype(BF16)
            wqkv_ref[:, QW + d * nk : QW + (d + 1) * nk] = tmp[:, nq : nq + nk].astype(BF16)
            wqkv_ref[:, QW + KVW + d * nk : QW + KVW + (d + 1) * nk] = tmp[:, nq + nk : nq + 2 * nk].astype(BF16)
        gain_ref[:, 0:2] = tmp[:, nq + 2 * nk : nq + 2 * nk + 2]
        gm[0].step(2)
        gm[1].step(1)
        wt[...] = jnp.transpose(wqkv_ref[...])
        nt_ref[...] = (scaled[...] * gain_ref[:, 0:1]).astype(BF16)

        @pl.loop(0, T // QB)
        def _(i):
            cols = pl.ds(pl.multiple_of(i * QB, QB), QB)
            raw = dot(wt[...], nt_ref[:, cols])
            cs, sn = cos_ref[:, cols], sin_ref[:, cols]
            for h in range(Q_HEADS + KV_HEADS):
                u1, u2 = raw[h * HEAD_DIM : h * HEAD_DIM + half], raw[h * HEAD_DIM + half : (h + 1) * HEAD_DIM]
                o1 = (u1 * cs - u2 * sn).astype(BF16)
                o2 = (u2 * cs + u1 * sn).astype(BF16)
                if h < Q_HEADS:
                    scale = HEAD_DIM ** (-0.5)
                    qa_ref[h, 0:half, cols] = o1 * scale
                    qa_ref[h, half:HEAD_DIM, cols] = o2 * scale
                else:
                    g = (h - Q_HEADS) * HEAD_DIM
                    kv_ref[g : g + half, cols] = o1
                    kv_ref[g + half : g + HEAD_DIM, cols] = o2
            kv_ref[KVW:, cols] = raw[QW + KVW :].astype(BF16)

        gm[0].step(3)
        gm[1].step(2)
        if G > 2:
            gm[2].step(1)
        row = lax.broadcasted_iota(jnp.int32, (16, T), 0)
        same = row == seg_ref[...]
        qrows = jnp.where(row < 3, jnp.where(same, 0.0, MASKED), 0.0).astype(BF16)
        kt[HEAD_DIM:, :] = jnp.where(row < 3, jnp.where(same, 1.0, 0.0), jnp.where(row < 6, 1.0, 0.0)).astype(BF16)
        for h in range(Q_HEADS):
            qa_ref[h, HEAD_DIM:, :] = qrows
        for g in range(KV_HEADS):
            kt[0:HEAD_DIM, :] = kv_ref[g * HEAD_DIM : (g + 1) * HEAD_DIM, :]
            ka_ref[g] = jnp.transpose(kt[...])
        causal = lax.broadcasted_iota(jnp.int32, (QB, QB), 0) <= lax.broadcasted_iota(jnp.int32, (QB, QB), 1)
        for i in range(T // QB):
            q0, k0 = i * QB, 0 if i == 0 else 128

            @pl.loop(0, Q_HEADS)
            def _(h):
                g = h // (Q_HEADS // KV_HEADS)
                vrow = pl.ds(pl.multiple_of(KVW + g * HEAD_DIM, HEAD_DIM), HEAD_DIM)
                qcol = qa_ref[h, :, q0 : q0 + QB]
                s = jnp.where(causal, dot(ka_ref[g, q0 : q0 + QB, :], qcol), MASKED)
                top = jnp.max(s, axis=0, keepdims=True)
                if i:
                    s2 = dot(ka_ref[g, k0:q0, :], qcol)
                    top = jnp.maximum(top, jnp.max(s2, axis=0, keepdims=True))
                e = jnp.exp(s - top)
                total = jnp.sum(e, axis=0, keepdims=True)
                if i:
                    e2 = jnp.exp(s2 - top)
                    total = total + jnp.sum(e2, axis=0, keepdims=True)
                inv = 1.0 / total
                out = dot(kv_ref[vrow, q0 : q0 + QB], (e * inv).astype(BF16))
                if i:
                    out = out + dot(kv_ref[vrow, k0:q0], (e2 * inv).astype(BF16))
                mix_ref[pl.ds(pl.multiple_of(h * HEAD_DIM, HEAD_DIM), HEAD_DIM), q0 : q0 + QB] = out.astype(BF16)
                lse_ref[h, :, q0 : q0 + QB] = top + jnp.log(total)

            if i == 1:
                gm[1].step(3)
                if G > 2:
                    gm[2].step(2)
            if i == 2 and G > 2:
                gm[2].step(3)
        base = qrows.astype(F32)
        for h in range(Q_HEADS):
            qa_ref[h, HEAD_DIM:, :] = split_rows(-lse_ref[h], 3, base).astype(BF16)
        for gather in gm:
            gather.step(4)

    n = lay.gather_sems
    sd = jax.ShapeDtypeStruct
    V = pltpu.VMEM
    return pl.pallas_call(
        kernel,
        out_shape=[sd(lay.slots + (rows_p, width_of(g)), BF16) for g in groups]
        + [sd((D, E), BF16), sd((D, 8), F32), sd((D, T), BF16),
           sd((Q_HEADS, aug, T), BF16), sd((KV_HEADS, T, aug), BF16), sd((2 * KVW, T), BF16), sd((QW, T), BF16),
           sd((half, T), F32), sd((half, T), F32), sd((lay.pieces * lay.shards, 8, wa), BF16)],
        in_specs=[VMEM] * 13, out_specs=[ANY] * G + [VMEM] * 10,
        scratch_shapes=[V((rows_p, width_of(g)), BF16) for g in groups]
        + [V((rows_p, wa), BF16), V(lay.slots + (rows_p, wa), BF16), V((D, wa), F32), V((D, T), F32), V((E, D), BF16), V((aug, T), BF16), V((Q_HEADS, 1, T), F32)]
        + [pltpu.SemaphoreType.DMA((n,))] * (2 + 2 * G),
        compiler_params=params(0), name="gather_attend",
    )(*weights, *gains, xt, segments, positions, frequency)


def middle(lay, part, nf, nq, gms, oex, mix, gain, xt, ct):
    D, T = xt.shape
    FF = nf * lay.pieces
    groups = groups_of(nf)
    G = len(groups)
    places = out_places(part, nq, groups, oex.shape[-1])
    wmax = max(width_of(g) for g in groups)
    rows_p = gms[0].shape[-2]
    items = [(k, d) for k in range(G) for d in range(lay.pieces)]

    def kernel(*rest):
        gm_refs, rest = rest[:G], rest[G:]
        oex_ref, rest = rest[0], rest[1:]
        (mix_ref, gain_ref, x_ref, c_ref, o_out, r_out, gg_ref, wo_ref, n_out, h_out, g_out, u_out), rest = rest[:12], rest[12:]
        stages, rest = rest[:G], rest[G:]
        tmp, wg, wu, wd, wgt, wut, wdt, wot, out_ref, gr_ref, normed, hidden, dgate, dup, sem, out_sem = rest

        def fetch(n):
            k, d = items[n]
            c, y = d % lay.C, d // lay.C
            return pltpu.make_async_copy(gm_refs[k].at[c, y], stages[k].at[d % 2], sem.at[n])

        def put(k, d, f, rows):
            for b, (pack, lane) in enumerate(places):
                if pack == k:
                    at = d * nq + 8 * b
                    gr_ref[at : at + 8, f * part : (f + 1) * part] = rows[:, lane : lane + part]

        fetch(0).start()
        fetch(1).start()
        for n, (k, d) in enumerate(items):
            fetch(n).wait()
            size = width_of(groups[k])
            for f in range(lay.shards):
                piece = stages[k][d % 2, f % lay.X, f // lay.X].astype(F32)
                tmp[f * part : (f + 1) * part, 0:size] = piece[:part]
                put(k, d, f, piece[rows_p - 8 :])
            if n + 2 < len(items):
                fetch(n + 2).start()
            for which, at, w in groups[k]:
                (wg, wu, wd)[which][:, d * w : (d + 1) * w] = tmp[:, at : at + w].astype(BF16)
        for d in range(lay.pieces):
            for f in range(lay.shards):
                put(G, d, f, oex_ref[d * lay.shards + f].astype(F32))
        wo_ref[...] = gr_ref[:, 0:D].astype(BF16)
        wot[...] = jnp.transpose(wo_ref[...])
        wgt[...] = jnp.transpose(wg[...])
        wut[...] = jnp.transpose(wu[...])
        wdt[...] = jnp.transpose(wd[...])
        gain = gain_ref[:, 1:2]

        def send(i, cols):
            pairs = ((hidden, h_out), (dgate, g_out), (dup, u_out), (out_ref, o_out), (gr_ref, r_out), (normed, n_out))
            return [pltpu.make_async_copy(a.at[:, cols], b.at[:, cols], out_sem.at[i, k]) for k, (a, b) in enumerate(pairs)]

        gg_ref[...] = jnp.zeros_like(gg_ref)

        @pl.loop(0, T // QB)
        def _(i):
            cols = pl.ds(pl.multiple_of(i * QB, QB), QB)
            cot = c_ref[:, cols]
            resid = x_ref[:, cols].astype(F32) + dot(wot[...], mix_ref[:, cols])
            inverse = lax.rsqrt(jnp.mean(resid * resid, axis=0, keepdims=True) + EPS)
            scaled = resid * inverse
            nb = (scaled * gain).astype(BF16)
            normed[:, cols] = nb
            out = resid
            gnm = jnp.zeros_like(resid)
            for j in range(2):
                rows = slice(j * (FF // 2), (j + 1) * (FF // 2))
                gate = dot(wgt[rows, :], nb)
                upp = dot(wut[rows, :], nb)
                gh = dot(wdt[rows, :], cot)
                s = jax.nn.sigmoid(gate)
                act = gate * s
                hb = (act * upp).astype(BF16)
                hidden[rows, cols] = hb
                dg = (gh * upp * (s * (1.0 + gate * (1.0 - s)))).astype(BF16)
                du = (gh * act).astype(BF16)
                dgate[rows, cols] = dg
                dup[rows, cols] = du
                out = out + dot(wd[:, rows], hb)
                gnm = gnm + dot(wg[:, rows], dg) + dot(wu[:, rows], du)
            out_ref[:, cols] = out.astype(BF16)
            gg_ref[:, 0:1] += jnp.sum(gnm * scaled, axis=1, keepdims=True)
            m = gnm * gain
            back = inverse * (m - scaled * jnp.mean(m * scaled, axis=0, keepdims=True))
            gr_ref[:, cols] = cot.astype(F32) + back
            for copy in send(i, cols):
                copy.start()

        for i in range(T // QB):
            for copy in send(i, slice(i * QB, (i + 1) * QB)):
                copy.wait()

    sd = jax.ShapeDtypeStruct
    V = pltpu.VMEM
    res = pl.pallas_call(
        kernel,
        out_shape=[sd((D, T), BF16), sd((D, T), F32), sd((D, 8), F32), sd((QW, D), BF16), sd((D, T), BF16)] + [sd((FF, T), BF16)] * 3,
        in_specs=[ANY] * G + [VMEM] * 5, out_specs=[ANY] * 2 + [VMEM] * 2 + [ANY] * 4,
        scratch_shapes=[V((2, lay.X, lay.Z) + g.shape[-2:], BF16) for g in gms]
        + [V((D, wmax), F32)] + [V((D, FF), BF16)] * 3 + [V((FF, D), BF16)] * 3 + [V((D, QW), BF16), V((D, T), BF16), V((D, T), F32), V((D, T), BF16)]
        + [V((FF, T), BF16)] * 3 + [pltpu.SemaphoreType.DMA((len(items),)), pltpu.SemaphoreType.DMA((T // QB, 6))],
        compiler_params=params(), name="mlp",
    )(*gms, oex, mix, gain, xt, ct)
    return res


def back(lay, part, nf, nq, nk, acts, gr, ct, nm, xt, nt, mix, qa, ka, kv, wqkv, wo, gain, ggain, cosine, sine):
    D, T = xt.shape
    E = QW + 2 * KVW
    aug = HEAD_DIM + 16
    half = HEAD_DIM // 2
    groups = groups_of(nf)
    G = len(groups)
    rows_p = up(part + 8, 16)
    wa = up(nq + 2 * nk + 2, 128)
    places = out_places(part, nq, groups, wa)
    last = slice(rows_p - 8, rows_p)
    FF = nf * lay.pieces
    if G > 2:
        early = ((), ((0, 1),), ((1, 1),))
        ready = ()
        plan = ((0, 0, 2), (1, 2, 1), (3, 1, 2), (3, 0, 3), (5, 2, 2), (5, 1, 3), (7, 0, 4), (8, 1, 4))
    else:
        early = ((), ((0, 1),))
        ready = ()
        plan = ((0, 1, 1), (1, 0, 2), (3, 0, 3), (4, 1, 2), (6, 0, 4), (7, 1, 3))
    nbuf = 2 if G > 2 else 1

    def kernel(*rest):
        a_refs, gr_in, rest = rest[:3], rest[3], rest[4:]
        (ct_ref, nm_ref, x_ref, nt_ref, mix_ref, qa_ref, ka_ref, kv_ref, wqkv_ref, wo_ref, gain_ref, gg_ref, cos_ref, sin_ref), rest = rest[:14], rest[14:]
        gt_ref, oa, rest = rest[0], rest[1], rest[2:]
        oms, rest = rest[:G], rest[G:]
        mbufs, rest = [rest[6 * k : 6 * k + 6] for k in range(G)], rest[6 * G :]
        abufs, rest = rest[:6], rest[6:]
        p_refs, rest = rest[:G], rest[G:]
        (big, gb, don, doa, qn, va, dk, dv, dq, draw, dw, wide, line, pa, big_sem), sems = rest[:15], rest[15:]
        me = lay.here()
        lay.barrier(me)
        reds = [Reduce(lay, me, p_refs[k], mbufs[k], sems[2 * k], sems[2 * k + 1], True) for k in range(G)]

        def fetch(which):
            return pltpu.make_async_copy(a_refs[which], big.at[which % nbuf], big_sem.at[which])

        load = pltpu.make_async_copy(gr_in, gt_ref, big_sem.at[3])
        for which in range(nbuf):
            fetch(which).start()
        load.start()
        load.wait()
        gb[...] = gt_ref[...].astype(BF16)
        wide[:, 0:D] = dot(mix_ref[...], gb[...], 1, 1)
        packs = list(p_refs) + [pa]
        for d in range(lay.pieces):
            for f in range(lay.shards):
                for k in sorted({pack for pack, _ in places}):
                    for b, (pack, lane) in enumerate(places):
                        if pack == k:
                            at = d * nq + 8 * b
                            line[k, :, lane : lane + part] = wide[at : at + 8, f * part : (f + 1) * part]
                    width = packs[k].shape[-1]
                    packs[k][slot_of(lay, d, f) + (last,)] = line[k, :, 0:width].astype(BF16)
        for k, group in enumerate(groups):
            for which, at, w in group:
                fetch(which).wait()
                for d in range(lay.pieces):
                    rows = slice(d * w, (d + 1) * w)
                    value = dot(ct_ref[...] if which == 2 else nm_ref[...], big[which % nbuf, rows, :], 1, 1)
                    wide[:, 0:w] = value
                    for f in range(lay.shards):
                        p_refs[k][slot_of(lay, d, f) + (slice(0, part), slice(at, at + w))] = wide[f * part : (f + 1) * part, 0:w].astype(BF16)
                if which + nbuf < 3:
                    fetch(which + nbuf).start()
            reds[k].step(0)
            for kk, n in early[k]:
                reds[kk].step(n)
        zero = jnp.zeros((16, T), F32)

        @pl.loop(0, Q_HEADS)
        def _(h):
            rows = pl.ds(pl.multiple_of(h * HEAD_DIM, HEAD_DIM), HEAD_DIM)
            t = dot(wo_ref[rows, :], gb[...]).astype(BF16)
            doa[h, 0:HEAD_DIM, :] = t
            don[h] = jnp.transpose(t)
            delta = jnp.sum(t.astype(F32) * mix_ref[rows, :].astype(F32), axis=0, keepdims=True)
            doa[h, HEAD_DIM:, :] = split_rows(-delta, 0, zero).astype(BF16)
            qn[h] = jnp.transpose(qa_ref[h, 0:HEAD_DIM, :])

        for k, n in ready:
            reds[k].step(n)
        ones = jnp.where(lax.broadcasted_iota(jnp.int32, (T, 16), 1) < 3, 1.0, 0.0).astype(BF16)
        for g in range(KV_HEADS):
            va[g, :, 0:HEAD_DIM] = jnp.transpose(kv_ref[KVW + g * HEAD_DIM : KVW + (g + 1) * HEAD_DIM, :])
            va[g, :, HEAD_DIM:] = ones
        dk[...] = jnp.zeros_like(dk)
        dv[...] = jnp.zeros_like(dv)
        causal = lax.broadcasted_iota(jnp.int32, (QB, QB), 0) <= lax.broadcasted_iota(jnp.int32, (QB, QB), 1)

        @pl.loop(0, Q_HEADS)
        def _(h):
            g = h // (Q_HEADS // KV_HEADS)
            krow = pl.ds(pl.multiple_of(g * HEAD_DIM, HEAD_DIM), HEAD_DIM)
            for j in range(T // QB):
                k0, k1 = j * QB, (j + 1) * QB
                blocks = [(k0, k1, k0, k1, True)]
                if k1 < T:
                    blocks.append((k0 if j else 128, k1, k1, T, False))
                for a, b, c, d, diagonal in blocks:
                    st = dot(ka_ref[g, a:b, :], qa_ref[h, :, c:d])
                    p = jnp.exp(st)
                    if diagonal:
                        p = jnp.where(causal, p, 0.0)
                    dp = dot(va[g, a:b, :], doa[h, :, c:d])
                    ds = (p * dp).astype(BF16)
                    dv[g, a:b, :] += dot(p.astype(BF16), don[h, c:d, :])
                    dk[g, a:b, :] += dot(ds, qn[h, c:d, :])
                    part_q = dot(kv_ref[krow, a:b], ds)
                    if j == 0:
                        dq[:, c:d] = part_q
                    else:
                        dq[:, c:d] += part_q
            scale = HEAD_DIM ** (-0.5)
            d1, d2 = dq[0:half, :] * scale, dq[half:, :] * scale
            cs, sn = cos_ref[...], sin_ref[...]
            at = pl.multiple_of(h * HEAD_DIM, HEAD_DIM)
            draw[pl.ds(at, half), :] = (d1 * cs + d2 * sn).astype(BF16)
            draw[pl.ds(at + half, half), :] = (d2 * cs - d1 * sn).astype(BF16)
            for when, k, n in plan:

                @pl.when(h == when)
                def _():
                    reds[k].step(n, oms[k])

        cs, sn = cos_ref[...], sin_ref[...]
        for g in range(KV_HEADS):
            t = jnp.transpose(dk[g])
            d1, d2 = t[0:half], t[half:]
            at = QW + g * HEAD_DIM
            draw[at : at + half, :] = (d1 * cs + d2 * sn).astype(BF16)
            draw[at + half : at + HEAD_DIM, :] = (d2 * cs - d1 * sn).astype(BF16)
            at = QW + KVW + g * HEAD_DIM
            draw[at : at + HEAD_DIM, :] = jnp.transpose(dv[g]).astype(BF16)
        wide[:, 0:E] = dot(nt_ref[...], draw[...], 1, 1)
        again = gain_ref[:, 0:1]
        if G > 2:
            reds[2].step(3, oms[2])
        gattn = jnp.sum(wide[:, 0:E] * wqkv_ref[...].astype(F32), axis=1, keepdims=True) / again
        for d in range(lay.pieces):
            dw[:, 0:nq] = wide[:, d * nq : (d + 1) * nq]
            dw[:, nq : nq + nk] = wide[:, QW + d * nk : QW + (d + 1) * nk]
            dw[:, nq + nk : nq + 2 * nk] = wide[:, QW + KVW + d * nk : QW + KVW + (d + 1) * nk]
            dw[:, nq + 2 * nk : nq + 2 * nk + 1] = gattn
            dw[:, nq + 2 * nk + 1 : nq + 2 * nk + 2] = gg_ref[:, 0:1]
            for f in range(lay.shards):
                pa[slot_of(lay, d, f) + (slice(0, part),)] = dw[f * part : (f + 1) * part, :].astype(BF16)
        ared = Reduce(lay, me, pa, abufs, sems[2 * G], sems[2 * G + 1], True)
        ared.step(0)
        for i in range(4):
            cols = slice(i * (T // 4), (i + 1) * (T // 4))
            v = x_ref[:, cols].astype(F32)
            inverse = lax.rsqrt(jnp.mean(v * v, axis=0, keepdims=True) + EPS)
            scaled = v * inverse
            m = dot(wqkv_ref[...], draw[:, cols]) * again
            gt_ref[:, cols] += inverse * (m - scaled * jnp.mean(m * scaled, axis=0, keepdims=True))
            if i == 0:
                ared.step(1)
                reds[G - 1].step(4, oms[G - 1])
            if i == 1:
                ared.step(2)
            if i == 2:
                ared.step(3)
        ared.step(4, oa)

    n = lay.reduce_sems
    sd = jax.ShapeDtypeStruct
    V = pltpu.VMEM
    scratch = []
    for g in groups:
        scratch += Reduce.scratch(lay, rows_p, width_of(g), True)
    scratch += Reduce.scratch(lay, rows_p, wa, True)
    res = pl.pallas_call(
        kernel,
        out_shape=[sd((D, T), F32), sd((rows_p, wa), F32)] + [sd((rows_p, width_of(g)), F32) for g in groups],
        in_specs=[ANY] * 4 + [VMEM] * 14, out_specs=[VMEM] * (2 + G),
        scratch_shapes=scratch + [V(lay.slots + (rows_p, width_of(g)), BF16) for g in groups]
        + [V((nbuf, FF, T), BF16), V((D, T), BF16), V((Q_HEADS, T, HEAD_DIM), BF16), V((Q_HEADS, aug, T), BF16),
           V((Q_HEADS, T, HEAD_DIM), BF16), V((KV_HEADS, T, aug), BF16),
           V((KV_HEADS, T, HEAD_DIM), F32), V((KV_HEADS, T, HEAD_DIM), F32), V((HEAD_DIM, T), F32), V((E, T), BF16),
           V((D, wa), F32), V((D, E), F32), V((G + 1, 8, max([wa] + [width_of(g) for g in groups])), F32), V(lay.slots + (rows_p, wa), BF16), pltpu.SemaphoreType.DMA((4,))]
        + [pltpu.SemaphoreType.DMA((n,))] * (2 * G + 2),
        compiler_params=params(1), name="attend_back",
    )(*acts, gr, ct, nm, xt, nt, mix, qa, ka, kv, wqkv, wo, gain, ggain, cosine, sine)
    return finish(part, nf, nq, nk, groups, places, *res)


def finish(part, nf, nq, nk, groups, places, gt, attn, *mlp):
    G = len(groups)

    def kernel(*rest):
        gt_in, oa, oms, outs = rest[0], rest[1], rest[2 : 2 + G], rest[2 + G :]
        gt_ref, gq_ref, gk_ref, gv_ref, go_ref, gg_out, gu_out, gd_out, ga_out, gm_out = outs
        gt_ref[...] = gt_in[...]
        for k, group in enumerate(groups):
            for which, at, w in group:
                (gg_out, gu_out, gd_out)[which][...] = oms[k][0:part, at : at + w]
        rows_p = oa.shape[0]
        for b, (k, lane) in enumerate(places):
            go_ref[8 * b : 8 * b + 8, :] = (list(oms) + [oa])[k][rows_p - 8 : rows_p, lane : lane + part]
        gq_ref[...] = oa[0:part, 0:nq]
        turned = jnp.transpose(oa[...])
        gk_ref[...] = turned[nq : nq + nk, 0:part]
        gv_ref[...] = turned[nq + nk : nq + 2 * nk, 0:part]
        ga_out[...] = turned[nq + 2 * nk : nq + 2 * nk + 1, 0:part]
        gm_out[...] = turned[nq + 2 * nk + 1 : nq + 2 * nk + 2, 0:part]

    sd = jax.ShapeDtypeStruct
    return pl.pallas_call(
        kernel,
        out_shape=[sd(gt.shape, F32), sd((part, nq), F32), sd((nk, part), F32), sd((nk, part), F32), sd((nq, part), F32)]
        + [sd((part, nf), F32)] * 3 + [sd((1, part), F32)] * 2,
        in_specs=[VMEM] * (2 + G), out_specs=[VMEM] * 10,
        compiler_params=params(), name="cut_out",
    )(gt, attn, *mlp)


def on_device(tokens, segments, positions, attn_gain, mlp_gain, w_query, w_key, w_value, w_output, w_gate, w_up, w_down, cotangent):
    lay = Layout(lax.axis_size("dp"), lax.axis_size("fsdp"))
    part = attn_gain.shape[0]
    nq, nk, nf = w_query.shape[1], w_key.shape[1], w_gate.shape[1]
    half = HEAD_DIM // 2
    frequency = ROPE_BASE ** (-(2.0 * np.arange(half, dtype=np.float64)) / HEAD_DIM)
    frequency = jnp.asarray(frequency.astype(np.float32)[:, None])
    xt, ct = tokens.T, cotangent.T
    weights = (w_query, w_key.T, w_value.T, w_output, w_gate, w_up, w_down.T)
    gains = (attn_gain[None], mlp_gain[None])
    res = front(lay, weights, gains, xt, segments, positions, frequency)
    gms, (wqkv, gain, nt, qa, ka, kv, mix, cosine, sine, oex) = res[:-10], res[-10:]
    out, gr, ggain, wo, nm, hidden, dgate, dup = middle(lay, part, nf, nq, gms, oex, mix, gain, xt, ct)
    gt, gq, gk, gv, go, gg, gu, gd, ga, gm = back(
        lay, part, nf, nq, nk, (dgate, dup, hidden), gr, ct, nm, xt, nt, mix, qa, ka, kv, wqkv, wo, gain, ggain, cosine, sine)
    return (out.T, gt.T, ga[0], gm[0], gq, gk.T, gv.T, go, gg, gu, gd.T)


def solution(mesh):
    in_specs = (
        P(("dp", "fsdp"), None),
        P(("dp", "fsdp"), None),
        P(("dp", "fsdp"), None),
        P("fsdp"),
        P("fsdp"),
        P("fsdp", "dp"),
        P("fsdp", "dp"),
        P("fsdp", "dp"),
        P("dp", "fsdp"),
        P("fsdp", "dp"),
        P("fsdp", "dp"),
        P("dp", "fsdp"),
        P(("dp", "fsdp"), None),
    )
    out_specs = (
        P(("dp", "fsdp"), None),
        P(("dp", "fsdp"), None),
        P("fsdp"),
        P("fsdp"),
        P("fsdp", "dp"),
        P("fsdp", "dp"),
        P("fsdp", "dp"),
        P("dp", "fsdp"),
        P("fsdp", "dp"),
        P("fsdp", "dp"),
        P("dp", "fsdp"),
    )
    return jax.shard_map(
        on_device, mesh=mesh, in_specs=in_specs, out_specs=out_specs, check_vma=False
    )
```

```python
import numpy as np

import jax
import jax.numpy as jnp
from jax import lax
from jax.experimental import pallas as pl
from jax.experimental.pallas import tpu as pltpu
from jax.sharding import PartitionSpec as P


Q_HEADS = 9
KV_HEADS = 3
HEAD_DIM = 64
QW = 576
KVW = 192
EPS = 1e-05
ROPE_BASE = 100000.0
MASKED = -1e30
BF16 = jnp.bfloat16
F32 = jnp.float32
MESH = pl.DeviceIdType.MESH
ANY = pl.BlockSpec(memory_space=pl.ANY)
VMEM = pl.BlockSpec(memory_space=pltpu.VMEM)


def up(value, step):
    return -(-value // step) * step


class Layout:
    def __init__(self, pieces, shards):
        self.pieces, self.shards = pieces, shards
        self.C = 2 if pieces % 2 == 0 else 1
        self.Y = pieces // self.C
        self.X = 2 if shards <= 8 else 4
        self.Z = shards // self.X
        self.H = self.Z // 2
        self.slots = (self.C, self.Y, self.X, self.Z)
        n = (self.X - 1) + (self.Y - 1)
        self.gather_sems = 1 + (self.Z - 1) + 2 * n + 1 + 2 * n
        self.reduce_sems = 2 + 2 * n + (self.Z - 1)
        self.peers = (self.X - 1) + (self.Y - 1) + (self.Z - 1) + (self.C - 1)

    def here(self):
        dp, fs = lax.axis_index("dp"), lax.axis_index("fsdp")
        return lax.rem(dp, self.C), dp // self.C, lax.rem(fs, self.X), fs // self.X

    def device(self, c, y, x, z):
        return (y * self.C + c, z * self.X + x)

    def others(self, me, axis):
        size = self.slots[axis]
        for k in range(1, size):
            place = list(me)
            place[axis] = lax.rem(me[axis] + k, size)
            yield k, place

    def barrier(self, me):
        sem = pltpu.get_barrier_semaphore()
        for axis in range(4):
            for _, place in self.others(me, axis):
                pl.semaphore_signal(sem, inc=1, device_id=self.device(*place), device_id_type=MESH)
        pl.semaphore_wait(sem, self.peers)


class Sender:
    def __init__(self, layout, me, send, recv):
        self.lay, self.me, self.send, self.recv, self.used = layout, me, send, recv, 0

    def to(self, place, src, dst):
        k = self.used
        self.used += 1
        return pltpu.make_async_remote_copy(
            src_ref=src, dst_ref=dst, send_sem=self.send.at[k], recv_sem=self.recv.at[k],
            device_id=self.lay.device(*place), device_id_type=MESH)


def start(copies):
    for copy in copies:
        copy.start()


def wait(copies):
    for copy in copies:
        copy.wait()


class Gather:
    def __init__(self, lay, me, src, slots, send, recv):
        c, y, x, z = me
        s = Sender(lay, me, send, recv)
        X, Y, H, R = lay.X, lay.Y, lay.H, lay.Z - lay.H
        lo, hi = pl.ds(0, H), pl.ds(H, R)
        ax, ay = pl.ds(0, X), pl.ds(0, Y)
        sib = (1 - c, y, x, z)
        self.own = pltpu.make_async_copy(src, slots.at[c, y, x, z], recv.at[s.used])
        s.used += 1
        self.z = [s.to(p, src, slots.at[c, y, x, z]) for _, p in lay.others(me, 3)]
        part = slots.at[c, y, x, lo]
        self.xy1 = [s.to(p, part, part) for _, p in lay.others(me, 2)]
        part2 = slots.at[c, y, x, hi]
        self.xy1 += [s.to(p, part2, part2) for _, p in lay.others(me, 1)]
        part3 = slots.at[c, y, ax, lo]
        self.xy2 = [s.to(p, part3, part3) for _, p in lay.others(me, 1)]
        part4 = slots.at[c, ay, x, hi]
        self.xy2 += [s.to(p, part4, part4) for _, p in lay.others(me, 2)]
        self.core = [[], [], []]
        if lay.C > 1:
            whole = slots.at[c, y, x]
            self.core[0] = [s.to(sib, whole, whole)]
            for _, p in lay.others(me, 2):
                piece = slots.at[c, y, p[2], lo]
                self.core[1].append(s.to(sib, piece, piece))
            for _, p in lay.others(me, 1):
                piece = slots.at[c, p[1], x, hi]
                self.core[1].append(s.to(sib, piece, piece))
            for _, p in lay.others(me, 1):
                piece = slots.at[c, p[1], ax, lo]
                self.core[2].append(s.to(sib, piece, piece))
            for _, p in lay.others(me, 2):
                piece = slots.at[c, ay, p[2], hi]
                self.core[2].append(s.to(sib, piece, piece))

    def step(self, n):
        if n == 0:
            self.own.start()
            start(self.z)
        elif n == 1:
            self.own.wait()
            wait(self.z)
            start(self.xy1)
            start(self.core[0])
        elif n == 2:
            wait(self.xy1)
            start(self.xy2)
            start(self.core[1])
        elif n == 3:
            wait(self.xy2)
            start(self.core[2])
        else:
            for copies in self.core:
                wait(copies)


class Reduce:
    def __init__(self, lay, me, parts, bufs, send, recv, inplace):
        c, y, x, z = me
        self.lay, self.me = lay, me
        self.far, self.r2a, self.r2b, self.r3a, self.r3b, self.r4 = bufs[:6]
        self.out = parts.at[c] if inplace else bufs[6]
        s = Sender(lay, me, send, recv)
        X, Y, H, R = lay.X, lay.Y, lay.H, lay.Z - lay.H
        lo, hi = pl.ds(0, H), pl.ds(H, R)
        ax, ay = pl.ds(0, X), pl.ds(0, Y)
        out = self.out
        self.own = None if inplace else pltpu.make_async_copy(parts.at[c], self.out, recv.at[s.used])
        s.used += 1
        self.core = [s.to((1 - c, y, x, z), parts.at[1 - c], self.far)] if lay.C > 1 else []
        self.xy1 = [s.to(p, out.at[p[1], ax, lo], self.r2a.at[k - 1]) for k, p in lay.others(me, 1)]
        self.xy1 += [s.to(p, out.at[ay, p[2], hi], self.r2b.at[k - 1]) for k, p in lay.others(me, 2)]
        self.xy2 = [s.to(p, out.at[y, p[2], lo], self.r3a.at[k - 1]) for k, p in lay.others(me, 2)]
        self.xy2 += [s.to(p, out.at[p[1], x, hi], self.r3b.at[k - 1]) for k, p in lay.others(me, 1)]
        self.zs = [s.to(p, out.at[y, x, p[3]], self.r4.at[k - 1]) for k, p in lay.others(me, 3)]

    @staticmethod
    def scratch(lay, rows, width, inplace):
        X, Y, Z, H = lay.X, lay.Y, lay.Z, lay.H
        R = Z - H
        tail = (rows, width)
        return [
            pltpu.VMEM((Y, X, Z) + tail, BF16),
            pltpu.VMEM((Y - 1, X, H) + tail, BF16), pltpu.VMEM((X - 1, Y, R) + tail, BF16),
            pltpu.VMEM((X - 1, H) + tail, BF16), pltpu.VMEM((Y - 1, R) + tail, BF16),
            pltpu.VMEM((Z - 1,) + tail, BF16),
        ] + ([] if inplace else [pltpu.VMEM((Y, X, Z) + tail, BF16)])

    def step(self, n, result=None):
        lay, (c, y, x, z) = self.lay, self.me
        X, Y, Z, H = lay.X, lay.Y, lay.Z, lay.H
        out = self.out
        if n == 0:
            if self.own is not None:
                self.own.start()
            start(self.core)
        elif n == 1:
            if self.own is not None:
                self.own.wait()
            wait(self.core)

            @pl.loop(0, Y * X * Z)
            def _(i):
                yy, xx, zz = i // (X * Z), lax.rem(i // Z, X), lax.rem(i, Z)
                v = out[yy, xx, zz].astype(F32)
                if lay.C > 1:
                    v = v + self.far[yy, xx, zz].astype(F32)
                out[yy, xx, zz] = v.astype(BF16)

            start(self.xy1)
        elif n == 2:
            wait(self.xy1)

            @pl.loop(0, X * H)
            def _(i):
                xx, zz = i // H, lax.rem(i, H)
                v = out[y, xx, zz].astype(F32)
                for k in range(Y - 1):
                    v = v + self.r2a[k, xx, zz].astype(F32)
                out[y, xx, zz] = v.astype(BF16)

            @pl.loop(0, Y * (Z - H))
            def _(i):
                yy, zz = i // (Z - H), lax.rem(i, Z - H)
                v = out[yy, x, H + zz].astype(F32)
                for k in range(X - 1):
                    v = v + self.r2b[k, yy, zz].astype(F32)
                out[yy, x, H + zz] = v.astype(BF16)

            start(self.xy2)
        elif n == 3:
            wait(self.xy2)

            @pl.loop(0, H)
            def _(i):
                v = out[y, x, i].astype(F32)
                for k in range(X - 1):
                    v = v + self.r3a[k, i].astype(F32)
                out[y, x, i] = v.astype(BF16)

            @pl.loop(0, Z - H)
            def _(i):
                v = out[y, x, H + i].astype(F32)
                for k in range(Y - 1):
                    v = v + self.r3b[k, i].astype(F32)
                out[y, x, H + i] = v.astype(BF16)

            start(self.zs)
        else:
            wait(self.zs)
            v = out[y, x, z].astype(F32)
            for k in range(Z - 1):
                v = v + self.r4[k].astype(F32)
            result[...] = v


QB = 256


def dot(a, b, ca=1, cb=0):
    return lax.dot_general(a, b, (((ca,), (cb,)), ((), ())), preferred_element_type=F32)


def slot_of(lay, d, f):
    return (d % lay.C, d // lay.C, f % lay.X, f // lay.X)


def groups_of(nf):
    if nf % 128 == 0:
        return (((0, 0, nf),), ((1, 0, nf),), ((2, 0, nf),))
    return (((0, 0, nf), (1, nf, nf)), ((2, 0, nf),))


def out_places(part, nq, groups, wa):
    places = []
    for k, width in enumerate([width_of(g) for g in groups] + [wa]):
        places += [(k, j * part) for j in range(width // part)]
    return places[: nq // 8]


def width_of(group):
    return up(group[-1][1] + group[-1][2], 128)


def params(which=None):
    extra = {} if which is None else dict(collective_id=which, has_side_effects=True)
    return pltpu.CompilerParams(vmem_limit_bytes=62 * 2**20, **extra)


def eye(n):
    return (lax.broadcasted_iota(jnp.int32, (n, n), 0) == lax.broadcasted_iota(jnp.int32, (n, n), 1)).astype(F32).astype(BF16)


def split_rows(value, first, base):
    hi = value.astype(BF16).astype(F32)
    mid = (value - hi).astype(BF16).astype(F32)
    low = value - hi - mid
    row = lax.broadcasted_iota(jnp.int32, base.shape, 0)
    return jnp.where(row == first, hi, jnp.where(row == first + 1, mid, jnp.where(row == first + 2, low, base)))


def column(one, ref):
    wide = jnp.broadcast_to(ref[...].astype(F32), (16, ref.shape[1])).astype(BF16)
    return dot(one, wide, 1, 1)[:, 0:1].astype(BF16)


def front(lay, weights, gains, xt, segments, positions, frequency):
    wq, wkt, wvt, wo, wg, wu, wdt = weights
    part, nq = wq.shape
    nk, nf = wkt.shape[0], wg.shape[1]
    rows_p = up(part + 8, 16)
    wa = up(nq + 2 * nk + 2, 128)
    D, T = xt.shape
    E = QW + 2 * KVW
    half = HEAD_DIM // 2
    groups = groups_of(nf)
    G = len(groups)
    places = out_places(part, nq, groups, wa)
    last = slice(rows_p - 8, rows_p)
    aug = HEAD_DIM + 16

    def kernel(wq_ref, wkt_ref, wvt_ref, wo_in, wg_ref, wu_ref, wdt_ref, ag_ref, mg_ref, x_ref, seg_ref, pos_ref, fr_ref, *rest):
        gms, rest = rest[:G], rest[G:]
        (wqkv_ref, gain_ref, nt_ref, qa_ref, ka_ref, kv_ref, mix_ref, cos_ref, sin_ref, oex_ref), rest = rest[:10], rest[10:]
        pms, rest = rest[:G], rest[G:]
        (pa, ga_ref, tmp, scaled, wt, kt, lse_ref), sems = rest[:7], rest[7:]
        one = eye(part)
        pa[0:part, 0:nq] = wq_ref[...]
        pa[0:part, nq : nq + nk] = dot(one, wkt_ref[...], 1, 1).astype(BF16)
        pa[0:part, nq + nk : nq + 2 * nk] = dot(one, wvt_ref[...], 1, 1).astype(BF16)
        pa[0:part, nq + 2 * nk : nq + 2 * nk + 1] = column(one, ag_ref)
        pa[0:part, nq + 2 * nk + 1 : nq + 2 * nk + 2] = column(one, mg_ref)
        for b, (k, lane) in enumerate(places):
            (list(pms) + [pa])[k][last, lane : lane + part] = wo_in[8 * b : 8 * b + 8, :]
        me = lay.here()
        lay.barrier(me)
        ga = Gather(lay, me, pa, ga_ref, sems[0], sems[1])
        gm = [Gather(lay, me, pms[k], gms[k], sems[2 + 2 * k], sems[3 + 2 * k]) for k in range(G)]
        ga.step(0)
        for k, group in enumerate(groups):
            for which, at, size in group:
                pms[k][0:part, at : at + size] = (wg_ref, wu_ref, wdt_ref)[which][...]
        v = x_ref[...].astype(F32)
        scaled[...] = v * lax.rsqrt(jnp.mean(v * v, axis=0, keepdims=True) + EPS)
        angles = fr_ref[...] * pos_ref[...].astype(F32)
        cos_ref[...] = jnp.cos(angles)
        sin_ref[...] = jnp.sin(angles)
        ga.step(1)
        for gather in gm:
            gather.step(0)
        ga.step(2)
        ga.step(3)
        gm[0].step(1)
        ga.step(4)
        for d in range(lay.pieces):
            for f in range(lay.shards):
                tmp[f * part : (f + 1) * part, :] = ga_ref[slot_of(lay, d, f)].astype(F32)[:part]
                oex_ref[d * lay.shards + f] = ga_ref[slot_of(lay, d, f) + (last,)]
            wqkv_ref[:, d * nq : (d + 1) * nq] = tmp[:, 0:nq].astype(BF16)
            wqkv_ref[:, QW + d * nk : QW + (d + 1) * nk] = tmp[:, nq : nq + nk].astype(BF16)
            wqkv_ref[:, QW + KVW + d * nk : QW + KVW + (d + 1) * nk] = tmp[:, nq + nk : nq + 2 * nk].astype(BF16)
        gain_ref[:, 0:2] = tmp[:, nq + 2 * nk : nq + 2 * nk + 2]
        gm[0].step(2)
        gm[1].step(1)
        wt[...] = jnp.transpose(wqkv_ref[...])
        nt_ref[...] = (scaled[...] * gain_ref[:, 0:1]).astype(BF16)

        @pl.loop(0, T // QB)
        def _(i):
            cols = pl.ds(pl.multiple_of(i * QB, QB), QB)
            raw = dot(wt[...], nt_ref[:, cols])
            cs, sn = cos_ref[:, cols], sin_ref[:, cols]
            for h in range(Q_HEADS + KV_HEADS):
                u1, u2 = raw[h * HEAD_DIM : h * HEAD_DIM + half], raw[h * HEAD_DIM + half : (h + 1) * HEAD_DIM]
                o1 = (u1 * cs - u2 * sn).astype(BF16)
                o2 = (u2 * cs + u1 * sn).astype(BF16)
                if h < Q_HEADS:
                    scale = HEAD_DIM ** (-0.5)
                    qa_ref[h, 0:half, cols] = o1 * scale
                    qa_ref[h, half:HEAD_DIM, cols] = o2 * scale
                else:
                    g = (h - Q_HEADS) * HEAD_DIM
                    kv_ref[g : g + half, cols] = o1
                    kv_ref[g + half : g + HEAD_DIM, cols] = o2
            kv_ref[KVW:, cols] = raw[QW + KVW :].astype(BF16)

        gm[0].step(3)
        gm[1].step(2)
        if G > 2:
            gm[2].step(1)
        row = lax.broadcasted_iota(jnp.int32, (16, T), 0)
        same = row == seg_ref[...]
        qrows = jnp.where(row < 3, jnp.where(same, 0.0, MASKED), 0.0).astype(BF16)
        kt[HEAD_DIM:, :] = jnp.where(row < 3, jnp.where(same, 1.0, 0.0), jnp.where(row < 6, 1.0, 0.0)).astype(BF16)
        for h in range(Q_HEADS):
            qa_ref[h, HEAD_DIM:, :] = qrows
        for g in range(KV_HEADS):
            kt[0:HEAD_DIM, :] = kv_ref[g * HEAD_DIM : (g + 1) * HEAD_DIM, :]
            ka_ref[g] = jnp.transpose(kt[...])
        causal = lax.broadcasted_iota(jnp.int32, (QB, QB), 0) <= lax.broadcasted_iota(jnp.int32, (QB, QB), 1)
        for i in range(T // QB):
            q0, k0 = i * QB, 0 if i == 0 else 128

            @pl.loop(0, Q_HEADS)
            def _(h):
                g = h // (Q_HEADS // KV_HEADS)
                vrow = pl.ds(pl.multiple_of(KVW + g * HEAD_DIM, HEAD_DIM), HEAD_DIM)
                qcol = qa_ref[h, :, q0 : q0 + QB]
                s = jnp.where(causal, dot(ka_ref[g, q0 : q0 + QB, :], qcol), MASKED)
                top = jnp.max(s, axis=0, keepdims=True)
                if i:
                    s2 = dot(ka_ref[g, k0:q0, :], qcol)
                    top = jnp.maximum(top, jnp.max(s2, axis=0, keepdims=True))
                e = jnp.exp(s - top)
                total = jnp.sum(e, axis=0, keepdims=True)
                if i:
                    e2 = jnp.exp(s2 - top)
                    total = total + jnp.sum(e2, axis=0, keepdims=True)
                inv = 1.0 / total
                out = dot(kv_ref[vrow, q0 : q0 + QB], (e * inv).astype(BF16))
                if i:
                    out = out + dot(kv_ref[vrow, k0:q0], (e2 * inv).astype(BF16))
                mix_ref[pl.ds(pl.multiple_of(h * HEAD_DIM, HEAD_DIM), HEAD_DIM), q0 : q0 + QB] = out.astype(BF16)
                lse_ref[h, :, q0 : q0 + QB] = top + jnp.log(total)

            if i == 1:
                gm[1].step(3)
                if G > 2:
                    gm[2].step(2)
            if i == 2 and G > 2:
                gm[2].step(3)
        base = qrows.astype(F32)
        for h in range(Q_HEADS):
            qa_ref[h, HEAD_DIM:, :] = split_rows(-lse_ref[h], 3, base).astype(BF16)
        for gather in gm:
            gather.step(4)

    n = lay.gather_sems
    sd = jax.ShapeDtypeStruct
    V = pltpu.VMEM
    return pl.pallas_call(
        kernel,
        out_shape=[sd(lay.slots + (rows_p, width_of(g)), BF16) for g in groups]
        + [sd((D, E), BF16), sd((D, 8), F32), sd((D, T), BF16),
           sd((Q_HEADS, aug, T), BF16), sd((KV_HEADS, T, aug), BF16), sd((2 * KVW, T), BF16), sd((QW, T), BF16),
           sd((half, T), F32), sd((half, T), F32), sd((lay.pieces * lay.shards, 8, wa), BF16)],
        in_specs=[VMEM] * 13, out_specs=[ANY] * G + [VMEM] * 10,
        scratch_shapes=[V((rows_p, width_of(g)), BF16) for g in groups]
        + [V((rows_p, wa), BF16), V(lay.slots + (rows_p, wa), BF16), V((D, wa), F32), V((D, T), F32), V((E, D), BF16), V((aug, T), BF16), V((Q_HEADS, 1, T), F32)]
        + [pltpu.SemaphoreType.DMA((n,))] * (2 + 2 * G),
        compiler_params=params(0), name="gather_attend",
    )(*weights, *gains, xt, segments, positions, frequency)


MB = 512


def middle(lay, part, nf, nq, gms, oex, mix, gain, xt, ct):
    D, T = xt.shape
    FF = nf * lay.pieces
    groups = groups_of(nf)
    G = len(groups)
    places = out_places(part, nq, groups, oex.shape[-1])
    wmax = max(width_of(g) for g in groups)
    rows_p = gms[0].shape[-2]
    items = [(k, d) for k in range(G) for d in range(lay.pieces)]

    def kernel(*rest):
        gm_refs, rest = rest[:G], rest[G:]
        oex_ref, rest = rest[0], rest[1:]
        (mix_ref, gain_ref, x_ref, c_ref, o_out, r_out, gg_ref, wo_ref, n_out, h_out, g_out, u_out), rest = rest[:12], rest[12:]
        stages, rest = rest[:G], rest[G:]
        tmp, wg, wu, wd, wgt, wut, wdt, wot, out_ref, gr_ref, normed, hidden, dgate, dup, sem, out_sem = rest

        def fetch(n):
            k, d = items[n]
            c, y = d % lay.C, d // lay.C
            return pltpu.make_async_copy(gm_refs[k].at[c, y], stages[k].at[d % 2], sem.at[n])

        def put(k, d, f, rows):
            for b, (pack, lane) in enumerate(places):
                if pack == k:
                    at = d * nq + 8 * b
                    gr_ref[at : at + 8, f * part : (f + 1) * part] = rows[:, lane : lane + part]

        fetch(0).start()
        fetch(1).start()
        for n, (k, d) in enumerate(items):
            fetch(n).wait()
            size = width_of(groups[k])
            for f in range(lay.shards):
                piece = stages[k][d % 2, f % lay.X, f // lay.X].astype(F32)
                tmp[f * part : (f + 1) * part, 0:size] = piece[:part]
                put(k, d, f, piece[rows_p - 8 :])
            if n + 2 < len(items):
                fetch(n + 2).start()
            for which, at, w in groups[k]:
                (wg, wu, wd)[which][:, d * w : (d + 1) * w] = tmp[:, at : at + w].astype(BF16)
        for d in range(lay.pieces):
            for f in range(lay.shards):
                put(G, d, f, oex_ref[d * lay.shards + f].astype(F32))
        wo_ref[...] = gr_ref[:, 0:D].astype(BF16)
        wot[...] = jnp.transpose(wo_ref[...])
        wgt[...] = jnp.transpose(wg[...])
        wut[...] = jnp.transpose(wu[...])
        wdt[...] = jnp.transpose(wd[...])
        gain = gain_ref[:, 1:2]

        def send(i, cols):
            pairs = ((hidden, h_out), (dgate, g_out), (dup, u_out), (out_ref, o_out), (gr_ref, r_out), (normed, n_out))
            return [pltpu.make_async_copy(a.at[:, cols], b.at[:, cols], out_sem.at[i, k]) for k, (a, b) in enumerate(pairs)]

        gg_ref[...] = jnp.zeros_like(gg_ref)

        @pl.loop(0, T // MB)
        def _(i):
            cols = pl.ds(pl.multiple_of(i * MB, MB), MB)
            cot = c_ref[:, cols]
            resid = x_ref[:, cols].astype(F32) + dot(wot[...], mix_ref[:, cols])
            inverse = lax.rsqrt(jnp.mean(resid * resid, axis=0, keepdims=True) + EPS)
            scaled = resid * inverse
            nb = (scaled * gain).astype(BF16)
            normed[:, cols] = nb
            out = resid
            gnm = jnp.zeros_like(resid)
            for j in range(2):
                rows = slice(j * (FF // 2), (j + 1) * (FF // 2))
                gate = dot(wgt[rows, :], nb)
                upp = dot(wut[rows, :], nb)
                gh = dot(wdt[rows, :], cot)
                s = jax.nn.sigmoid(gate)
                act = gate * s
                hb = (act * upp).astype(BF16)
                hidden[rows, cols] = hb
                dg = (gh * upp * (s * (1.0 + gate * (1.0 - s)))).astype(BF16)
                du = (gh * act).astype(BF16)
                dgate[rows, cols] = dg
                dup[rows, cols] = du
                out = out + dot(wd[:, rows], hb)
                gnm = gnm + dot(wg[:, rows], dg) + dot(wu[:, rows], du)
            out_ref[:, cols] = out.astype(BF16)
            gg_ref[:, 0:1] += jnp.sum(gnm * scaled, axis=1, keepdims=True)
            m = gnm * gain
            back = inverse * (m - scaled * jnp.mean(m * scaled, axis=0, keepdims=True))
            gr_ref[:, cols] = cot.astype(F32) + back
            for copy in send(i, cols):
                copy.start()

        for i in range(T // MB):
            for copy in send(i, slice(i * MB, (i + 1) * MB)):
                copy.wait()

    sd = jax.ShapeDtypeStruct
    V = pltpu.VMEM
    res = pl.pallas_call(
        kernel,
        out_shape=[sd((D, T), BF16), sd((D, T), F32), sd((D, 8), F32), sd((QW, D), BF16), sd((D, T), BF16)] + [sd((FF, T), BF16)] * 3,
        in_specs=[ANY] * G + [VMEM] * 5, out_specs=[ANY] * 2 + [VMEM] * 2 + [ANY] * 4,
        scratch_shapes=[V((2, lay.X, lay.Z) + g.shape[-2:], BF16) for g in gms]
        + [V((D, wmax), F32)] + [V((D, FF), BF16)] * 3 + [V((FF, D), BF16)] * 3 + [V((D, QW), BF16), V((D, T), BF16), V((D, T), F32), V((D, T), BF16)]
        + [V((FF, T), BF16)] * 3 + [pltpu.SemaphoreType.DMA((len(items),)), pltpu.SemaphoreType.DMA((T // MB, 6))],
        compiler_params=params(), name="mlp",
    )(*gms, oex, mix, gain, xt, ct)
    return res


def back(lay, part, nf, nq, nk, acts, gr, ct, nm, xt, nt, mix, qa, ka, kv, wqkv, wo, gain, ggain, cosine, sine):
    D, T = xt.shape
    E = QW + 2 * KVW
    aug = HEAD_DIM + 16
    half = HEAD_DIM // 2
    groups = groups_of(nf)
    G = len(groups)
    rows_p = up(part + 8, 16)
    wa = up(nq + 2 * nk + 2, 128)
    places = out_places(part, nq, groups, wa)
    last = slice(rows_p - 8, rows_p)
    FF = nf * lay.pieces
    if G > 2:
        early = ((), ((0, 1),), ((1, 1),))
        ready = ()
        plan = ((0, 0, 2), (1, 2, 1), (3, 1, 2), (3, 0, 3), (5, 2, 2), (5, 1, 3), (7, 0, 4), (8, 1, 4))
    else:
        early = ((), ((0, 1),))
        ready = ()
        plan = ((0, 1, 1), (1, 0, 2), (3, 0, 3), (4, 1, 2), (6, 0, 4), (7, 1, 3))
    nbuf = 2 if G > 2 else 1

    def kernel(*rest):
        a_refs, gr_in, rest = rest[:3], rest[3], rest[4:]
        (ct_ref, nm_ref, x_ref, nt_ref, mix_ref, qa_ref, ka_ref, kv_ref, wqkv_ref, wo_ref, gain_ref, gg_ref, cos_ref, sin_ref), rest = rest[:14], rest[14:]
        gt_ref, oa, rest = rest[0], rest[1], rest[2:]
        oms, rest = rest[:G], rest[G:]
        mbufs, rest = [rest[6 * k : 6 * k + 6] for k in range(G)], rest[6 * G :]
        abufs, rest = rest[:6], rest[6:]
        p_refs, rest = rest[:G], rest[G:]
        (big, gb, don, doa, qn, va, dk, dv, dq, draw, dw, wide, line, pa, big_sem), sems = rest[:15], rest[15:]
        me = lay.here()
        lay.barrier(me)
        reds = [Reduce(lay, me, p_refs[k], mbufs[k], sems[2 * k], sems[2 * k + 1], True) for k in range(G)]

        def fetch(which):
            return pltpu.make_async_copy(a_refs[which], big.at[which % nbuf], big_sem.at[which])

        load = pltpu.make_async_copy(gr_in, gt_ref, big_sem.at[3])
        for which in range(nbuf):
            fetch(which).start()
        load.start()
        load.wait()
        gb[...] = gt_ref[...].astype(BF16)
        wide[:, 0:D] = dot(mix_ref[...], gb[...], 1, 1)
        packs = list(p_refs) + [pa]
        for d in range(lay.pieces):
            for f in range(lay.shards):
                for k in sorted({pack for pack, _ in places}):
                    for b, (pack, lane) in enumerate(places):
                        if pack == k:
                            at = d * nq + 8 * b
                            line[k, :, lane : lane + part] = wide[at : at + 8, f * part : (f + 1) * part]
                    width = packs[k].shape[-1]
                    packs[k][slot_of(lay, d, f) + (last,)] = line[k, :, 0:width].astype(BF16)
        for k, group in enumerate(groups):
            for which, at, w in group:
                fetch(which).wait()
                for d in range(lay.pieces):
                    rows = slice(d * w, (d + 1) * w)
                    value = dot(ct_ref[...] if which == 2 else nm_ref[...], big[which % nbuf, rows, :], 1, 1)
                    wide[:, 0:w] = value
                    for f in range(lay.shards):
                        p_refs[k][slot_of(lay, d, f) + (slice(0, part), slice(at, at + w))] = wide[f * part : (f + 1) * part, 0:w].astype(BF16)
                if which + nbuf < 3:
                    fetch(which + nbuf).start()
            reds[k].step(0)
            for kk, n in early[k]:
                reds[kk].step(n)
        zero = jnp.zeros((16, T), F32)

        @pl.loop(0, Q_HEADS)
        def _(h):
            rows = pl.ds(pl.multiple_of(h * HEAD_DIM, HEAD_DIM), HEAD_DIM)
            t = dot(wo_ref[rows, :], gb[...]).astype(BF16)
            doa[h, 0:HEAD_DIM, :] = t
            don[h] = jnp.transpose(t)
            delta = jnp.sum(t.astype(F32) * mix_ref[rows, :].astype(F32), axis=0, keepdims=True)
            doa[h, HEAD_DIM:, :] = split_rows(-delta, 0, zero).astype(BF16)
            qn[h] = jnp.transpose(qa_ref[h, 0:HEAD_DIM, :])

        for k, n in ready:
            reds[k].step(n)
        ones = jnp.where(lax.broadcasted_iota(jnp.int32, (T, 16), 1) < 3, 1.0, 0.0).astype(BF16)
        for g in range(KV_HEADS):
            va[g, :, 0:HEAD_DIM] = jnp.transpose(kv_ref[KVW + g * HEAD_DIM : KVW + (g + 1) * HEAD_DIM, :])
            va[g, :, HEAD_DIM:] = ones
        dk[...] = jnp.zeros_like(dk)
        dv[...] = jnp.zeros_like(dv)
        causal = lax.broadcasted_iota(jnp.int32, (QB, QB), 0) <= lax.broadcasted_iota(jnp.int32, (QB, QB), 1)

        @pl.loop(0, Q_HEADS)
        def _(h):
            g = h // (Q_HEADS // KV_HEADS)
            krow = pl.ds(pl.multiple_of(g * HEAD_DIM, HEAD_DIM), HEAD_DIM)
            for j in range(T // QB):
                k0, k1 = j * QB, (j + 1) * QB
                blocks = [(k0, k1, k0, k1, True)]
                if k1 < T:
                    blocks.append((k0 if j else 128, k1, k1, T, False))
                for a, b, c, d, diagonal in blocks:
                    st = dot(ka_ref[g, a:b, :], qa_ref[h, :, c:d])
                    p = jnp.exp(st)
                    if diagonal:
                        p = jnp.where(causal, p, 0.0)
                    dp = dot(va[g, a:b, :], doa[h, :, c:d])
                    ds = (p * dp).astype(BF16)
                    dv[g, a:b, :] += dot(p.astype(BF16), don[h, c:d, :])
                    dk[g, a:b, :] += dot(ds, qn[h, c:d, :])
                    part_q = dot(kv_ref[krow, a:b], ds)
                    if j == 0:
                        dq[:, c:d] = part_q
                    else:
                        dq[:, c:d] += part_q
            scale = HEAD_DIM ** (-0.5)
            d1, d2 = dq[0:half, :] * scale, dq[half:, :] * scale
            cs, sn = cos_ref[...], sin_ref[...]
            at = pl.multiple_of(h * HEAD_DIM, HEAD_DIM)
            draw[pl.ds(at, half), :] = (d1 * cs + d2 * sn).astype(BF16)
            draw[pl.ds(at + half, half), :] = (d2 * cs - d1 * sn).astype(BF16)
            for when, k, n in plan:

                @pl.when(h == when)
                def _():
                    reds[k].step(n, oms[k])

        cs, sn = cos_ref[...], sin_ref[...]
        for g in range(KV_HEADS):
            t = jnp.transpose(dk[g])
            d1, d2 = t[0:half], t[half:]
            at = QW + g * HEAD_DIM
            draw[at : at + half, :] = (d1 * cs + d2 * sn).astype(BF16)
            draw[at + half : at + HEAD_DIM, :] = (d2 * cs - d1 * sn).astype(BF16)
            at = QW + KVW + g * HEAD_DIM
            draw[at : at + HEAD_DIM, :] = jnp.transpose(dv[g]).astype(BF16)
        wide[:, 0:E] = dot(nt_ref[...], draw[...], 1, 1)
        again = gain_ref[:, 0:1]
        if G > 2:
            reds[2].step(3, oms[2])
        gattn = jnp.sum(wide[:, 0:E] * wqkv_ref[...].astype(F32), axis=1, keepdims=True) / again
        for d in range(lay.pieces):
            dw[:, 0:nq] = wide[:, d * nq : (d + 1) * nq]
            dw[:, nq : nq + nk] = wide[:, QW + d * nk : QW + (d + 1) * nk]
            dw[:, nq + nk : nq + 2 * nk] = wide[:, QW + KVW + d * nk : QW + KVW + (d + 1) * nk]
            dw[:, nq + 2 * nk : nq + 2 * nk + 1] = gattn
            dw[:, nq + 2 * nk + 1 : nq + 2 * nk + 2] = gg_ref[:, 0:1]
            for f in range(lay.shards):
                pa[slot_of(lay, d, f) + (slice(0, part),)] = dw[f * part : (f + 1) * part, :].astype(BF16)
        ared = Reduce(lay, me, pa, abufs, sems[2 * G], sems[2 * G + 1], True)
        ared.step(0)
        for i in range(4):
            cols = slice(i * (T // 4), (i + 1) * (T // 4))
            v = x_ref[:, cols].astype(F32)
            inverse = lax.rsqrt(jnp.mean(v * v, axis=0, keepdims=True) + EPS)
            scaled = v * inverse
            m = dot(wqkv_ref[...], draw[:, cols]) * again
            gt_ref[:, cols] += inverse * (m - scaled * jnp.mean(m * scaled, axis=0, keepdims=True))
            if i == 0:
                ared.step(1)
                reds[G - 1].step(4, oms[G - 1])
            if i == 1:
                ared.step(2)
            if i == 2:
                ared.step(3)
        ared.step(4, oa)

    n = lay.reduce_sems
    sd = jax.ShapeDtypeStruct
    V = pltpu.VMEM
    scratch = []
    for g in groups:
        scratch += Reduce.scratch(lay, rows_p, width_of(g), True)
    scratch += Reduce.scratch(lay, rows_p, wa, True)
    res = pl.pallas_call(
        kernel,
        out_shape=[sd((D, T), F32), sd((rows_p, wa), F32)] + [sd((rows_p, width_of(g)), F32) for g in groups],
        in_specs=[ANY] * 4 + [VMEM] * 14, out_specs=[VMEM] * (2 + G),
        scratch_shapes=scratch + [V(lay.slots + (rows_p, width_of(g)), BF16) for g in groups]
        + [V((nbuf, FF, T), BF16), V((D, T), BF16), V((Q_HEADS, T, HEAD_DIM), BF16), V((Q_HEADS, aug, T), BF16),
           V((Q_HEADS, T, HEAD_DIM), BF16), V((KV_HEADS, T, aug), BF16),
           V((KV_HEADS, T, HEAD_DIM), F32), V((KV_HEADS, T, HEAD_DIM), F32), V((HEAD_DIM, T), F32), V((E, T), BF16),
           V((D, wa), F32), V((D, E), F32), V((G + 1, 8, max([wa] + [width_of(g) for g in groups])), F32), V(lay.slots + (rows_p, wa), BF16), pltpu.SemaphoreType.DMA((4,))]
        + [pltpu.SemaphoreType.DMA((n,))] * (2 * G + 2),
        compiler_params=params(1), name="attend_back",
    )(*acts, gr, ct, nm, xt, nt, mix, qa, ka, kv, wqkv, wo, gain, ggain, cosine, sine)
    return finish(part, nf, nq, nk, groups, places, *res)


def finish(part, nf, nq, nk, groups, places, gt, attn, *mlp):
    G = len(groups)

    def kernel(*rest):
        gt_in, oa, oms, outs = rest[0], rest[1], rest[2 : 2 + G], rest[2 + G :]
        gt_ref, gq_ref, gk_ref, gv_ref, go_ref, gg_out, gu_out, gd_out, ga_out, gm_out = outs
        gt_ref[...] = gt_in[...]
        for k, group in enumerate(groups):
            for which, at, w in group:
                (gg_out, gu_out, gd_out)[which][...] = oms[k][0:part, at : at + w]
        rows_p = oa.shape[0]
        for b, (k, lane) in enumerate(places):
            go_ref[8 * b : 8 * b + 8, :] = (list(oms) + [oa])[k][rows_p - 8 : rows_p, lane : lane + part]
        gq_ref[...] = oa[0:part, 0:nq]
        turned = jnp.transpose(oa[...])
        gk_ref[...] = turned[nq : nq + nk, 0:part]
        gv_ref[...] = turned[nq + nk : nq + 2 * nk, 0:part]
        ga_out[...] = turned[nq + 2 * nk : nq + 2 * nk + 1, 0:part]
        gm_out[...] = turned[nq + 2 * nk + 1 : nq + 2 * nk + 2, 0:part]

    sd = jax.ShapeDtypeStruct
    return pl.pallas_call(
        kernel,
        out_shape=[sd(gt.shape, F32), sd((part, nq), F32), sd((nk, part), F32), sd((nk, part), F32), sd((nq, part), F32)]
        + [sd((part, nf), F32)] * 3 + [sd((1, part), F32)] * 2,
        in_specs=[VMEM] * (2 + G), out_specs=[VMEM] * 10,
        compiler_params=params(), name="cut_out",
    )(gt, attn, *mlp)


def on_device(tokens, segments, positions, attn_gain, mlp_gain, w_query, w_key, w_value, w_output, w_gate, w_up, w_down, cotangent):
    lay = Layout(lax.axis_size("dp"), lax.axis_size("fsdp"))
    part = attn_gain.shape[0]
    nq, nk, nf = w_query.shape[1], w_key.shape[1], w_gate.shape[1]
    half = HEAD_DIM // 2
    frequency = ROPE_BASE ** (-(2.0 * np.arange(half, dtype=np.float64)) / HEAD_DIM)
    frequency = jnp.asarray(frequency.astype(np.float32)[:, None])
    xt, ct = tokens.T, cotangent.T
    weights = (w_query, w_key.T, w_value.T, w_output, w_gate, w_up, w_down.T)
    gains = (attn_gain[None], mlp_gain[None])
    res = front(lay, weights, gains, xt, segments, positions, frequency)
    gms, (wqkv, gain, nt, qa, ka, kv, mix, cosine, sine, oex) = res[:-10], res[-10:]
    out, gr, ggain, wo, nm, hidden, dgate, dup = middle(lay, part, nf, nq, gms, oex, mix, gain, xt, ct)
    gt, gq, gk, gv, go, gg, gu, gd, ga, gm = back(
        lay, part, nf, nq, nk, (dgate, dup, hidden), gr, ct, nm, xt, nt, mix, qa, ka, kv, wqkv, wo, gain, ggain, cosine, sine)
    return (out.T, gt.T, ga[0], gm[0], gq, gk.T, gv.T, go, gg, gu, gd.T)


def solution(mesh):
    in_specs = (
        P(("dp", "fsdp"), None),
        P(("dp", "fsdp"), None),
        P(("dp", "fsdp"), None),
        P("fsdp"),
        P("fsdp"),
        P("fsdp", "dp"),
        P("fsdp", "dp"),
        P("fsdp", "dp"),
        P("dp", "fsdp"),
        P("fsdp", "dp"),
        P("fsdp", "dp"),
        P("dp", "fsdp"),
        P(("dp", "fsdp"), None),
    )
    out_specs = (
        P(("dp", "fsdp"), None),
        P(("dp", "fsdp"), None),
        P("fsdp"),
        P("fsdp"),
        P("fsdp", "dp"),
        P("fsdp", "dp"),
        P("fsdp", "dp"),
        P("dp", "fsdp"),
        P("fsdp", "dp"),
        P("fsdp", "dp"),
        P("dp", "fsdp"),
    )
    return jax.shard_map(
        on_device, mesh=mesh, in_specs=in_specs, out_specs=out_specs, check_vma=False
    )
```
